32 devices in a mesh: dp: 4 (over y, x), seq: 8 (over z, core).
Axes of the slice: x: 2, y: 2, z: 4, core: 2. Of those that a mesh axis runs over, the one named last changes fastest.
Arguments:
- tokens: bfloat16 [8, 512, 1024], P('dp', 'seq'), may hold values from -6 to 6
- memory: bfloat16 [8, 512, 1024], P('dp', 'seq'), may hold values from -6 to 6
- cotangent: bfloat16 [8, 512, 1024], P('dp', 'seq'), may hold values from -6 to 6
- block_ids: int32 [8, 512], P('dp'), may hold values from 0 to 3, never falling along the last dimension, each value on 1 to 256 neighbouring positions
- seq_lengths: int32 [8], P('dp'), may hold values from 256 to 512, as said below
- self_query: bfloat16 [1024, 1024], P(('dp', 'seq')), may hold values from -0.1875 to 0.1875
- self_key: bfloat16 [1024, 1024], P(('dp', 'seq')), may hold values from -0.1875 to 0.1875
- self_value: bfloat16 [1024, 1024], P(('dp', 'seq')), may hold values from -0.1875 to 0.1875
- self_out: bfloat16 [1024, 1024], P(('dp', 'seq')), may hold values from -3 to 3
- cross_query: bfloat16 [1024, 1024], P(('dp', 'seq')), may hold values from -0.1875 to 0.1875
- cross_key: bfloat16 [1024, 1024], P(('dp', 'seq')), may hold values from -0.1875 to 0.1875
- cross_value: bfloat16 [1024, 1024], P(('dp', 'seq')), may hold values from -0.1875 to 0.1875
- cross_out: bfloat16 [1024, 1024], P(('dp', 'seq')), may hold values from -3 to 3
- ffn_up: bfloat16 [1024, 4096], P(('dp', 'seq')), may hold values from -0.1875 to 0.1875
- ffn_down: bfloat16 [4096, 1024], P(('dp', 'seq')), may hold values from -0.09375 to 0.09375
- attn_gain: bfloat16 [1024], P(('dp', 'seq')), may hold values from 0.25 to 1.75
- attn_bias: bfloat16 [1024], P(('dp', 'seq')), may hold values from -3 to 3
- cross_gain: bfloat16 [1024], P(('dp', 'seq')), may hold values from 0.25 to 1.75
- cross_bias: bfloat16 [1024], P(('dp', 'seq')), may hold values from -3 to 3
- feedforward_norm_gain: bfloat16 [1024], P(('dp', 'seq')), may hold values from 0.25 to 1.75
- ffn_bias: bfloat16 [1024], P(('dp', 'seq')), may hold values from -3 to 3
Outputs:
- layer_out: bfloat16 [8, 512, 1024], P('dp', 'seq')
- tokens_grad: bfloat16 [8, 512, 1024], P('dp', 'seq')
- memory_grad: bfloat16 [8, 512, 1024], P('dp', 'seq')
- self_query_grad: float32 [1024, 1024], P(('dp', 'seq'))
- self_key_grad: float32 [1024, 1024], P(('dp', 'seq'))
- self_value_grad: float32 [1024, 1024], P(('dp', 'seq'))
- self_out_grad: float32 [1024, 1024], P(('dp', 'seq'))
- cross_query_grad: float32 [1024, 1024], P(('dp', 'seq'))
- cross_key_grad: float32 [1024, 1024], P(('dp', 'seq'))
- cross_value_grad: float32 [1024, 1024], P(('dp', 'seq'))
- cross_out_grad: float32 [1024, 1024], P(('dp', 'seq'))
- ffn_up_grad: float32 [1024, 4096], P(('dp', 'seq'))
- ffn_down_grad: float32 [4096, 1024], P(('dp', 'seq'))
- attn_gain_grad: float32 [1024], P(('dp', 'seq'))
- attn_bias_grad: float32 [1024], P(('dp', 'seq'))
- cross_gain_grad: float32 [1024], P(('dp', 'seq'))
- cross_bias_grad: float32 [1024], P(('dp', 'seq'))
- ffn_gain_grad: float32 [1024], P(('dp', 'seq'))
- ffn_bias_grad: float32 [1024], P(('dp', 'seq'))
The draws below stay inside these ranges and needn't reach their ends.
Inputs may be any that keep to these rules, and one draw needn't show every extreme that they name: `seq_lengths`: some sequence in every draw has all 512 tokens live. `block_ids`: along each sequence the block ids never fall, and each block spans 1 to 256 positions, some block exactly 256.
All inputs are finite; a program needn't handle non-finite values.
Results may differ from the reference program's by a relative error of at most 0.025.
Values may be sent and summed in bfloat16 or wider, within the bound.
No kernel may reach another device: no remote copies, remote signals or barrier semaphores. Data moves between devices by JAX's collectives and lax.ppermute only.
A program may use at most 192 MiB of HBM per device.

```python
import math
import jax
import jax.numpy as jnp
import numpy as np
from jax import lax

D = 1024
HEADS = 16
HEAD_DIM = 64
FF = 4096
BLOCK = 256
LENGTH = 512
MEM_LEN = 512
SEQS = 8


def draw_seq_lengths(key, part):
    first_key, second_key = jax.random.split(key)
    shortfall = jax.random.randint(first_key, (SEQS,), 0, LENGTH // 2 + 1)
    full_index = jax.random.randint(second_key, (), 0, SEQS)
    shortfall = jnp.where(jnp.arange(SEQS) == full_index, 0, shortfall)
    return (LENGTH - shortfall).astype(jnp.int32)


def shard_levels(own_key, dims, pieces, least, top_value):
    def one(position, parts):
        draws = jax.random.uniform(jax.random.fold_in(jax.random.fold_in(own_key, 6), position), (parts,), jnp.float32, least / len(pieces), top_value / len(pieces))
        return jnp.repeat(jnp.exp(draws), dims[position] // parts).reshape((-1,) + (1,) * (len(dims) - position - 1))

    loudness = one(*pieces[0])
    for cut in pieces[1:]:
        loudness = loudness * one(*cut)
    return loudness


def profile(amount, total, reach, slope):
    portions = [(1 << 20) // math.isqrt(standing ** slope) + 1 for standing in range(2, amount + 1)]
    spare, given = total - reach - (amount - 1), [1] * (amount - 1)
    while spare > 0:
        candidates = [i for i in range(amount - 1) if given[i] < reach]
        whole, remaining = sum([portions[i] for i in candidates]), spare
        for i in candidates:
            more = min(reach - given[i], max(1, remaining * portions[i] // whole), spare)
            given[i] = given[i] + more
            spare = spare - more
    return np.array([reach] + given)


def ragged(stream_key, number_of, total, reach, lean):
    if number_of == 2:
        one = jax.random.randint(stream_key, (), max(1, total - reach), min(reach, total - 1) + 1)
        return jnp.stack([one, total - one])
    lengths = jnp.asarray(profile(number_of, total, reach, lean), jnp.int32)
    couples = (number_of - 1) // 2
    donor, taker = lengths[1:1 + 2 * couples:2], lengths[2:2 + 2 * couples:2]
    room = jnp.minimum(donor - 1, reach - taker)
    moved = jax.random.randint(jax.random.fold_in(stream_key, 1), (couples,), 0, 1 << 20) % (room + 1)
    lengths = lengths.at[1:1 + 2 * couples:2].set(donor - moved).at[2:2 + 2 * couples:2].set(taker + moved)
    return lengths[jax.random.permutation(jax.random.fold_in(stream_key, 2), number_of)]


def noise(rng, extent, deviation, bound, pieces=(), dtype=jnp.bfloat16):
    entries = deviation * jax.random.normal(rng, extent, jnp.float32)
    if pieces:
        entries = entries * shard_levels(rng, extent, pieces, -0.22, 0.18)
    return jnp.clip(entries, -bound, bound).astype(dtype)


def setup_inputs(seed: int = 0) -> dict:
    splits = jax.random.split(jax.random.key(seed), 22)
    tokens = noise(splits[0], (SEQS, LENGTH, D), 1.0, 6.0, ((0, 4), (1, 8)))
    memory = noise(splits[1], (SEQS, MEM_LEN, D), 1.0, 6.0, ((0, 4), (1, 8)))
    cotangent = noise(splits[2], (SEQS, LENGTH, D), 1.0, 6.0, ((0, 4), (1, 8)))
    block_ids = jax.vmap(lambda own: jnp.searchsorted(jnp.cumsum(ragged(own, 2 * LENGTH // BLOCK, LENGTH, BLOCK, 0)), jnp.arange(LENGTH), side="right"))(jax.random.split(splits[3], SEQS)).reshape((SEQS, LENGTH)).astype(jnp.int32)
    seq_lengths = draw_seq_lengths(jax.random.fold_in(splits[21], 71), 0)
    self_query = noise(splits[5], (D, D), D ** -0.5, 0.1875, ((0, 32),))
    self_key = noise(splits[6], (D, D), D ** -0.5, 0.1875, ((0, 32),))
    self_value = noise(splits[7], (D, D), D ** -0.5, 0.1875, ((0, 32),))
    self_out = noise(splits[8], (D, D), (max(D // 256, 1)) ** -0.5, 3.0, ((0, 32),))
    cross_query = noise(splits[9], (D, D), D ** -0.5, 0.1875, ((0, 32),))
    cross_key = noise(splits[10], (D, D), D ** -0.5, 0.1875, ((0, 32),))
    cross_value = noise(splits[11], (D, D), D ** -0.5, 0.1875, ((0, 32),))
    cross_out = noise(splits[12], (D, D), (max(D // 256, 1)) ** -0.5, 3.0, ((0, 32),))
    ffn_up = noise(splits[13], (D, FF), D ** -0.5, 0.1875, ((0, 32),))
    ffn_down = noise(splits[14], (FF, D), FF ** -0.5, 0.09375, ((0, 32),))
    attn_gain = jnp.clip(1.0 + 0.15 * jax.random.normal(splits[15], (D,), jnp.float32), 0.25, 1.75).astype(jnp.bfloat16)
    attn_bias = noise(splits[16], (D,), 0.3, 3.0, ((0, 32),))
    cross_gain = jnp.clip(1.0 + 0.15 * jax.random.normal(splits[17], (D,), jnp.float32), 0.25, 1.75).astype(jnp.bfloat16)
    cross_bias = noise(splits[18], (D,), 0.3, 3.0, ((0, 32),))
    feedforward_norm_gain = jnp.clip(1.0 + 0.15 * jax.random.normal(splits[19], (D,), jnp.float32), 0.25, 1.75).astype(jnp.bfloat16)
    ffn_bias = noise(splits[20], (D,), 0.3, 3.0, ((0, 32),))
    return {"tokens": tokens, "memory": memory, "cotangent": cotangent, "block_ids": block_ids, "seq_lengths": seq_lengths, "self_query": self_query, "self_key": self_key, "self_value": self_value, "self_out": self_out, "cross_query": cross_query, "cross_key": cross_key, "cross_value": cross_value, "cross_out": cross_out, "ffn_up": ffn_up, "ffn_down": ffn_down, "attn_gain": attn_gain, "attn_bias": attn_bias, "cross_gain": cross_gain, "cross_bias": cross_bias, "feedforward_norm_gain": feedforward_norm_gain, "ffn_bias": ffn_bias}


@jax.custom_vjp
def low(v):
    return lax.optimization_barrier(v.astype(jnp.bfloat16)).astype(jnp.float32)

@jax.custom_vjp
def low_back(v):
    return v

def low_keep(v):
    return (low(v), None)

def low_pass(kept, grad):
    return (grad,)

def back_keep(v):
    return (v, None)

def back_low(kept, grad):
    return (low(grad),)
low.defvjp(low_keep, low_pass)
low_back.defvjp(back_keep, back_low)
eps_norm = 1e-05
residual_scale = 18.0 ** 0.25
gelu_coef = 0.7978845608028654
highest = lax.Precision.HIGHEST

def gelu_tanh(values_in):
    inner = gelu_coef * (values_in + 0.044715 * values_in * values_in * values_in)
    return 0.5 * values_in * (1.0 + jnp.tanh(inner))

def rounded(value):
    return low_back(low(value))

def matmul(first_mat, second_mat):
    return jnp.dot(first_mat, second_mat, precision=highest, preferred_element_type=jnp.float32)

def layer_norm(values_in, gain_vec, bias_vec):
    average = lax.optimization_barrier(jnp.mean(values_in, axis=-1, keepdims=True))
    centred = values_in - average
    variance = lax.optimization_barrier(jnp.mean(centred * centred, axis=-1, keepdims=True))
    return centred * lax.rsqrt(variance + eps_norm) * gain_vec + bias_vec

def attend_rows(query_rows, key_heads, value_heads, allowed):
    scores = jnp.einsum('qhd,khd->hqk', query_rows, key_heads, precision=highest) * HEAD_DIM ** (-0.5)
    scores = low_back(scores)
    scores = jnp.where(allowed[None], scores, -1e+30)
    row_max = lax.optimization_barrier(jnp.max(scores, axis=-1, keepdims=True))
    expo_vals = jnp.exp(scores - row_max)
    attn_probs = expo_vals / lax.optimization_barrier(jnp.sum(expo_vals, axis=-1, keepdims=True))
    mixed_heads = jnp.einsum('hqk,khd->qhd', low(attn_probs), value_heads, precision=highest)
    return mixed_heads.reshape(mixed_heads.shape[0], HEADS * HEAD_DIM)

def blocked_attention(queries, key_rows, value_rows, query_ids, key_ids, key_live):
    total_rows = queries.shape[0]
    block_rows = min(512, total_rows)
    block_count = total_rows // block_rows
    query_heads = queries.reshape(block_count, block_rows, HEADS, HEAD_DIM)
    key_heads = key_rows.reshape(key_rows.shape[0], HEADS, HEAD_DIM)
    value_heads = value_rows.reshape(value_rows.shape[0], HEADS, HEAD_DIM)
    id_blocks = query_ids.reshape(block_count, block_rows)

    def one_block(packed):
        query_rows, row_ids = packed
        allowed = (key_ids[None, :] <= row_ids[:, None]) & key_live[None, :]
        return attend_rows(query_rows, key_heads, value_heads, allowed)
    mixed_rows = lax.map(jax.checkpoint(one_block), (query_heads, id_blocks))
    return mixed_rows.reshape(total_rows, HEADS * HEAD_DIM)

def layer(x_in, mem_in, params, seq_blocks, seq_length):
    self_query, self_key, self_value, self_out, cross_query, cross_key, cross_value, cross_out, ffn_up, ffn_down, attn_gain, attn_bias, cross_gain, cross_bias, feedforward_norm_gain, ffn_bias = params
    positions = jnp.arange(seq_blocks.shape[0])
    key_live = positions < seq_length
    queries = rounded(matmul(x_in, self_query))
    key_rows = rounded(matmul(x_in, self_key))
    value_rows = rounded(matmul(x_in, self_value))
    attended = rounded(blocked_attention(queries, key_rows, value_rows, seq_blocks, seq_blocks, key_live))
    branch_one = low_back(matmul(attended, self_out))
    hidden_one = low(layer_norm(residual_scale * x_in + branch_one, attn_gain, attn_bias))
    cross_rows = rounded(matmul(hidden_one, cross_query))
    mem_keys = rounded(matmul(mem_in, cross_key))
    mem_values = rounded(matmul(mem_in, cross_value))
    zero_ids = jnp.zeros(seq_blocks.shape, jnp.int32)
    mem_ids = jnp.zeros((mem_in.shape[0],), jnp.int32)
    mem_live = mem_ids == 0
    crossed = rounded(blocked_attention(cross_rows, mem_keys, mem_values, zero_ids, mem_ids, mem_live))
    branch_two = low_back(matmul(crossed, cross_out))
    hidden_two = low(layer_norm(residual_scale * hidden_one + branch_two, cross_gain, cross_bias))
    upper_rows = low_back(matmul(hidden_two, ffn_up))
    active_rows = low(gelu_tanh(upper_rows))
    branch_three = low_back(matmul(active_rows, ffn_down))
    return layer_norm(residual_scale * hidden_two + branch_three, feedforward_norm_gain, ffn_bias)

def reference(tokens, memory, cotangent, block_ids, seq_lengths, self_query, self_key, self_value, self_out, cross_query, cross_key, cross_value, cross_out, ffn_up, ffn_down, attn_gain, attn_bias, cross_gain, cross_bias, feedforward_norm_gain, ffn_bias):
    params = tuple((weight.astype(jnp.float32) for weight in (self_query, self_key, self_value, self_out, cross_query, cross_key, cross_value, cross_out, ffn_up, ffn_down, attn_gain, attn_bias, cross_gain, cross_bias, feedforward_norm_gain, ffn_bias)))

    def one_sequence(grad_sums, scan_items):
        seq_tokens, seq_memory, seq_cot, seq_blocks, seq_length = scan_items

        def forward(x_in, mem_in, weights_in):
            return layer(x_in, mem_in, weights_in, seq_blocks, seq_length)
        result, pullback = jax.vjp(forward, seq_tokens.astype(jnp.float32), seq_memory.astype(jnp.float32), params)
        grad_x, grad_mem, grad_weights = pullback(seq_cot.astype(jnp.float32))
        grad_sums = tuple((running + grad_item for running, grad_item in zip(grad_sums, grad_weights)))
        return (grad_sums, (result.astype(jnp.bfloat16), grad_x.astype(jnp.bfloat16), grad_mem.astype(jnp.bfloat16)))
    starts = tuple((jnp.zeros(weight.shape, jnp.float32) for weight in params))
    sums_all, outs_all = lax.scan(one_sequence, starts, (tokens, memory, cotangent, block_ids, seq_lengths))
    layer_out, tokens_grad, memory_grad = outs_all
    return (layer_out, tokens_grad, memory_grad, sums_all[0], sums_all[1], sums_all[2], sums_all[3], sums_all[4], sums_all[5], sums_all[6], sums_all[7], sums_all[8], sums_all[9], sums_all[10], sums_all[11], sums_all[12], sums_all[13], sums_all[14], sums_all[15])
```

```python
import jax
import jax.numpy as jnp
from jax import lax
from jax.experimental import pallas as pl
from jax.experimental.pallas import tpu as pltpu
from jax.sharding import Mesh, PartitionSpec as P

HEAD_DIM = 64
CORES = 2

eps_norm = 1e-05
residual_scale = 18.0**0.25
gelu_coef = 0.7978845608028654
neg_large = -1e30
bf16 = jnp.bfloat16
f32 = jnp.float32


def gelu_tanh(values_in):
    inner = gelu_coef * (values_in + 0.044715 * values_in * values_in * values_in)
    return 0.5 * values_in * (1.0 + jnp.tanh(inner))


def gelu_slope(values_in):
    squared = values_in * values_in
    tanh_val = jnp.tanh(gelu_coef * (values_in + 0.044715 * squared * values_in))
    return 0.5 * (1.0 + tanh_val) + 0.5 * values_in * (1.0 - tanh_val * tanh_val) * gelu_coef * (
        1.0 + 3.0 * 0.044715 * squared
    )


def matmul(first_mat, second_mat):
    return jnp.dot(first_mat, second_mat, preferred_element_type=f32)


def transposed_product(first_mat, second_mat):
    return lax.dot_general(first_mat, second_mat, (((1,), (1,)), ((), ())), preferred_element_type=f32)


def outer_product_sum(first_mat, second_mat):
    return lax.dot_general(first_mat, second_mat, (((0,), (0,)), ((), ())), preferred_element_type=f32)


def norm_forward(values_in):
    average = jnp.mean(values_in, axis=-1, keepdims=True)
    centred = values_in - average
    inv_std = lax.rsqrt(jnp.mean(centred * centred, axis=-1, keepdims=True) + eps_norm)
    return (centred * inv_std, inv_std)


def norm_backward(grad_out, normed, inv_std, gain_vec):
    scaled = grad_out * gain_vec
    grad_in = inv_std * (
        scaled
        - jnp.mean(scaled, axis=-1, keepdims=True)
        - normed * jnp.mean(scaled * normed, axis=-1, keepdims=True)
    )
    return (grad_in, jnp.sum(grad_out * normed, axis=0), jnp.sum(grad_out, axis=0))


def _head_mask(width, head):
    lane = lax.broadcasted_iota(jnp.int32, (1, width), 1)
    return (lane // HEAD_DIM) == head


def _attend_kernel(has_bias, *refs):
    if has_bias:
        q_ref, k_ref, v_ref, bias_ref, out_ref, probs_ref, acc_ref = refs
    else:
        q_ref, k_ref, v_ref, out_ref, probs_ref, acc_ref = refs
    head = pl.program_id(0)
    mask = _head_mask(q_ref.shape[1], head)
    q = jnp.where(mask, q_ref[...].astype(f32) * HEAD_DIM ** (-0.5), 0.0).astype(bf16)
    scores = lax.dot_general(q, k_ref[...], (((1,), (1,)), ((), ())), preferred_element_type=f32)
    if has_bias:
        scores = scores + bias_ref[...]
    expo = jnp.exp(scores - jnp.max(scores, axis=-1, keepdims=True))
    probs = (expo / jnp.sum(expo, axis=-1, keepdims=True)).astype(bf16)
    probs_ref[0] = probs
    mixed = jnp.dot(probs, v_ref[...], preferred_element_type=f32)

    @pl.when(head == 0)
    def _():
        acc_ref[...] = mixed

    @pl.when(head != 0)
    def _():
        acc_ref[...] = jnp.where(mask, mixed, acc_ref[...])

    out_ref[...] = acc_ref[...].astype(bf16)


def attention_forward(queries, keys, values, bias):
    rows, width = queries.shape
    keys_rows = keys.shape[0]
    heads = width // HEAD_DIM
    whole = lambda shape: pl.BlockSpec(shape, lambda h: (0,) * len(shape))
    ins = [queries, keys, values] + ([] if bias is None else [bias])
    return pl.pallas_call(
        lambda *refs: _attend_kernel(bias is not None, *refs),
        grid=(heads,),
        in_specs=[whole(x.shape) for x in ins],
        out_specs=[whole((rows, width)), pl.BlockSpec((1, rows, keys_rows), lambda h: (h, 0, 0))],
        out_shape=[
            jax.ShapeDtypeStruct((rows, width), bf16),
            jax.ShapeDtypeStruct((heads, rows, keys_rows), bf16),
        ],
        scratch_shapes=[pltpu.VMEM((rows, width), f32)],
        compiler_params=pltpu.CompilerParams(vmem_limit_bytes=56 * 1024 * 1024),
        name="attend",
    )(*ins)


def _attend_back_kernel(q_ref, k_ref, v_ref, p_ref, g_ref, dq_ref, dk_ref, dv_ref, aq, ak, av):
    head = pl.program_id(0)
    mask = _head_mask(q_ref.shape[1], head)
    zero = jnp.zeros((), bf16)
    g = jnp.where(mask, g_ref[...], zero)
    k = jnp.where(mask, k_ref[...], zero)
    q = jnp.where(mask, q_ref[...], zero)
    probs = p_ref[0]
    g_probs = lax.dot_general(g, v_ref[...], (((1,), (1,)), ((), ())), preferred_element_type=f32)
    wide = probs.astype(f32)
    row_dot = jnp.sum(g_probs * wide, axis=-1, keepdims=True)
    g_scores = (wide * (g_probs - row_dot)).astype(bf16)
    dq = jnp.dot(g_scores, k, preferred_element_type=f32) * HEAD_DIM ** (-0.5)
    dk = lax.dot_general(g_scores, q, (((0,), (0,)), ((), ())), preferred_element_type=f32) * HEAD_DIM ** (-0.5)
    dv = lax.dot_general(probs, g, (((0,), (0,)), ((), ())), preferred_element_type=f32)

    @pl.when(head == 0)
    def _():
        aq[...] = dq
        ak[...] = dk
        av[...] = dv

    @pl.when(head != 0)
    def _():
        aq[...] += dq
        ak[...] += dk
        av[...] += dv

    @pl.when(head == pl.num_programs(0) - 1)
    def _():
        dq_ref[...] = aq[...].astype(bf16)
        dk_ref[...] = ak[...].astype(bf16)
        dv_ref[...] = av[...].astype(bf16)


def attention_backward(queries, keys, values, probs, grad_mixed):
    rows, width = queries.shape
    keys_rows = keys.shape[0]
    heads = width // HEAD_DIM
    whole = lambda shape: pl.BlockSpec(shape, lambda h: (0,) * len(shape))
    return pl.pallas_call(
        _attend_back_kernel,
        grid=(heads,),
        in_specs=[
            whole(queries.shape),
            whole(keys.shape),
            whole(values.shape),
            pl.BlockSpec((1, rows, keys_rows), lambda h: (h, 0, 0)),
            whole(grad_mixed.shape),
        ],
        out_specs=[whole((rows, width)), whole((keys_rows, width)), whole((keys_rows, width))],
        out_shape=[
            jax.ShapeDtypeStruct((rows, width), bf16),
            jax.ShapeDtypeStruct((keys_rows, width), bf16),
            jax.ShapeDtypeStruct((keys_rows, width), bf16),
        ],
        scratch_shapes=[
            pltpu.VMEM((rows, width), f32),
            pltpu.VMEM((keys_rows, width), f32),
            pltpu.VMEM((keys_rows, width), f32),
        ],
        compiler_params=pltpu.CompilerParams(vmem_limit_bytes=56 * 1024 * 1024),
        name="attend_back",
    )(queries, keys, values, probs, grad_mixed)


def swap(values, name, size, flip):
    return lax.ppermute(values, name, [(i, i ^ flip) for i in range(size)])


def flip_bits(size):
    return [1 << b for b in range(size.bit_length() - 1)]


def tie(value, *others):
    return lax.optimization_barrier((value,) + others)[0]


SMALL = pltpu.CompilerParams(vmem_limit_bytes=56 * 1024 * 1024)
SCALAR = pl.BlockSpec(memory_space=pltpu.SMEM)
WHOLE = pl.BlockSpec(memory_space=pltpu.VMEM)


def lay_out(ranks, query, key, value, mem_key, mem_value, cross, up, own_out, mem_out):
    rows, width = query.shape
    part = width // ranks
    ff_part = up.shape[1] // ranks
    groups = ff_part * ranks // up.shape[1] * (width // (ranks * rows))
    unit = ff_part // groups

    def kernel(*refs):
        ins, (self_ref, cross_ref, up_ref, so_ref, co_ref) = refs[:9], refs[9:]
        for r in range(ranks):
            cols = slice(r * part, (r + 1) * part)
            for i in range(3):
                self_ref[r, :, i * part : (i + 1) * part] = ins[i][:, cols]
                cross_ref[r, :, i * part : (i + 1) * part] = ins[3 + i][:, cols]
            so_ref[r] = ins[7][:, cols]
            co_ref[r] = ins[8][:, cols]
            for g in range(groups):
                first = (g * ranks + r) * unit
                up_ref[r, :, g * unit : (g + 1) * unit] = ins[6][:, first : first + unit]

    shapes = [3 * part, 3 * part, ff_part, part, part]
    return pl.pallas_call(
        kernel,
        in_specs=[WHOLE] * 9,
        out_specs=[WHOLE] * 5,
        out_shape=[jax.ShapeDtypeStruct((ranks, rows, n), bf16) for n in shapes],
        compiler_params=SMALL,
        name="lay_out",
    )(query, key, value, mem_key, mem_value, cross, up, own_out, mem_out)


def columns_back(pieces, counts, unit_first):
    ranks, rows, _ = pieces.shape

    def kernel(in_ref, *outs):
        first = 0
        for out, count in zip(outs, counts):
            if out is outs[0] and unit_first:
                units = count // unit_first
                for r in range(ranks):
                    for g in range(units):
                        at = (g * ranks + r) * unit_first
                        out[:, at : at + unit_first] = in_ref[
                            r, :, first + g * unit_first : first + (g + 1) * unit_first
                        ].astype(f32)
            else:
                for r in range(ranks):
                    out[:, r * count : (r + 1) * count] = in_ref[r, :, first : first + count].astype(f32)
            first += count

    return pl.pallas_call(
        kernel,
        in_specs=[WHOLE],
        out_specs=[WHOLE] * len(counts),
        out_shape=[jax.ShapeDtypeStruct((rows, ranks * n), f32) for n in counts],
        compiler_params=SMALL,
        name="columns_back",
    )(pieces)


def join_rows(pieces, rank):
    ranks = len(pieces)
    sets, blocks, rows, part = pieces[0].shape

    def kernel(rank_ref, *refs):
        out = refs[-1]
        for r in range(ranks):
            at = rank_ref[0] ^ r
            for p in range(sets):
                for b in range(blocks):
                    out[p, at, :, b * part : (b + 1) * part] = refs[r][p, b]

    joined = pl.pallas_call(
        kernel,
        in_specs=[SCALAR] + [WHOLE] * ranks,
        out_specs=WHOLE,
        out_shape=jax.ShapeDtypeStruct((sets, ranks, rows, blocks * part), bf16),
        compiler_params=SMALL,
        name="join_rows",
    )(rank.reshape(1), *pieces)
    return joined.reshape(sets * ranks * rows, blocks * part)


def pack_grads(columns, pieces, rank):
    groups, n, m = columns.shape
    ranks = len(pieces)
    sets, rows, width = pieces[0].shape
    part = width // ranks

    def kernel(rank_ref, col_ref, *refs):
        out = refs[-1]
        out[:, :, :m] = col_ref[...]
        for r in range(ranks):
            at = (rank_ref[0] ^ r) * sets
            for p in range(sets):
                for b in range(ranks):
                    out[at + p, b * rows : (b + 1) * rows, m:] = refs[r][p, :, b * part : (b + 1) * part]

    return pl.pallas_call(
        kernel,
        in_specs=[SCALAR] + [WHOLE] * (ranks + 1),
        out_specs=WHOLE,
        out_shape=jax.ShapeDtypeStruct((groups, n, m + part), bf16),
        compiler_params=SMALL,
        name="pack_grads",
    )(rank.reshape(1), columns, *pieces)


def make_body(dp_size, g_size, z_size):
    ranks = z_size * CORES
    groups = dp_size * g_size
    every = ("dp", "g", "z", "c")

    def body(
        tokens,
        memory,
        cotangent,
        block_ids,
        seq_lengths,
        self_query,
        self_key,
        self_value,
        self_out,
        cross_query,
        cross_key,
        cross_value,
        cross_out,
        ffn_up,
        ffn_down,
        attn_gain,
        attn_bias,
        cross_gain,
        cross_bias,
        feedforward_norm_gain,
        ffn_bias,
    ):
        dp_own = lax.axis_index("dp")
        g_own = lax.axis_index("g")
        rank_own = lax.axis_index("z") * CORES + lax.axis_index("c")
        piece_rows = tokens.shape[1]
        width = tokens.shape[2]
        weight_rows = self_query.shape[0]
        rank_rows = ranks * weight_rows
        part = width // ranks
        sets = groups // ranks
        ff_rows = ffn_down.shape[0]
        ff_part = groups * ff_rows
        ff_blocks = width // ff_part

        def bits_of(name, size, own):
            return [(name, size, f, (own // f) % 2) for f in reversed(flip_bits(size))]

        axes = bits_of("dp", dp_size, dp_own) + bits_of("g", g_size, g_own)
        n_dp = dp_size.bit_length() - 1
        g_axes = list(range(n_dp, len(axes)))
        order_a = list(reversed(range(n_dp)))
        order_b = list(range(n_dp))

        def gather_axes(values, dims, order):
            for ax in order:
                name, size, flip, bit = axes[ax]
                other = swap(values, name, size, flip)
                pos = len([d for d in dims if d < ax])
                values = jnp.where(
                    bit == 1, jnp.stack([other, values], pos), jnp.stack([values, other], pos)
                )
                dims = sorted(dims + [ax])
            return values

        def scatter_axes(values, dims, order):
            dims = list(dims)
            for i, ax in enumerate(order):
                name, size, flip, bit = axes[ax]
                pos = dims.index(ax)
                other = swap(
                    lax.dynamic_index_in_dim(values, 1 - bit, pos, keepdims=False), name, size, flip
                )
                kept = lax.dynamic_index_in_dim(values, bit, pos, keepdims=False)
                values = kept.astype(f32) + other.astype(f32)
                dims.remove(ax)
                if dims:
                    values = values.astype(bf16)
            return values

        def halves(n):
            return (2,) * n

        def finish(values):
            shape = values.shape[1:]
            return scatter_axes(values.reshape(halves(len(g_axes)) + shape), g_axes, g_axes)

        def rank_swap(values, flip):
            return swap(values, ("z", "c"), ranks, flip)

        def from_ranks(pieces, axis):
            got = []
            for f in range(ranks):
                piece = lax.dynamic_index_in_dim(pieces, rank_own ^ f, axis, keepdims=False)
                got.append(piece if f == 0 else rank_swap(piece, f))
            return got

        def gather_rows(values):
            blocks = [values]
            for flip in flip_bits(z_size):
                blocks = blocks + [swap(b, "z", z_size, flip) for b in blocks]
            blocks = blocks + [swap(b, "c", CORES, 1) for b in blocks]
            return jnp.concatenate(blocks, axis=0)

        def sum_rows(parts, product):
            half = parts[0].shape[0] // 2
            leaving = product([x[half:] for x in parts]).astype(bf16)
            staying = product([x[:half] for x in parts])
            own_rows = half // z_size
            sums = [None] * z_size
            for b in reversed(range(z_size)):
                rows = slice(b * own_rows, (b + 1) * own_rows)
                sums[b] = staying[rows] + swap(leaving[rows], "c", CORES, 1).astype(f32)
            for flip in reversed(flip_bits(z_size)):
                sums = [
                    sums[b] + swap(sums[b + flip].astype(bf16), "z", z_size, flip).astype(f32)
                    for b in range(flip)
                ]
            return sums[0]

        def bring_home(values):
            got = []
            for f in range(g_size):
                piece = lax.dynamic_index_in_dim(values, g_own ^ f, 0, keepdims=False)
                got.append(piece if f == 0 else swap(piece, "g", g_size, f))
            return jnp.concatenate(got, axis=-2)

        def send_back(values):
            blocks = values.reshape(g_size, piece_rows, width)
            got = [blocks[0]] + [swap(blocks[f], "g", g_size, f) for f in range(1, g_size)]
            got = jnp.stack(got)
            return jnp.stack(
                [lax.dynamic_index_in_dim(got, g_own ^ f, 0, keepdims=False) for f in range(g_size)]
            )

        own_tokens = bring_home(tokens)
        self_parts, cross_parts, up_parts, so_parts, co_parts = lay_out(
            ranks,
            self_query,
            self_key,
            self_value,
            cross_key,
            cross_value,
            cross_query,
            ffn_up,
            self_out,
            cross_out,
        )

        def to_ranks(parts_in):
            return lax.all_to_all(parts_in, ("z", "c"), 0, 0, tiled=True)

        self_own = to_ranks(self_parts)
        self_set = jnp.concatenate([self_own, so_parts], axis=2).reshape(rank_rows, 4 * part)
        self_set = gather_axes(self_set, [], g_axes)
        other_own = to_ranks(tie(jnp.concatenate([cross_parts, up_parts], axis=2), self_own))
        vectors = jnp.stack(
            [attn_gain, attn_bias, cross_gain, cross_bias, feedforward_norm_gain, ffn_bias]
        )
        vectors = jnp.broadcast_to(vectors[None], (groups * ranks,) + vectors.shape)
        vectors = lax.all_to_all(tie(vectors, other_own), every, 0, 0, tiled=True)
        vectors = vectors.transpose(1, 0, 2).reshape(6, width).astype(f32)
        gain_one, bias_one, gain_two, bias_two, gain_three, bias_three = [
            vectors[i : i + 1] for i in range(6)
        ]
        all_tokens = gather_rows(own_tokens)

        set_a = gather_axes(self_set[..., : 2 * part], g_axes, order_a)
        set_b = gather_axes(self_set[..., 2 * part :], g_axes, order_b)
        w_qk = set_a.reshape(width, 2 * part)
        set_b = set_b.reshape(groups, rank_rows, 2 * part)
        w_v = set_b[..., :part].reshape(width, part)

        other_own, _ = lax.optimization_barrier((other_own, self_set))
        cross_set = jnp.concatenate([other_own[..., : 3 * part], co_parts], axis=2)
        cross_set = gather_axes(cross_set.reshape(rank_rows, 4 * part), [], g_axes)
        own_memory = bring_home(tie(memory, cross_set))
        down_rows = ffn_down.reshape(ff_rows, ff_blocks, ff_part).transpose(1, 0, 2)
        ffn_set = jnp.concatenate(
            [
                other_own[..., 3 * part :].reshape(rank_rows, ff_part),
                down_rows.reshape(rank_rows, ff_part),
            ],
            axis=0,
        )
        ffn_set = gather_axes(tie(ffn_set, own_memory), [], g_axes)
        own_cotangent = bring_home(tie(cotangent, ffn_set))
        cross_set = lax.all_gather(cross_set.reshape(g_size * rank_rows, 4 * part), "dp", axis=0, tiled=True)
        cross_set = cross_set.reshape(groups, rank_rows, 4 * part)
        ffn_set = lax.all_gather(ffn_set.reshape(g_size * 2 * rank_rows, ff_part), "dp", axis=0, tiled=True)
        ffn_set = ffn_set.reshape(groups, 2, rank_rows, ff_part)

        def out_rows(rows_in):
            pieces = rows_in.reshape(ranks, sets, ranks, weight_rows, part)
            return join_rows(from_ranks(pieces, 0), rank_own)

        w_sout = out_rows(set_b[..., part:])

        n_pieces = g_size * ranks
        seq_own = g_own * ranks + rank_own
        ids = lax.dynamic_index_in_dim(block_ids, g_own, 0, keepdims=False)
        length = lax.dynamic_index_in_dim(seq_lengths, g_own, 0, keepdims=False)
        live = jnp.arange(ids.shape[0], dtype=jnp.int32) < length
        both = jnp.stack([ids, jnp.where(live, ids, jnp.int32(2**30))]).reshape(2, n_pieces, piece_rows)
        for flip in flip_bits(n_pieces):
            turned = both.reshape(2, n_pieces // (2 * flip), 2, flip, piece_rows)
            turned = jnp.concatenate([turned[:, :, 1:], turned[:, :, :1]], axis=2).reshape(both.shape)
            both = jnp.where((seq_own & flip) != 0, turned, both)
        both = both.reshape(2, g_size, z_size, CORES, piece_rows).transpose(0, 3, 2, 1, 4).reshape(2, -1)
        bias = jnp.where(both[1][None, :] <= both[0][:, None], 0.0, neg_large).astype(f32)

        qk = matmul(all_tokens, w_qk).astype(bf16)
        queries, keys = qk[:, :part], qk[:, part:]
        values = matmul(all_tokens, w_v).astype(bf16)
        attended, self_probs = attention_forward(queries, keys, values, bias)
        branch = sum_rows([attended], lambda x: matmul(x[0], w_sout))
        normed_one, inv_one = norm_forward(residual_scale * own_tokens.astype(f32) + branch)
        hidden_one = (normed_one * gain_one + bias_one).astype(bf16)

        all_memory = gather_rows(own_memory)
        w_ckv = cross_set[..., : 2 * part].reshape(width, 2 * part)
        w_cq = cross_set[..., 2 * part : 3 * part].reshape(width, part)
        w_cout = out_rows(cross_set[..., 3 * part :])
        mem_kv = matmul(all_memory, w_ckv).astype(bf16)
        mem_keys, mem_values = mem_kv[:, :part], mem_kv[:, part:]

        all_one = gather_rows(hidden_one)
        cross_rows = matmul(all_one, w_cq).astype(bf16)
        crossed, cross_probs = attention_forward(cross_rows, mem_keys, mem_values, None)
        branch = sum_rows([crossed], lambda x: matmul(x[0], w_cout))
        normed_two, inv_two = norm_forward(residual_scale * hidden_one.astype(f32) + branch)
        hidden_two = (normed_two * gain_two + bias_two).astype(bf16)
        all_two = gather_rows(hidden_two)
        w_up = ffn_set[:, 0].reshape(width, ff_part)
        w_down = ffn_set[:, 1].reshape(groups, ff_blocks, ff_rows, ff_part).transpose(0, 2, 1, 3)
        w_down = w_down.reshape(ff_part, width)
        upper_rows = matmul(all_two, w_up)
        active_rows = gelu_tanh(upper_rows).astype(bf16)
        branch = sum_rows([active_rows], lambda x: matmul(x[0], w_down))
        slope_rows = lax.optimization_barrier(gelu_slope(tie(upper_rows, active_rows)))
        normed_three, inv_three = norm_forward(residual_scale * hidden_two.astype(f32) + branch)
        layer_rows = (normed_three * gain_three + bias_three).astype(bf16)
        layer_out = send_back(layer_rows)

        grad_three, gain_three_grad, bias_three_grad = norm_backward(
            own_cotangent.astype(f32), normed_three, inv_three, gain_three
        )
        all_branch = gather_rows(grad_three.astype(bf16))
        grad_upper = (transposed_product(all_branch, w_down) * slope_rows).astype(bf16)
        branch = sum_rows([grad_upper], lambda x: transposed_product(x[0], w_up))
        down_grad = outer_product_sum(active_rows, all_branch).astype(bf16)
        down_grad = down_grad.reshape(groups, ff_rows, ff_blocks, ff_part).transpose(0, 2, 1, 3)
        up_grad = outer_product_sum(all_two, grad_upper).astype(bf16)
        ffn_grads = jnp.concatenate(
            [up_grad.reshape(groups, rank_rows, ff_part), down_grad.reshape(groups, rank_rows, ff_part)],
            axis=1,
        )
        branch = tie(branch, ffn_grads)
        ffn_grads = lax.psum_scatter(
            ffn_grads.reshape(groups * 2 * rank_rows, ff_part), "dp", scatter_dimension=0, tiled=True
        )
        grad_two, gain_two_grad, bias_two_grad = norm_backward(
            residual_scale * grad_three + branch, normed_two, inv_two, gain_two
        )

        all_branch = gather_rows(grad_two.astype(bf16))
        grad_crossed = transposed_product(all_branch, w_cout).astype(bf16)
        cout_grad = outer_product_sum(crossed, all_branch).astype(bf16)
        grad_cross_rows, grad_mem_keys, grad_mem_values = attention_backward(
            cross_rows, mem_keys, mem_values, cross_probs, grad_crossed
        )
        branch = sum_rows([grad_cross_rows], lambda x: transposed_product(x[0], w_cq))
        grad_mem_kv = jnp.concatenate([grad_mem_keys, grad_mem_values], axis=1)
        cout_pieces = from_ranks(cout_grad.reshape(sets, ranks, weight_rows, width), 1)
        cross_grads = jnp.concatenate(
            [outer_product_sum(all_memory, grad_mem_kv), outer_product_sum(all_one, grad_cross_rows)], axis=1
        ).astype(bf16)
        cross_grads = pack_grads(cross_grads.reshape(groups, rank_rows, 3 * part), cout_pieces, rank_own)
        branch = tie(branch, cross_grads)
        cross_grads = lax.psum_scatter(
            cross_grads.reshape(groups * rank_rows, 4 * part), "dp", scatter_dimension=0, tiled=True
        )
        memory_rows = sum_rows([tie(grad_mem_kv, branch)], lambda x: transposed_product(x[0], w_ckv))
        memory_grad = send_back(memory_rows.astype(bf16))

        grad_one, gain_one_grad, bias_one_grad = norm_backward(
            residual_scale * grad_two + branch, normed_one, inv_one, gain_one
        )
        sums = jnp.stack(
            [gain_one_grad, bias_one_grad, gain_two_grad, bias_two_grad, gain_three_grad, bias_three_grad]
        )
        sums = sums.reshape(6, groups * ranks, weight_rows).transpose(1, 0, 2)
        vec_grads = jnp.sum(lax.all_to_all(sums, every, 0, 0, tiled=True), axis=0)

        all_branch = gather_rows(grad_one.astype(bf16))
        grad_attended = transposed_product(all_branch, w_sout).astype(bf16)
        sout_grad = outer_product_sum(attended, all_branch).astype(bf16)
        grad_queries, grad_keys, grad_values = attention_backward(
            queries, keys, values, self_probs, grad_attended
        )
        ffn_grads = finish(tie(ffn_grads, grad_attended).reshape(g_size, 2 * rank_rows, ff_part))
        up_pieces = to_ranks(ffn_grads[:rank_rows].astype(bf16).reshape(ranks, weight_rows, ff_part))
        sout_pieces = from_ranks(sout_grad.reshape(sets, ranks, weight_rows, width), 1)
        grad_qkv = jnp.concatenate([grad_queries, grad_keys, grad_values], axis=1)
        grad_qkv = tie(grad_qkv, up_pieces)
        self_grads = outer_product_sum(all_tokens, grad_qkv).astype(bf16)
        self_grads = pack_grads(self_grads.reshape(groups, rank_rows, 3 * part), sout_pieces, rank_own)
        self_grads = self_grads.reshape(halves(len(axes)) + (rank_rows, 4 * part))
        dims = list(range(len(axes)))
        half_a = scatter_axes(self_grads[..., : 2 * part], dims, order_a + g_axes)
        half_b = scatter_axes(self_grads[..., 2 * part :], dims, order_b + g_axes)
        branch = sum_rows(
            [grad_qkv],
            lambda x: transposed_product(x[0][:, : 2 * part], w_qk)
            + transposed_product(x[0][:, 2 * part :], w_v),
        )
        tokens_grad = send_back((residual_scale * grad_one + branch).astype(bf16))

        cross_grads = finish(tie(cross_grads, half_a).reshape(g_size, rank_rows, 4 * part))
        down_grad = ffn_grads[rank_rows:].reshape(ff_blocks, ff_rows, ff_part).transpose(1, 0, 2)
        down_grad = down_grad.reshape(ff_rows, width)

        def own_rows_of(values):
            return values.reshape(ranks, weight_rows, part).transpose(1, 0, 2).reshape(weight_rows, width)

        (up_grad,) = columns_back(up_pieces, (ff_part,), ff_rows)
        pieces = jnp.concatenate([half_a, half_b[:, :part], cross_grads[:, : 3 * part]], axis=1).astype(bf16)
        pieces = to_ranks(pieces.reshape(ranks, weight_rows, 6 * part))
        query_grad, key_grad, value_grad, mem_key_grad, mem_value_grad, cross_grad = columns_back(
            pieces, (part,) * 6, 0
        )

        return (
            layer_out,
            tokens_grad,
            memory_grad,
            query_grad,
            key_grad,
            value_grad,
            own_rows_of(half_b[:, part:]),
            cross_grad,
            mem_key_grad,
            mem_value_grad,
            own_rows_of(cross_grads[:, 3 * part :]),
            up_grad,
            down_grad,
            vec_grads[0],
            vec_grads[1],
            vec_grads[2],
            vec_grads[3],
            vec_grads[4],
            vec_grads[5],
        )

    return body


def solution(mesh):
    dp_size, seq_size = mesh.shape["dp"], mesh.shape["seq"]

    def layer_step(*args):
        g_size = args[0].shape[0] // dp_size
        z_size = seq_size // (g_size * CORES)
        split_mesh = Mesh(
            mesh.devices.reshape(dp_size, g_size, z_size, CORES), ("dp", "g", "z", "c")
        )
        seq = ("g", "z", "c")
        every = ("dp", "g", "z", "c")
        rows = P("dp", seq, None)
        matrix = P(every, None)
        vector = P(every)
        return jax.shard_map(
            make_body(dp_size, g_size, z_size),
            mesh=split_mesh,
            in_specs=(rows,) * 3 + (P("dp", None), P("dp")) + (matrix,) * 10 + (vector,) * 6,
            out_specs=(rows,) * 3 + (matrix,) * 10 + (vector,) * 6,
            check_vma=False,
        )(*args)

    return layer_step
```

```python
import jax
import jax.numpy as jnp
from jax import lax
from jax.experimental import pallas as pl
from jax.experimental.pallas import tpu as pltpu
from jax.sharding import Mesh, PartitionSpec as P

HEAD_DIM = 64
CORES = 2

eps_norm = 1e-05
residual_scale = 18.0**0.25
gelu_coef = 0.7978845608028654
neg_large = -1e30
bf16 = jnp.bfloat16
f32 = jnp.float32


def gelu_tanh(values_in):
    inner = gelu_coef * (values_in + 0.044715 * values_in * values_in * values_in)
    return 0.5 * values_in * (1.0 + jnp.tanh(inner))


def gelu_slope(values_in):
    squared = values_in * values_in
    tanh_val = jnp.tanh(gelu_coef * (values_in + 0.044715 * squared * values_in))
    return 0.5 * (1.0 + tanh_val) + 0.5 * values_in * (1.0 - tanh_val * tanh_val) * gelu_coef * (
        1.0 + 3.0 * 0.044715 * squared
    )


def matmul(first_mat, second_mat):
    return jnp.dot(first_mat, second_mat, preferred_element_type=f32)


def transposed_product(first_mat, second_mat):
    return lax.dot_general(first_mat, second_mat, (((1,), (1,)), ((), ())), preferred_element_type=f32)


def outer_product_sum(first_mat, second_mat):
    return lax.dot_general(first_mat, second_mat, (((0,), (0,)), ((), ())), preferred_element_type=f32)


LIMIT = pltpu.CompilerParams(vmem_limit_bytes=16 * 1024 * 1024)
ALL_OF_IT = pltpu.CompilerParams(vmem_limit_bytes=60 * 1024 * 1024)
SCALAR = pl.BlockSpec(memory_space=pltpu.SMEM)
WHOLE = pl.BlockSpec(memory_space=pltpu.VMEM)


def on_chip(values):
    return pltpu.with_memory_space_constraint(values, pltpu.VMEM)


def chip_call(kernel, outs, name, *args, scalar=None):
    scalars = [] if scalar is None else [scalar.reshape(1)]
    return pl.pallas_call(
        kernel,
        in_specs=[SCALAR] * len(scalars) + [WHOLE] * len(args),
        out_specs=[WHOLE] * len(outs),
        out_shape=[pltpu.VMEM(shape, dtype) for shape, dtype in outs],
        compiler_params=LIMIT,
        name=name,
    )(*scalars, *[on_chip(x) for x in args])


ANY = pl.BlockSpec(memory_space=pl.ANY)
FAR = pl.BlockSpec(memory_space=pltpu.HBM)


def copy_call(copies, out, name, scalar, *args):
    count = []

    def kernel(scalar_ref, *refs):
        sems = refs[-1]
        running = [
            pltpu.make_async_copy(source, target, sems.at[i])
            for i, (source, target) in enumerate(copies(scalar_ref[0], refs[:-2], refs[-2]))
        ]
        for one in running:
            one.start()
        for one in running:
            one.wait()

    class Probe:
        at = property(lambda self: self)

        def __getitem__(self, index):
            return self

    count = len(copies(0, [Probe()] * len(args), Probe()))
    return pl.pallas_call(
        kernel,
        in_specs=[SCALAR] + [ANY] * len(args),
        out_specs=ANY,
        out_shape=jax.ShapeDtypeStruct(*out),
        scratch_shapes=[pltpu.SemaphoreType.DMA((count,))],
        compiler_params=LIMIT,
        name=name,
    )(scalar.reshape(1), *args)


def _mean(values):
    return jnp.mean(values, axis=-1, keepdims=True)


def _normed(residual, kept, came):
    values = residual_scale * residual.astype(f32) + (kept + came.astype(f32))
    centred = values - _mean(values)
    inv_std = lax.rsqrt(_mean(centred * centred) + eps_norm)
    return centred * inv_std, inv_std


def _norm_back(grad_out, normed, inv_std, gain):
    scaled = grad_out * gain
    grad_in = inv_std * (scaled - _mean(scaled) - normed * _mean(scaled * normed))
    sums = [jnp.sum(grad_out * normed, axis=0, keepdims=True), jnp.sum(grad_out, axis=0, keepdims=True)]
    return grad_in, jnp.concatenate(sums, axis=0)


def norm_rows(residual, kept, came, vectors, row):
    def kernel(res, kept, came, vec, hidden, normed, inv):
        n, r = _normed(res[...], kept[...], came[...])
        hidden[...] = (n * vec[row : row + 1, :] + vec[row + 1 : row + 2, :]).astype(bf16)
        normed[...] = n
        inv[...] = jnp.broadcast_to(r, inv.shape)

    shape = residual.shape
    outs = [(shape, bf16), (shape, f32), ((shape[0], 128), f32)]
    return chip_call(kernel, outs, "norm_rows", residual, kept, came, vectors)


def norm_turn(residual, kept, came, vectors, row, cotangent):
    def kernel(res, kept, came, vec, cot, layer, grad, rounded, sums):
        gain = vec[row : row + 1, :]
        n, r = _normed(res[...], kept[...], came[...])
        layer[...] = (n * gain + vec[row + 1 : row + 2, :]).astype(bf16)
        g, s = _norm_back(cot[...].astype(f32), n, r, gain)
        grad[...] = g
        rounded[...] = g.astype(bf16)
        sums[...] = s

    shape = residual.shape
    outs = [(shape, bf16), (shape, f32), (shape, bf16), ((2, shape[1]), f32)]
    return chip_call(kernel, outs, "norm_turn", residual, kept, came, vectors, cotangent)


def norm_back(grad_prev, kept, came, normed, inv_std, vectors, row):
    shape = grad_prev.shape
    args = [grad_prev, kept, came, normed, inv_std]

    def kernel(*refs):
        vec, grad, rounded, sums = refs[5:9]
        prev, kept, came, normed, inv = refs[9:14]
        running = [pltpu.make_async_copy(refs[i], refs[9 + i], refs[14].at[i]) for i in range(5)]
        for one in running:
            one.start()
        for one in running:
            one.wait()
        grad_out = residual_scale * prev[...] + (kept[...] + came[...].astype(f32))
        g, s = _norm_back(grad_out, normed[...], inv[:, :1], vec[row : row + 1, :])
        grad[...] = g
        rounded[...] = g.astype(bf16)
        sums[...] = s

    outs = [(shape, f32), (shape, bf16), ((2, shape[1]), f32)]
    return pl.pallas_call(
        kernel,
        in_specs=[FAR] * 5 + [WHOLE],
        out_specs=[WHOLE] * 3,
        out_shape=[pltpu.VMEM(x, dtype) for x, dtype in outs],
        scratch_shapes=[pltpu.VMEM(x.shape, x.dtype) for x in args] + [pltpu.SemaphoreType.DMA((5,))],
        compiler_params=LIMIT,
        name="norm_back",
    )(*args, on_chip(vectors))


PAIR = 2 * HEAD_DIM


def _head_of_pair(values, head):
    lane = lax.broadcasted_iota(jnp.int32, (1, PAIR), 1)
    return jnp.where((lane // HEAD_DIM) == head, values, jnp.zeros((), values.dtype))


def _times(first, second, dims):
    return lax.dot_general(first, second, ((dims[:1], dims[1:]), ((), ())), preferred_element_type=f32)


def attention_forward(queries, keys, values, bias):
    rows, width = queries.shape
    key_rows = keys.shape[0]
    scale = HEAD_DIM ** (-0.5)

    def kernel(q_ref, k_ref, v_ref, *rest):
        out_ref, probs_ref = rest[-2:]
        for pair in range(width // PAIR):
            cols = slice(pair * PAIR, (pair + 1) * PAIR)
            q, k, v = q_ref[:, cols] * jnp.asarray(scale, bf16), k_ref[:, cols], v_ref[:, cols]
            mixed = None
            for head in range(2):
                scores = _times(k, _head_of_pair(q, head), (1, 1))
                if bias is not None:
                    scores = scores + rest[0][...]
                expo = jnp.exp(scores - jnp.max(scores, axis=0, keepdims=True))
                probs = (expo * (1.0 / jnp.sum(expo, axis=0, keepdims=True))).astype(bf16)
                probs_ref[2 * pair + head] = probs
                part = _times(_head_of_pair(v, head), probs, (0, 0))
                mixed = part if mixed is None else mixed + part
            out_ref[:, cols] = mixed.T.astype(bf16)

    args = [queries, keys, values] + ([] if bias is None else [bias])
    outs = [((rows, width), bf16), ((width // HEAD_DIM, key_rows, rows), bf16)]
    return chip_call(kernel, outs, "attend", *args)


def attention_backward(queries, keys, values, probs, first, grad_mixed, sums, last):
    rows, width = queries.shape
    key_rows = keys.shape[0]
    scale = HEAD_DIM ** (-0.5)

    def kernel(q_ref, k_ref, v_ref, p_ref, g_ref, *rest):
        before, (dq_ref, dk_ref, dv_ref) = rest[: len(sums)], rest[len(sums) :]
        for pair in range(width // PAIR):
            cols = slice(pair * PAIR, (pair + 1) * PAIR)
            q, k, v, g = q_ref[:, cols], k_ref[:, cols], v_ref[:, cols], g_ref[:, cols]
            dq = None
            dk, dv = [x[:, cols] for x in before] if sums else (None, None)
            for head in range(2):
                g_one = _head_of_pair(g, head)
                rounded = p_ref[2 * pair + head, :, first : first + rows]
                wide = rounded.astype(f32)
                weighted = _times(v, g_one, (1, 1)) * wide
                g_scores = (weighted - wide * jnp.sum(weighted, axis=0, keepdims=True)).astype(bf16)
                part_q = _times(_head_of_pair(k, head), g_scores, (0, 0))
                part_k = _times(g_scores, _head_of_pair(q, head), (1, 0))
                part_v = _times(rounded, g_one, (1, 0))
                dq = part_q if dq is None else dq + part_q
                dk = part_k if dk is None else dk + part_k
                dv = part_v if dv is None else dv + part_v
            dq_ref[:, cols] = (dq.T * scale).astype(bf16)
            dk_ref[:, cols] = (dk * scale).astype(bf16) if last else dk
            dv_ref[:, cols] = dv.astype(dv_ref.dtype)

    kind = bf16 if last else f32
    outs = [((rows, width), bf16), ((key_rows, width), kind), ((key_rows, width), kind)]
    return chip_call(kernel, outs, "attend_back", queries, keys, values, probs, grad_mixed, *sums)


def swap(values, name, size, flip):
    return lax.ppermute(values, name, [(i, i ^ flip) for i in range(size)])


def flip_bits(size):
    return [1 << b for b in range(size.bit_length() - 1)]


sync = lambda *values: lax.optimization_barrier(values)


def tie(value, *others):
    return lax.optimization_barrier((value,) + others)[0]


def lay_out(ranks, query, key, value, mem_key, mem_value, cross, up, own_out, mem_out):
    rows, width = query.shape
    part = width // ranks
    ff_part = up.shape[1] // ranks
    groups = ff_part * ranks // up.shape[1] * (width // (ranks * rows))
    unit = ff_part // groups

    def kernel(*refs):
        (self_ref, cross_ref, up_ref, so_ref, co_ref), ins, sems = refs[9:14], refs[14:23], refs[23]
        running = [pltpu.make_async_copy(refs[i], ins[i], sems.at[i]) for i in range(9)]
        for one in running:
            one.start()
        for one in running:
            one.wait()
        for r in range(ranks):
            cols = slice(r * part, (r + 1) * part)
            for i in range(3):
                self_ref[r, :, i * part : (i + 1) * part] = ins[i][:, cols]
                cross_ref[r, :, i * part : (i + 1) * part] = ins[3 + i][:, cols]
            so_ref[r] = ins[7][:, cols]
            co_ref[r] = ins[8][:, cols]
            for g in range(groups):
                first = (g * ranks + r) * unit
                up_ref[r, :, g * unit : (g + 1) * unit] = ins[6][:, first : first + unit]

    shapes = [3 * part, 3 * part, ff_part, part, part]
    return pl.pallas_call(
        kernel,
        in_specs=[FAR] * 9,
        out_specs=[WHOLE] * 5,
        scratch_shapes=[pltpu.VMEM((rows, width), bf16)] * 6
        + [pltpu.VMEM(up.shape, bf16)]
        + [pltpu.VMEM((rows, width), bf16)] * 2
        + [pltpu.SemaphoreType.DMA((9,))],
        out_shape=[pltpu.VMEM((ranks, rows, n), bf16) for n in shapes],
        compiler_params=ALL_OF_IT,
        name="lay_out",
    )(query, key, value, mem_key, mem_value, cross, up, own_out, mem_out)


def columns_back(pieces, counts, unit_first):
    ranks, rows, _ = pieces.shape

    def kernel(in_ref, *outs):
        first = 0
        for out, count in zip(outs, counts):
            if out is outs[0] and unit_first:
                units = count // unit_first
                for r in range(ranks):
                    for g in range(units):
                        at = (g * ranks + r) * unit_first
                        out[:, at : at + unit_first] = in_ref[
                            r, :, first + g * unit_first : first + (g + 1) * unit_first
                        ].astype(f32)
            else:
                for r in range(ranks):
                    out[:, r * count : (r + 1) * count] = in_ref[r, :, first : first + count].astype(f32)
            first += count

    return pl.pallas_call(
        kernel,
        in_specs=[WHOLE],
        out_specs=[WHOLE] * len(counts),
        out_shape=[jax.ShapeDtypeStruct((rows, ranks * n), f32) for n in counts],
        compiler_params=LIMIT,
        name="columns_back",
    )(on_chip(pieces))


def join_rows(pieces, rank):
    ranks = len(pieces)
    sets, blocks, rows, part = pieces[0].shape

    def copies(own, refs, out):
        return [
            (refs[r].at[p, b], out.at[p, own ^ r, :, b * part : (b + 1) * part])
            for r in range(ranks)
            for p in range(sets)
            for b in range(blocks)
        ]

    joined = copy_call(copies, ((sets, ranks, rows, blocks * part), bf16), "join_rows", rank, *pieces)
    return joined.reshape(sets * ranks * rows, blocks * part)


def pack_grads(rank, *parts):
    args = []
    places = []
    first = 0
    for one in parts:
        if isinstance(one, list):
            ranks, (sets, rows, width) = len(one), one[0].shape
            part = width // ranks
            for r in range(ranks):
                for p in range(sets):
                    for b in range(ranks):
                        at = slice(b * rows, (b + 1) * rows), slice(first, first + part)
                        places.append((len(args) + r, (p, slice(None), slice(b * part, (b + 1) * part)), (r, sets, p), at))
            args += one
            first += part
        else:
            groups, n, m = one.shape
            places.append((len(args), (slice(None),) * 3, None, (slice(None), slice(first, first + m))))
            args.append(one)
            first += m

    def copies(own, refs, out):
        found = []
        for i, source, piece, at in places:
            lead = slice(None) if piece is None else (own ^ piece[0]) * piece[1] + piece[2]
            found.append((refs[i].at[source], out.at[(lead,) + at]))
        return found

    return copy_call(copies, ((groups, n, first), bf16), "pack_grads", rank, *args)


def make_body(dp_size, g_size, z_size):
    ranks = z_size * CORES
    groups = dp_size * g_size
    every = ("dp", "g", "z", "c")

    def body(
        tokens,
        memory,
        cotangent,
        block_ids,
        seq_lengths,
        self_query,
        self_key,
        self_value,
        self_out,
        cross_query,
        cross_key,
        cross_value,
        cross_out,
        ffn_up,
        ffn_down,
        attn_gain,
        attn_bias,
        cross_gain,
        cross_bias,
        feedforward_norm_gain,
        ffn_bias,
    ):
        dp_own = lax.axis_index("dp")
        g_own = lax.axis_index("g")
        rank_own = lax.axis_index("z") * CORES + lax.axis_index("c")
        piece_rows = tokens.shape[1]
        width = tokens.shape[2]
        weight_rows = self_query.shape[0]
        rank_rows = ranks * weight_rows
        part = width // ranks
        sets = groups // ranks
        ff_rows = ffn_down.shape[0]
        ff_part = groups * ff_rows
        ff_blocks = width // ff_part

        def bits_of(name, size, own):
            return [(name, size, f, (own // f) % 2) for f in reversed(flip_bits(size))]

        axes = bits_of("dp", dp_size, dp_own) + bits_of("g", g_size, g_own)
        n_dp = dp_size.bit_length() - 1
        g_axes = list(range(n_dp, len(axes)))
        order_a = list(reversed(range(n_dp)))
        order_b = list(range(n_dp))

        def gather_axes(values, dims, order, after=()):
            for ax in order:
                name, size, flip, bit = axes[ax]
                other = tie(swap(values, name, size, flip), *after)
                pos = len([d for d in dims if d < ax])
                values = jnp.where(
                    bit == 1, jnp.stack([other, values], pos), jnp.stack([values, other], pos)
                )
                dims = sorted(dims + [ax])
            return values

        def scatter_axes(values, dims, order):
            dims = list(dims)
            for i, ax in enumerate(order):
                name, size, flip, bit = axes[ax]
                pos = dims.index(ax)
                other = swap(
                    lax.dynamic_index_in_dim(values, 1 - bit, pos, keepdims=False), name, size, flip
                )
                kept = lax.dynamic_index_in_dim(values, bit, pos, keepdims=False)
                values = kept.astype(f32) + other.astype(f32)
                dims.remove(ax)
                if dims:
                    values = values.astype(bf16)
            return values

        def halves(n):
            return (2,) * n

        def finish(values):
            shape = values.shape[1:]
            return scatter_axes(values.reshape(halves(len(g_axes)) + shape), g_axes, g_axes)

        def rank_swap(values, flip):
            return swap(values, ("z", "c"), ranks, flip)

        def from_ranks(pieces, axis):
            got = []
            for f in range(ranks):
                piece = lax.dynamic_index_in_dim(pieces, rank_own ^ f, axis, keepdims=False)
                got.append(piece if f == 0 else rank_swap(piece, f))
            return got

        def gather_rows(values):
            return with_partner(gather_chips(values))

        def gather_chips(values):
            blocks = [values]
            for flip in flip_bits(z_size):
                blocks = blocks + [swap(b, "z", z_size, flip) for b in blocks]
            return blocks

        def with_partner(blocks):
            return [jnp.concatenate([b, swap(b, "c", CORES, 1)], axis=0) for b in blocks]

        def sum_rows(blocks, product, fill=None):
            own_rows = piece_rows * g_size
            sums = [None] * z_size
            for b in reversed(range(z_size)):
                partial = product(blocks[b])
                came = swap(partial[own_rows:].astype(bf16), "c", CORES, 1)
                sums[b] = partial[:own_rows] + came.astype(f32)
            for flip in reversed(flip_bits(z_size)):
                leaving = [sums[b + flip].astype(bf16) for b in range(flip)]
                came = [swap(x, "z", z_size, flip) for x in leaving]
                if flip > 1:
                    sums = [sums[b] + came[b].astype(f32) for b in range(flip)]
            if fill is None:
                return sums[0], came[0]
            filled = fill(leaving[0])
            kept, last, filled = lax.optimization_barrier((sums[0], came[0], filled))
            return kept, last, filled

        def bring_home(values):
            got = []
            for f in range(g_size):
                piece = lax.dynamic_index_in_dim(values, g_own ^ f, 0, keepdims=False)
                got.append(piece if f == 0 else swap(piece, "g", g_size, f))
            return jnp.concatenate(got, axis=-2)

        def send_back(values):
            blocks = values.reshape(g_size, piece_rows, width)
            got = [blocks[0]] + [swap(blocks[f], "g", g_size, f) for f in range(1, g_size)]
            got = jnp.stack(got)
            return jnp.stack(
                [lax.dynamic_index_in_dim(got, g_own ^ f, 0, keepdims=False) for f in range(g_size)]
            )

        own_tokens = bring_home(tokens)
        self_parts, cross_parts, up_parts, so_parts, co_parts = lay_out(
            ranks,
            self_query,
            self_key,
            self_value,
            cross_key,
            cross_value,
            cross_query,
            ffn_up,
            self_out,
            cross_out,
        )

        def to_ranks(parts_in):
            return lax.all_to_all(parts_in, ("z", "c"), 0, 0, tiled=True)

        self_own, own_tokens = sync(to_ranks(self_parts), own_tokens)
        self_set = jnp.concatenate([self_own, so_parts], axis=2).reshape(rank_rows, 4 * part)
        self_set = gather_axes(self_set, [], g_axes)
        token_blocks = gather_rows(own_tokens)
        other_own = to_ranks(tie(jnp.concatenate([cross_parts, up_parts], axis=2), self_own))
        half_a, half_b, *token_blocks = sync(
            self_set[..., : 2 * part], self_set[..., 2 * part :], *token_blocks
        )
        other_own = tie(other_own, half_a)

        first_a, rest_a = order_a[:1], order_a[1:]
        first_b, rest_b = order_b[:1], order_b[1:]

        def first_stage(pair):
            return [gather_axes(pair[0], g_axes, first_a), gather_axes(pair[1], g_axes, first_b)]

        def last_stage(pair):
            pair = [
                gather_axes(pair[0], sorted(g_axes + first_a), rest_a),
                gather_axes(pair[1], sorted(g_axes + first_b), rest_b),
            ]
            return [x.reshape((groups,) + x.shape[-2:]) for x in pair]

        assert len(g_axes) == 1
        g_axis = axes[g_axes[0]]

        def swap_groups(values):
            return swap(values, *g_axis[:3])

        def both_groups(own, other):
            return jnp.where(g_axis[3] == 1, jnp.stack([other, own]), jnp.stack([own, other]))

        self_pair = first_stage([half_a, half_b])
        cross_set = jnp.concatenate([other_own[..., : 3 * part], co_parts], axis=2)
        cross_set = cross_set.reshape(rank_rows, 4 * part)
        cross_other = swap_groups(cross_set)
        vectors = jnp.stack(
            [attn_gain, attn_bias, cross_gain, cross_bias, feedforward_norm_gain, ffn_bias]
        )
        vectors = jnp.broadcast_to(vectors[None], (groups * ranks,) + vectors.shape)
        vectors = lax.all_to_all(tie(vectors, self_pair[0]), every, 0, 0, tiled=True)
        vectors = vectors.transpose(1, 0, 2).reshape(6, width).astype(f32)
        own_memory = bring_home(tie(memory, self_set))
        all_tokens = jnp.concatenate(token_blocks, axis=0)
        self_pair = last_stage(self_pair)
        cross_other = tie(cross_other, *self_pair)
        w_qk = self_pair[0].reshape(width, 2 * part)
        w_v = self_pair[1][..., :part].reshape(width, part)
        cross_set = both_groups(cross_set, cross_other)
        cross_pair = first_stage([cross_set[..., : 2 * part], cross_set[..., 2 * part :]])
        memory_chips = gather_chips(own_memory)

        down_rows = ffn_down.reshape(ff_rows, ff_blocks, ff_part).transpose(1, 0, 2)
        up_own, down_own = sync(
            other_own[..., 3 * part :].reshape(rank_rows, ff_part),
            down_rows.reshape(rank_rows, ff_part),
            self_pair[0],
        )[:2]
        up_other = swap_groups(up_own)
        down_other = swap_groups(tie(down_own, up_other))

        def out_rows(rows_in):
            pieces = rows_in.reshape(ranks, sets, ranks, weight_rows, part)
            return join_rows(from_ranks(pieces, 0), rank_own)

        w_sout = out_rows(self_pair[1][..., part:])

        n_pieces = g_size * ranks
        seq_own = g_own * ranks + rank_own
        ids = lax.dynamic_index_in_dim(block_ids, g_own, 0, keepdims=False)
        length = lax.dynamic_index_in_dim(seq_lengths, g_own, 0, keepdims=False)
        live = jnp.arange(ids.shape[0], dtype=jnp.int32) < length
        both = jnp.stack([ids, jnp.where(live, ids, jnp.int32(2**30))]).reshape(2, n_pieces, piece_rows)
        for flip in flip_bits(n_pieces):
            turned = both.reshape(2, n_pieces // (2 * flip), 2, flip, piece_rows)
            turned = jnp.concatenate([turned[:, :, 1:], turned[:, :, :1]], axis=2).reshape(both.shape)
            both = jnp.where((seq_own & flip) != 0, turned, both)
        both = both.reshape(2, g_size, ranks, piece_rows).transpose(0, 2, 1, 3).reshape(2, -1)
        bias = jnp.where(both[1][:, None] <= both[0][None, :], 0.0, neg_large).astype(f32)

        def row_blocks(values):
            return jnp.split(values, z_size, axis=0)

        def joined(blocks):
            return jnp.concatenate(blocks, axis=0)

        qk = matmul(all_tokens, w_qk).astype(bf16)
        queries, keys = qk[:, :part], qk[:, part:]
        values = matmul(all_tokens, w_v).astype(bf16)
        attended, self_probs = attention_forward(queries, keys, values, bias)
        attended, cross_pair[0], cross_pair[1], up_other = sync(attended, *cross_pair, up_other)
        cross_pair = last_stage(cross_pair)
        kept, came, memory_blocks = sum_rows(
            row_blocks(attended),
            lambda x: matmul(x, w_sout),
            lambda term: with_partner([tie(x, term) for x in memory_chips]),
        )
        kept, came, down_other = sync(kept, came, down_other)
        hidden_one, normed_one, inv_one = norm_rows(own_tokens, kept, came, vectors, 0)
        ffn_pair = first_stage([both_groups(up_own, up_other), both_groups(down_own, down_other)])
        own_cotangent = bring_home(tie(cotangent, down_other))

        all_memory = joined(memory_blocks)
        w_ckv = cross_pair[0].reshape(width, 2 * part)
        w_cq = cross_pair[1][..., :part].reshape(width, part)
        w_cout = out_rows(cross_pair[1][..., part:])
        mem_kv = matmul(all_memory, w_ckv).astype(bf16)
        mem_keys, mem_values = mem_kv[:, :part], mem_kv[:, part:]

        one_blocks = gather_rows(hidden_one)
        one_blocks[-1], mem_keys, mem_values, w_cout, ffn_pair[0], ffn_pair[1] = sync(
            one_blocks[-1], mem_keys, mem_values, w_cout, *ffn_pair
        )
        ffn_pair = last_stage(ffn_pair)
        cross_rows = [matmul(x, w_cq).astype(bf16) for x in one_blocks]
        crossed = [attention_forward(x, mem_keys, mem_values, None) for x in cross_rows]
        cross_probs = [x[1] for x in crossed]
        crossed = [x[0] for x in crossed]
        kept, came = sum_rows(crossed, lambda x: matmul(x, w_cout))
        hidden_two, normed_two, inv_two = norm_rows(hidden_one, kept, came, vectors, 2)
        hidden_two, own_cotangent = sync(hidden_two, own_cotangent)
        two_blocks = gather_rows(hidden_two)
        w_up = ffn_pair[0].reshape(width, ff_part)
        w_down = ffn_pair[1].reshape(groups, ff_blocks, ff_rows, ff_part).transpose(0, 2, 1, 3)
        w_down = w_down.reshape(ff_part, width)
        upper_rows = [matmul(x, w_up) for x in two_blocks]
        active_rows = [gelu_tanh(x).astype(bf16) for x in upper_rows]
        kept, came, slopes = sum_rows(
            active_rows,
            lambda x: matmul(x, w_down),
            lambda term: [gelu_slope(tie(x, term)) for x in upper_rows],
        )
        layer_rows, grad_three, branch, sums_three = norm_turn(
            hidden_two, kept, came, vectors, 4, own_cotangent
        )

        branch_blocks = gather_rows(branch)
        grad_upper = [
            (transposed_product(x, w_down) * y).astype(bf16) for x, y in zip(branch_blocks, slopes)
        ]

        def ffn_gradients(term):
            rows, _ = lax.optimization_barrier((branch_blocks, term))
            down = outer_product_sum(joined(active_rows), joined(rows)).astype(bf16)
            down = down.reshape(groups, ff_rows, ff_blocks, ff_part).transpose(0, 2, 1, 3)
            up = outer_product_sum(joined(two_blocks), joined(grad_upper)).astype(bf16)
            return jnp.concatenate(
                [up.reshape(groups, rank_rows, ff_part), down.reshape(groups, rank_rows, ff_part)],
                axis=1,
            )

        kept, came, ffn_grads = sum_rows(
            grad_upper, lambda x: transposed_product(x, w_up), ffn_gradients
        )
        ffn_grads = lax.psum_scatter(
            ffn_grads.reshape(groups * 2 * rank_rows, ff_part), "dp", scatter_dimension=0, tiled=True
        )
        grad_two, branch, sums_two = norm_back(grad_three, kept, came, normed_two, inv_two, vectors, 2)
        layer_out = send_back(tie(layer_rows, branch))

        branch_blocks = gather_rows(branch)
        branch_blocks[-1], layer_out = sync(branch_blocks[-1], layer_out)
        grad_crossed = [transposed_product(x, w_cout).astype(bf16) for x in branch_blocks]
        grad_cross_rows, sums = [], []
        for b in range(z_size):
            grad_rows, *sums = attention_backward(
                cross_rows[b], mem_keys, mem_values, cross_probs[b], 0, grad_crossed[b], sums, b == z_size - 1
            )
            grad_cross_rows.append(grad_rows)
        grad_mem_kv = jnp.concatenate(sums, axis=1)

        def cout_gradient(term):
            rows, _ = lax.optimization_barrier((branch_blocks, term))
            return outer_product_sum(joined(crossed), joined(rows)).astype(bf16)

        kept, came, cout_grad = sum_rows(
            grad_cross_rows, lambda x: transposed_product(x, w_cq), cout_gradient
        )
        grad_one, branch, sums_one = norm_back(grad_two, kept, came, normed_one, inv_one, vectors, 0)
        branch_blocks = gather_rows(branch)
        cout_grad = tie(cout_grad, branch).reshape(sets, ranks, weight_rows, width)
        cout_pieces = from_ranks(cout_grad, 1)
        vec_sums = jnp.concatenate([sums_one, sums_two, sums_three], axis=0)
        for flip in flip_bits(dp_size):
            vec_sums = vec_sums + swap(vec_sums, "dp", dp_size, flip)
        branch_blocks[-1], vec_sums = sync(branch_blocks[-1], vec_sums)
        grad_mem_kv = tie(grad_mem_kv, branch)
        mem_kv_grad = outer_product_sum(all_memory, grad_mem_kv).astype(bf16)
        cross_grad = outer_product_sum(joined(one_blocks), joined(grad_cross_rows)).astype(bf16)
        all_dims = list(range(len(axes)))

        def first_sums(pair):
            pair = [x.reshape(halves(len(axes)) + x.shape[-2:]) for x in pair]
            return [scatter_axes(pair[0], all_dims, first_a), scatter_axes(pair[1], all_dims, first_b)]

        def more_sums(pair):
            return [
                scatter_axes(pair[0], [d for d in all_dims if d not in first_a], rest_a),
                scatter_axes(pair[1], [d for d in all_dims if d not in first_b], rest_b),
            ]

        def last_sums(pair):
            return [scatter_axes(x, g_axes, g_axes) for x in pair]

        grad_attended = [transposed_product(x, w_sout).astype(bf16) for x in branch_blocks]
        sout_grad = outer_product_sum(attended, joined(branch_blocks)).astype(bf16)
        sout_pieces = from_ranks(sout_grad.reshape(sets, ranks, weight_rows, width), 1)
        memory_kept, memory_came = sum_rows(
            row_blocks(grad_mem_kv), lambda x: transposed_product(x, w_ckv)
        )
        memory_rows = (memory_kept + memory_came.astype(f32)).astype(bf16)

        query_blocks = row_blocks(queries)
        chip_rows = queries.shape[0] // z_size
        grad_queries, sums = [], []
        for b in range(z_size):
            grad_rows, *sums = attention_backward(
                query_blocks[b],
                keys,
                values,
                self_probs,
                b * chip_rows,
                grad_attended[b],
                sums,
                b == z_size - 1,
            )
            grad_queries.append(grad_rows)
        grad_qk = jnp.concatenate([joined(grad_queries), sums[0]], axis=1)
        grad_values = sums[1]
        def by_group(grads):
            return grads.reshape(groups, rank_rows, -1)

        qk_grad = outer_product_sum(all_tokens, grad_qk).astype(bf16)
        grads_a = pack_grads(rank_own, by_group(qk_grad), by_group(mem_kv_grad))
        v_grad = outer_product_sum(all_tokens, grad_values).astype(bf16)
        grads_b = pack_grads(rank_own, by_group(v_grad), sout_pieces, by_group(cross_grad), cout_pieces)
        sums = first_sums([grads_a, grads_b])

        sent = (grads_a, grads_b)
        ffn_grads = tie(ffn_grads, *sent).reshape(g_size, 2, rank_rows, ff_part)
        up_grad = scatter_axes(ffn_grads[:, 0], g_axes, g_axes)
        down_grad = scatter_axes(ffn_grads[:, 1], g_axes, g_axes)
        row_pairs = zip(row_blocks(tie(grad_qk, *sent)), row_blocks(grad_values))
        kept, came = sum_rows(
            list(row_pairs),
            lambda x: transposed_product(x[0], w_qk) + transposed_product(x[1], w_v),
        )
        tokens_grad = (residual_scale * grad_one + (kept + came.astype(f32))).astype(bf16)
        memory_grad = send_back(tie(memory_rows, *sent))
        sums[0], sums[1], up_grad, down_grad, tokens_grad = sync(*sums, up_grad, down_grad, tokens_grad)

        sums = more_sums(sums)
        up_pieces = to_ranks(up_grad.astype(bf16).reshape(ranks, weight_rows, ff_part))
        tokens_grad = send_back(tokens_grad)
        vec_sums = tie(vec_sums, tokens_grad)
        for name, size in (("c", CORES), ("z", z_size), ("g", g_size)):
            for flip in flip_bits(size):
                vec_sums = vec_sums + swap(vec_sums, name, size, flip)
        sums = last_sums(sums)

        down_grad = down_grad.reshape(ff_blocks, ff_rows, ff_part).transpose(1, 0, 2)
        down_grad = down_grad.reshape(ff_rows, width)

        def own_rows_of(values):
            return values.reshape(ranks, weight_rows, part).transpose(1, 0, 2).reshape(weight_rows, width)

        (up_grad,) = columns_back(up_pieces, (ff_part,), ff_rows)
        pieces = [sums[0][:, : 2 * part], sums[1][:, :part], sums[0][:, 2 * part :], sums[1][:, 2 * part : 3 * part]]
        pieces = jnp.concatenate([x.astype(bf16) for x in pieces], axis=1)
        pieces = to_ranks(pieces.reshape(ranks, weight_rows, 6 * part))
        query_grad, key_grad, value_grad, mem_key_grad, mem_value_grad, cross_grad = columns_back(
            pieces, (part,) * 6, 0
        )

        first = ((dp_own * g_size + g_own) * ranks + rank_own) * weight_rows
        vec_grads = lax.dynamic_slice_in_dim(vec_sums, first, weight_rows, axis=1)

        return (
            layer_out,
            tokens_grad,
            memory_grad,
            query_grad,
            key_grad,
            value_grad,
            own_rows_of(sums[1][:, part : 2 * part]),
            cross_grad,
            mem_key_grad,
            mem_value_grad,
            own_rows_of(sums[1][:, 3 * part :]),
            up_grad,
            down_grad,
            vec_grads[0],
            vec_grads[1],
            vec_grads[2],
            vec_grads[3],
            vec_grads[4],
            vec_grads[5],
        )

    return body


def solution(mesh):
    dp_size, seq_size = mesh.shape["dp"], mesh.shape["seq"]

    def layer_step(*args):
        g_size = args[0].shape[0] // dp_size
        z_size = seq_size // (g_size * CORES)
        split_mesh = Mesh(
            mesh.devices.reshape(dp_size, g_size, z_size, CORES), ("dp", "g", "z", "c")
        )
        seq = ("g", "z", "c")
        every = ("dp", "g", "z", "c")
        rows = P("dp", seq, None)
        matrix = P(every, None)
        vector = P(every)
        return jax.shard_map(
            make_body(dp_size, g_size, z_size),
            mesh=split_mesh,
            in_specs=(rows,) * 3 + (P("dp", None), P("dp")) + (matrix,) * 10 + (vector,) * 6,
            out_specs=(rows,) * 3 + (matrix,) * 10 + (vector,) * 6,
            check_vma=False,
        )(*args)

    return layer_step
```

```python
import jax
import jax.numpy as jnp
from jax import lax
from jax.experimental import pallas as pl
from jax.experimental.pallas import tpu as pltpu
from jax.sharding import Mesh, PartitionSpec as P

HEAD_DIM = 64
CORES = 2

eps_norm = 1e-05
residual_scale = 18.0**0.25
gelu_coef = 0.7978845608028654
neg_large = -1e30
bf16 = jnp.bfloat16
f32 = jnp.float32


def gelu_tanh(values_in):
    inner = gelu_coef * (values_in + 0.044715 * values_in * values_in * values_in)
    return 0.5 * values_in * (1.0 + jnp.tanh(inner))


def gelu_slope(values_in):
    squared = values_in * values_in
    tanh_val = jnp.tanh(gelu_coef * (values_in + 0.044715 * squared * values_in))
    return 0.5 * (1.0 + tanh_val) + 0.5 * values_in * (1.0 - tanh_val * tanh_val) * gelu_coef * (
        1.0 + 3.0 * 0.044715 * squared
    )


def matmul(first_mat, second_mat):
    return jnp.dot(first_mat, second_mat, preferred_element_type=f32)


def transposed_product(first_mat, second_mat):
    return lax.dot_general(first_mat, second_mat, (((1,), (1,)), ((), ())), preferred_element_type=f32)


def outer_product_sum(first_mat, second_mat):
    return lax.dot_general(first_mat, second_mat, (((0,), (0,)), ((), ())), preferred_element_type=f32)


LIMIT = pltpu.CompilerParams(vmem_limit_bytes=16 * 1024 * 1024)
ALL_OF_IT = pltpu.CompilerParams(vmem_limit_bytes=60 * 1024 * 1024)
SCALAR = pl.BlockSpec(memory_space=pltpu.SMEM)
WHOLE = pl.BlockSpec(memory_space=pltpu.VMEM)


def on_chip(values):
    return pltpu.with_memory_space_constraint(values, pltpu.VMEM)


def chip_call(kernel, outs, name, *args, scalar=None):
    scalars = [] if scalar is None else [scalar.reshape(1)]
    return pl.pallas_call(
        kernel,
        in_specs=[SCALAR] * len(scalars) + [WHOLE] * len(args),
        out_specs=[WHOLE] * len(outs),
        out_shape=[pltpu.VMEM(shape, dtype) for shape, dtype in outs],
        compiler_params=LIMIT,
        name=name,
    )(*scalars, *[on_chip(x) for x in args])


ANY = pl.BlockSpec(memory_space=pl.ANY)
FAR = pl.BlockSpec(memory_space=pltpu.HBM)


def copy_call(copies, out, name, scalar, *args):
    count = []

    def kernel(scalar_ref, *refs):
        sems = refs[-1]
        running = [
            pltpu.make_async_copy(source, target, sems.at[i])
            for i, (source, target) in enumerate(copies(scalar_ref[0], refs[:-2], refs[-2]))
        ]
        for one in running:
            one.start()
        for one in running:
            one.wait()

    class Probe:
        at = property(lambda self: self)

        def __getitem__(self, index):
            return self

    count = len(copies(0, [Probe()] * len(args), Probe()))
    return pl.pallas_call(
        kernel,
        in_specs=[SCALAR] + [ANY] * len(args),
        out_specs=ANY,
        out_shape=jax.ShapeDtypeStruct(*out),
        scratch_shapes=[pltpu.SemaphoreType.DMA((count,))],
        compiler_params=LIMIT,
        name=name,
    )(scalar.reshape(1), *args)


def _mean(values):
    return jnp.mean(values, axis=-1, keepdims=True)


def _normed(residual, kept, came):
    values = residual_scale * residual.astype(f32) + (kept + came.astype(f32))
    centred = values - _mean(values)
    inv_std = lax.rsqrt(_mean(centred * centred) + eps_norm)
    return centred * inv_std, inv_std


def _norm_back(grad_out, normed, inv_std, gain):
    scaled = grad_out * gain
    grad_in = inv_std * (scaled - _mean(scaled) - normed * _mean(scaled * normed))
    sums = [jnp.sum(grad_out * normed, axis=0, keepdims=True), jnp.sum(grad_out, axis=0, keepdims=True)]
    return grad_in, jnp.concatenate(sums, axis=0)


def norm_rows(residual, kept, came, vectors, row):
    def kernel(res, kept, came, vec, hidden, normed, inv):
        n, r = _normed(res[...], kept[...], came[...])
        hidden[...] = (n * vec[row : row + 1, :] + vec[row + 1 : row + 2, :]).astype(bf16)
        normed[...] = n
        inv[...] = jnp.broadcast_to(r, inv.shape)

    shape = residual.shape
    outs = [(shape, bf16), (shape, f32), ((shape[0], 128), f32)]
    return chip_call(kernel, outs, "norm_rows", residual, kept, came, vectors)


def norm_turn(residual, kept, came, vectors, row, cotangent):
    def kernel(res, kept, came, vec, cot, layer, grad, rounded, sums):
        gain = vec[row : row + 1, :]
        n, r = _normed(res[...], kept[...], came[...])
        layer[...] = (n * gain + vec[row + 1 : row + 2, :]).astype(bf16)
        g, s = _norm_back(cot[...].astype(f32), n, r, gain)
        grad[...] = g
        rounded[...] = g.astype(bf16)
        sums[...] = s

    shape = residual.shape
    outs = [(shape, bf16), (shape, f32), (shape, bf16), ((2, shape[1]), f32)]
    return chip_call(kernel, outs, "norm_turn", residual, kept, came, vectors, cotangent)


def norm_back(grad_prev, kept, came, normed, inv_std, vectors, row, limit=LIMIT):
    shape = grad_prev.shape
    args = [grad_prev, kept, came, normed, inv_std]

    def kernel(*refs):
        vec, grad, rounded, sums = refs[5:9]
        prev, kept, came, normed, inv = refs[9:14]
        running = [pltpu.make_async_copy(refs[i], refs[9 + i], refs[14].at[i]) for i in range(5)]
        for one in running:
            one.start()
        for one in running:
            one.wait()
        grad_out = residual_scale * prev[...] + (kept[...] + came[...].astype(f32))
        g, s = _norm_back(grad_out, normed[...], inv[:, :1], vec[row : row + 1, :])
        grad[...] = g
        rounded[...] = g.astype(bf16)
        sums[...] = s

    outs = [(shape, f32), (shape, bf16), ((2, shape[1]), f32)]
    return pl.pallas_call(
        kernel,
        in_specs=[FAR] * 5 + [WHOLE],
        out_specs=[WHOLE] * 3,
        out_shape=[pltpu.VMEM(x, dtype) for x, dtype in outs],
        scratch_shapes=[pltpu.VMEM(x.shape, x.dtype) for x in args] + [pltpu.SemaphoreType.DMA((5,))],
        compiler_params=limit,
        name="norm_back",
    )(*args, on_chip(vectors))


PAIR = 2 * HEAD_DIM


def _head_of_pair(values, head):
    lane = lax.broadcasted_iota(jnp.int32, (1, PAIR), 1)
    return jnp.where((lane // HEAD_DIM) == head, values, jnp.zeros((), values.dtype))


def _times(first, second, dims):
    return lax.dot_general(first, second, ((dims[:1], dims[1:]), ((), ())), preferred_element_type=f32)


def attention_forward(queries, keys, values, bias):
    rows, width = queries.shape
    key_rows = keys.shape[0]
    scale = HEAD_DIM ** (-0.5)

    def kernel(q_ref, k_ref, v_ref, *rest):
        out_ref, probs_ref = rest[-2:]
        for pair in range(width // PAIR):
            cols = slice(pair * PAIR, (pair + 1) * PAIR)
            q, k, v = q_ref[:, cols] * jnp.asarray(scale, bf16), k_ref[:, cols], v_ref[:, cols]
            mixed = None
            for head in range(2):
                scores = _times(k, _head_of_pair(q, head), (1, 1))
                if bias is not None:
                    scores = scores + rest[0][...]
                expo = jnp.exp(scores - jnp.max(scores, axis=0, keepdims=True))
                probs = (expo * (1.0 / jnp.sum(expo, axis=0, keepdims=True))).astype(bf16)
                probs_ref[2 * pair + head] = probs
                part = _times(_head_of_pair(v, head), probs, (0, 0))
                mixed = part if mixed is None else mixed + part
            out_ref[:, cols] = mixed.T.astype(bf16)

    args = [queries, keys, values] + ([] if bias is None else [bias])
    outs = [((rows, width), bf16), ((width // HEAD_DIM, key_rows, rows), bf16)]
    return chip_call(kernel, outs, "attend", *args)


def attention_backward(queries, keys, values, probs, first, grad_mixed, sums, last):
    rows, width = queries.shape
    key_rows = keys.shape[0]
    scale = HEAD_DIM ** (-0.5)

    def kernel(q_ref, k_ref, v_ref, p_ref, g_ref, *rest):
        before, (dq_ref, dk_ref, dv_ref) = rest[: len(sums)], rest[len(sums) :]
        for pair in range(width // PAIR):
            cols = slice(pair * PAIR, (pair + 1) * PAIR)
            q, k, v, g = q_ref[:, cols], k_ref[:, cols], v_ref[:, cols], g_ref[:, cols]
            dq = None
            dk, dv = [x[:, cols] for x in before] if sums else (None, None)
            for head in range(2):
                g_one = _head_of_pair(g, head)
                rounded = p_ref[2 * pair + head, :, first : first + rows]
                wide = rounded.astype(f32)
                weighted = _times(v, g_one, (1, 1)) * wide
                g_scores = (weighted - wide * jnp.sum(weighted, axis=0, keepdims=True)).astype(bf16)
                part_q = _times(_head_of_pair(k, head), g_scores, (0, 0))
                part_k = _times(g_scores, _head_of_pair(q, head), (1, 0))
                part_v = _times(rounded, g_one, (1, 0))
                dq = part_q if dq is None else dq + part_q
                dk = part_k if dk is None else dk + part_k
                dv = part_v if dv is None else dv + part_v
            dq_ref[:, cols] = (dq.T * scale).astype(bf16)
            dk_ref[:, cols] = (dk * scale).astype(bf16) if last else dk
            dv_ref[:, cols] = dv.astype(dv_ref.dtype)

    kind = bf16 if last else f32
    outs = [((rows, width), bf16), ((key_rows, width), kind), ((key_rows, width), kind)]
    return chip_call(kernel, outs, "attend_back", queries, keys, values, probs, grad_mixed, *sums)


def swap(values, name, size, flip):
    return lax.ppermute(values, name, [(i, i ^ flip) for i in range(size)])


def flip_bits(size):
    return [1 << b for b in range(size.bit_length() - 1)]


sync = lambda *values: lax.optimization_barrier(values)


def tie(value, *others):
    return lax.optimization_barrier((value,) + others)[0]


def lay_out(ranks, query, key, value, mem_key, mem_value, cross, up, own_out, mem_out):
    rows, width = query.shape
    part = width // ranks
    ff_part = up.shape[1] // ranks
    groups = ff_part * ranks // up.shape[1] * (width // (ranks * rows))
    unit = ff_part // groups

    def kernel(*refs):
        (self_ref, cross_ref, up_ref, so_ref, co_ref), ins, sems = refs[9:14], refs[14:23], refs[23]
        running = [pltpu.make_async_copy(refs[i], ins[i], sems.at[i]) for i in range(9)]
        for one in running:
            one.start()
        for one in running:
            one.wait()
        for r in range(ranks):
            cols = slice(r * part, (r + 1) * part)
            for i in range(3):
                self_ref[r, :, i * part : (i + 1) * part] = ins[i][:, cols]
                cross_ref[r, :, i * part : (i + 1) * part] = ins[3 + i][:, cols]
            so_ref[r] = ins[7][:, cols]
            co_ref[r] = ins[8][:, cols]
            for g in range(groups):
                first = (g * ranks + r) * unit
                up_ref[r, :, g * unit : (g + 1) * unit] = ins[6][:, first : first + unit]

    shapes = [3 * part, 3 * part, ff_part, part, part]
    return pl.pallas_call(
        kernel,
        in_specs=[FAR] * 9,
        out_specs=[WHOLE] * 5,
        scratch_shapes=[pltpu.VMEM((rows, width), bf16)] * 6
        + [pltpu.VMEM(up.shape, bf16)]
        + [pltpu.VMEM((rows, width), bf16)] * 2
        + [pltpu.SemaphoreType.DMA((9,))],
        out_shape=[pltpu.VMEM((ranks, rows, n), bf16) for n in shapes],
        compiler_params=ALL_OF_IT,
        name="lay_out",
    )(query, key, value, mem_key, mem_value, cross, up, own_out, mem_out)


def columns_back(pieces, counts, unit_first):
    ranks, rows, _ = pieces.shape

    def kernel(in_ref, *outs):
        first = 0
        for out, count in zip(outs, counts):
            if out is outs[0] and unit_first:
                units = count // unit_first
                for r in range(ranks):
                    for g in range(units):
                        at = (g * ranks + r) * unit_first
                        out[:, at : at + unit_first] = in_ref[
                            r, :, first + g * unit_first : first + (g + 1) * unit_first
                        ].astype(f32)
            else:
                for r in range(ranks):
                    out[:, r * count : (r + 1) * count] = in_ref[r, :, first : first + count].astype(f32)
            first += count

    return pl.pallas_call(
        kernel,
        in_specs=[WHOLE],
        out_specs=[WHOLE] * len(counts),
        out_shape=[jax.ShapeDtypeStruct((rows, ranks * n), f32) for n in counts],
        compiler_params=LIMIT,
        name="columns_back",
    )(on_chip(pieces))


def join_rows(pieces, rank):
    ranks = len(pieces)
    sets, blocks, rows, part = pieces[0].shape

    def copies(own, refs, out):
        return [
            (refs[r].at[p, b], out.at[p, own ^ r, :, b * part : (b + 1) * part])
            for r in range(ranks)
            for p in range(sets)
            for b in range(blocks)
        ]

    joined = copy_call(copies, ((sets, ranks, rows, blocks * part), bf16), "join_rows", rank, *pieces)
    return joined.reshape(sets * ranks * rows, blocks * part)


def pack_grads(rank, *parts):
    args = []
    places = []
    first = 0
    for one in parts:
        if isinstance(one, list):
            ranks, (sets, rows, width) = len(one), one[0].shape
            part = width // ranks
            for r in range(ranks):
                for p in range(sets):
                    for b in range(ranks):
                        at = slice(b * rows, (b + 1) * rows), slice(first, first + part)
                        places.append((len(args) + r, (p, slice(None), slice(b * part, (b + 1) * part)), (r, sets, p), at))
            args += one
            first += part
        elif one.ndim == 4:
            ranks, sets, rows, width = one.shape
            part = width // ranks
            for r in range(ranks):
                for p in range(sets):
                    for b in range(ranks):
                        at = slice(b * rows, (b + 1) * rows), slice(first, first + part)
                        source = (r, p, slice(None), slice(b * part, (b + 1) * part))
                        places.append((len(args), source, r * sets + p, at))
            args.append(one)
            first += part
        else:
            groups, n, m = one.shape
            places.append((len(args), (slice(None),) * 3, None, (slice(None), slice(first, first + m))))
            args.append(one)
            first += m

    def copies(own, refs, out):
        found = []
        for i, source, piece, at in places:
            lead = slice(None) if piece is None else piece
            if isinstance(piece, tuple):
                lead = (own ^ piece[0]) * piece[1] + piece[2]
            found.append((refs[i].at[source], out.at[(lead,) + at]))
        return found

    return copy_call(copies, ((groups, n, first), bf16), "pack_grads", rank, *args)


def make_body(dp_size, g_size, z_size):
    ranks = z_size * CORES
    groups = dp_size * g_size
    every = ("dp", "g", "z", "c")

    def body(
        tokens,
        memory,
        cotangent,
        block_ids,
        seq_lengths,
        self_query,
        self_key,
        self_value,
        self_out,
        cross_query,
        cross_key,
        cross_value,
        cross_out,
        ffn_up,
        ffn_down,
        attn_gain,
        attn_bias,
        cross_gain,
        cross_bias,
        feedforward_norm_gain,
        ffn_bias,
    ):
        dp_own = lax.axis_index("dp")
        g_own = lax.axis_index("g")
        rank_own = lax.axis_index("z") * CORES + lax.axis_index("c")
        piece_rows = tokens.shape[1]
        width = tokens.shape[2]
        weight_rows = self_query.shape[0]
        rank_rows = ranks * weight_rows
        part = width // ranks
        sets = groups // ranks
        ff_rows = ffn_down.shape[0]
        ff_part = groups * ff_rows
        ff_blocks = width // ff_part

        def bits_of(name, size, own):
            return [(name, size, f, (own // f) % 2) for f in reversed(flip_bits(size))]

        axes = bits_of("dp", dp_size, dp_own) + bits_of("g", g_size, g_own)
        n_dp = dp_size.bit_length() - 1
        g_axes = list(range(n_dp, len(axes)))
        order_a = list(reversed(range(n_dp)))
        order_b = list(range(n_dp))

        def gather_axes(values, dims, order, after=()):
            for ax in order:
                name, size, flip, bit = axes[ax]
                other = tie(swap(values, name, size, flip), *after)
                pos = len([d for d in dims if d < ax])
                values = jnp.where(
                    bit == 1, jnp.stack([other, values], pos), jnp.stack([values, other], pos)
                )
                dims = sorted(dims + [ax])
            return values

        def scatter_axes(values, dims, order):
            dims = list(dims)
            for i, ax in enumerate(order):
                name, size, flip, bit = axes[ax]
                pos = dims.index(ax)
                other = swap(
                    lax.dynamic_index_in_dim(values, 1 - bit, pos, keepdims=False), name, size, flip
                )
                kept = lax.dynamic_index_in_dim(values, bit, pos, keepdims=False)
                values = kept.astype(f32) + other.astype(f32)
                dims.remove(ax)
                if dims:
                    values = values.astype(bf16)
            return values

        def halves(n):
            return (2,) * n

        def finish(values):
            shape = values.shape[1:]
            return scatter_axes(values.reshape(halves(len(g_axes)) + shape), g_axes, g_axes)

        def rank_swap(values, flip):
            return swap(values, ("z", "c"), ranks, flip)

        def from_ranks(pieces, axis):
            got = []
            for f in range(ranks):
                piece = lax.dynamic_index_in_dim(pieces, rank_own ^ f, axis, keepdims=False)
                got.append(piece if f == 0 else rank_swap(piece, f))
            return got

        def gather_rows(values):
            return with_partner(gather_chips(values))

        def gather_chips(values):
            blocks = [values]
            for flip in flip_bits(z_size):
                blocks = blocks + [swap(b, "z", z_size, flip) for b in blocks]
            return blocks

        def with_partner(blocks):
            return [jnp.concatenate([b, swap(b, "c", CORES, 1)], axis=0) for b in blocks]

        def sum_rows(blocks, product, fill=None):
            own_rows = piece_rows * g_size
            sums = [None] * z_size
            for b in reversed(range(z_size)):
                partial = product(blocks[b])
                came = swap(partial[own_rows:].astype(bf16), "c", CORES, 1)
                sums[b] = partial[:own_rows] + came.astype(f32)
            for flip in reversed(flip_bits(z_size)):
                leaving = [sums[b + flip].astype(bf16) for b in range(flip)]
                came = [swap(x, "z", z_size, flip) for x in leaving]
                if flip > 1:
                    sums = [sums[b] + came[b].astype(f32) for b in range(flip)]
            if fill is None:
                return sums[0], came[0]
            filled = fill(leaving[0])
            kept, last, filled = lax.optimization_barrier((sums[0], came[0], filled))
            return kept, last, filled

        def bring_home(values, *after):
            got = []
            for f in range(g_size):
                piece = lax.dynamic_index_in_dim(values, g_own ^ f, 0, keepdims=False)
                got.append(piece if f == 0 else tie(swap(piece, "g", g_size, f), *after))
            return jnp.concatenate(got, axis=-2)

        def send_back(values):
            blocks = values.reshape(g_size, piece_rows, width)
            got = [blocks[0]] + [swap(blocks[f], "g", g_size, f) for f in range(1, g_size)]
            got = jnp.stack(got)
            return jnp.stack(
                [lax.dynamic_index_in_dim(got, g_own ^ f, 0, keepdims=False) for f in range(g_size)]
            )

        own_tokens = bring_home(tokens)
        self_parts, cross_parts, up_parts, so_parts, co_parts = lay_out(
            ranks,
            self_query,
            self_key,
            self_value,
            cross_key,
            cross_value,
            cross_query,
            ffn_up,
            self_out,
            cross_out,
        )

        def to_ranks(parts_in):
            return lax.all_to_all(parts_in, ("z", "c"), 0, 0, tiled=True)

        self_own, own_tokens = sync(to_ranks(self_parts), own_tokens)
        self_set = jnp.concatenate([self_own, so_parts], axis=2).reshape(rank_rows, 4 * part)
        self_set = gather_axes(self_set, [], g_axes)
        token_blocks = gather_rows(own_tokens)
        other_own = to_ranks(tie(jnp.concatenate([cross_parts, up_parts], axis=2), self_own))
        half_a, half_b, *token_blocks = sync(
            self_set[..., : 2 * part], self_set[..., 2 * part :], *token_blocks
        )
        other_own = tie(other_own, half_a)

        first_a, rest_a = order_a[:1], order_a[1:]
        first_b, rest_b = order_b[:1], order_b[1:]

        def first_stage(pair):
            return [gather_axes(pair[0], g_axes, first_a), gather_axes(pair[1], g_axes, first_b)]

        def last_stage(pair):
            pair = [
                gather_axes(pair[0], sorted(g_axes + first_a), rest_a),
                gather_axes(pair[1], sorted(g_axes + first_b), rest_b),
            ]
            return [x.reshape((groups,) + x.shape[-2:]) for x in pair]

        assert len(g_axes) == 1
        g_axis = axes[g_axes[0]]

        def swap_groups(values):
            return swap(values, *g_axis[:3])

        def both_groups(own, other):
            return jnp.where(g_axis[3] == 1, jnp.stack([other, own]), jnp.stack([own, other]))

        self_pair = first_stage([half_a, half_b])
        cross_set = jnp.concatenate([other_own[..., : 3 * part], co_parts], axis=2)
        cross_set = cross_set.reshape(rank_rows, 4 * part)
        cross_other = swap_groups(cross_set)
        own_memory = bring_home(tie(memory, self_set), *self_pair)
        all_tokens = jnp.concatenate(token_blocks, axis=0)
        vectors = jnp.stack(
            [attn_gain, attn_bias, cross_gain, cross_bias, feedforward_norm_gain, ffn_bias]
        )
        vectors = jnp.broadcast_to(vectors[None], (groups * ranks,) + vectors.shape)
        self_pair[0], self_pair[1], vectors = sync(*self_pair, vectors)
        vectors = lax.all_to_all(vectors, every, 0, 0, tiled=True)
        vectors = vectors.transpose(1, 0, 2).reshape(6, width).astype(f32)
        self_pair = last_stage(self_pair)
        self_pair[0], self_pair[1], vectors = sync(*self_pair, vectors)
        cross_other = tie(cross_other, *self_pair)
        w_qk = self_pair[0].reshape(width, 2 * part)
        w_v = self_pair[1][..., :part].reshape(width, part)
        cross_set = both_groups(cross_set, cross_other)
        cross_pair = first_stage([cross_set[..., : 2 * part], cross_set[..., 2 * part :]])
        memory_chips = gather_chips(own_memory)

        down_rows = ffn_down.reshape(ff_rows, ff_blocks, ff_part).transpose(1, 0, 2)
        up_own, down_own = sync(
            other_own[..., 3 * part :].reshape(rank_rows, ff_part),
            down_rows.reshape(rank_rows, ff_part),
            self_pair[0],
        )[:2]
        up_other = swap_groups(up_own)
        down_other = swap_groups(tie(down_own, up_other))

        def out_rows(rows_in):
            pieces = rows_in.reshape(ranks, sets, ranks, weight_rows, part)
            return join_rows(from_ranks(pieces, 0), rank_own)

        w_sout = out_rows(self_pair[1][..., part:])

        n_pieces = g_size * ranks
        seq_own = g_own * ranks + rank_own
        ids = lax.dynamic_index_in_dim(block_ids, g_own, 0, keepdims=False)
        length = lax.dynamic_index_in_dim(seq_lengths, g_own, 0, keepdims=False)
        live = jnp.arange(ids.shape[0], dtype=jnp.int32) < length
        both = jnp.stack([ids, jnp.where(live, ids, jnp.int32(2**30))]).reshape(2, n_pieces, piece_rows)
        for flip in flip_bits(n_pieces):
            turned = both.reshape(2, n_pieces // (2 * flip), 2, flip, piece_rows)
            turned = jnp.concatenate([turned[:, :, 1:], turned[:, :, :1]], axis=2).reshape(both.shape)
            both = jnp.where((seq_own & flip) != 0, turned, both)
        both = both.reshape(2, g_size, ranks, piece_rows).transpose(0, 2, 1, 3).reshape(2, -1)
        bias = jnp.where(both[1][:, None] <= both[0][None, :], 0.0, neg_large).astype(f32)

        def row_blocks(values):
            return jnp.split(values, z_size, axis=0)

        def joined(blocks):
            return jnp.concatenate(blocks, axis=0)

        qk = matmul(all_tokens, w_qk).astype(bf16)
        queries, keys = qk[:, :part], qk[:, part:]
        values = matmul(all_tokens, w_v).astype(bf16)
        attended, self_probs = attention_forward(queries, keys, values, bias)
        attended, cross_pair[0], cross_pair[1], up_other = sync(attended, *cross_pair, up_other)
        cross_pair = last_stage(cross_pair)
        kept, came, memory_blocks = sum_rows(
            row_blocks(attended),
            lambda x: matmul(x, w_sout),
            lambda term: with_partner([tie(x, term) for x in memory_chips]),
        )
        kept, came, down_other = sync(kept, came, down_other)
        hidden_one, normed_one, inv_one = norm_rows(own_tokens, kept, came, vectors, 0)
        ffn_pair = first_stage([both_groups(up_own, up_other), both_groups(down_own, down_other)])
        own_cotangent = bring_home(tie(cotangent, down_other))

        all_memory = joined(memory_blocks)
        w_ckv = cross_pair[0].reshape(width, 2 * part)
        w_cq = cross_pair[1][..., :part].reshape(width, part)
        w_cout = out_rows(cross_pair[1][..., part:])
        mem_kv = matmul(all_memory, w_ckv).astype(bf16)
        mem_keys, mem_values = mem_kv[:, :part], mem_kv[:, part:]

        one_blocks = gather_rows(hidden_one)
        one_blocks[-1], mem_keys, mem_values, w_cout, ffn_pair[0], ffn_pair[1] = sync(
            one_blocks[-1], mem_keys, mem_values, w_cout, *ffn_pair
        )
        ffn_pair = last_stage(ffn_pair)
        cross_rows = [matmul(x, w_cq).astype(bf16) for x in one_blocks]
        crossed = [attention_forward(x, mem_keys, mem_values, None) for x in cross_rows]
        cross_probs = [x[1] for x in crossed]
        crossed = [x[0] for x in crossed]
        kept, came = sum_rows(crossed, lambda x: matmul(x, w_cout))
        hidden_two, normed_two, inv_two = norm_rows(hidden_one, kept, came, vectors, 2)
        hidden_two, own_cotangent = sync(hidden_two, own_cotangent)
        two_blocks = gather_rows(hidden_two)
        w_up = ffn_pair[0].reshape(width, ff_part)
        w_down = ffn_pair[1].reshape(groups, ff_blocks, ff_rows, ff_part).transpose(0, 2, 1, 3)
        w_down = w_down.reshape(ff_part, width)
        upper_rows = [matmul(x, w_up) for x in two_blocks]
        active_rows = [gelu_tanh(x).astype(bf16) for x in upper_rows]
        kept, came, slopes = sum_rows(
            active_rows,
            lambda x: matmul(x, w_down),
            lambda term: [gelu_slope(tie(x, term)) for x in upper_rows],
        )
        layer_rows, grad_three, branch, sums_three = norm_turn(
            hidden_two, kept, came, vectors, 4, own_cotangent
        )

        branch_blocks = gather_rows(branch)
        grad_upper = [
            (transposed_product(x, w_down) * y).astype(bf16) for x, y in zip(branch_blocks, slopes)
        ]

        def ffn_gradients(term):
            rows, _ = lax.optimization_barrier((branch_blocks, term))
            down = outer_product_sum(joined(active_rows), joined(rows)).astype(bf16)
            down = down.reshape(groups, ff_rows, ff_blocks, ff_part).transpose(0, 2, 1, 3)
            up = outer_product_sum(joined(two_blocks), joined(grad_upper)).astype(bf16)
            return jnp.concatenate(
                [up.reshape(groups, rank_rows, ff_part), down.reshape(groups, rank_rows, ff_part)],
                axis=1,
            )

        kept, came, ffn_grads = sum_rows(
            grad_upper, lambda x: transposed_product(x, w_up), ffn_gradients
        )
        ffn_grads = lax.psum_scatter(
            ffn_grads.reshape(groups * 2 * rank_rows, ff_part), "dp", scatter_dimension=0, tiled=True
        )
        grad_two, branch, sums_two = norm_back(
            grad_three, kept, came, normed_two, inv_two, vectors, 2, ALL_OF_IT
        )
        layer_out = send_back(tie(layer_rows, branch))

        branch_blocks = gather_rows(branch)
        grad_crossed = [transposed_product(x, w_cout).astype(bf16) for x in branch_blocks]
        grad_cross_rows, sums = [], []
        for b in range(z_size):
            grad_rows, *sums = attention_backward(
                cross_rows[b], mem_keys, mem_values, cross_probs[b], 0, grad_crossed[b], sums, b == z_size - 1
            )
            grad_cross_rows.append(grad_rows)
        grad_mem_kv = jnp.concatenate(sums, axis=1)

        def cout_gradient(term):
            rows, _ = lax.optimization_barrier((branch_blocks, term))
            return outer_product_sum(joined(crossed), joined(rows)).astype(bf16)

        kept, came, cout_grad = sum_rows(
            grad_cross_rows, lambda x: transposed_product(x, w_cq), cout_gradient
        )
        kept, layer_out = sync(kept, layer_out)
        grad_one, branch, sums_one = norm_back(grad_two, kept, came, normed_one, inv_one, vectors, 0)
        branch_blocks = gather_rows(branch)
        cout_grad = tie(cout_grad, branch).reshape(sets, ranks, weight_rows, width)
        cout_pieces = from_ranks(cout_grad, 1)
        vec_sums = jnp.concatenate([sums_one, sums_two, sums_three], axis=0)
        for flip in flip_bits(dp_size):
            vec_sums = vec_sums + swap(vec_sums, "dp", dp_size, flip)
        branch_blocks[-1], vec_sums = sync(branch_blocks[-1], vec_sums)
        grad_mem_kv = tie(grad_mem_kv, branch)
        mem_kv_grad = outer_product_sum(all_memory, grad_mem_kv).astype(bf16)
        cross_grad = outer_product_sum(joined(one_blocks), joined(grad_cross_rows)).astype(bf16)
        all_dims = list(range(len(axes)))

        def first_sums(pair):
            pair = [x.reshape(halves(len(axes)) + x.shape[-2:]) for x in pair]
            return [scatter_axes(pair[0], all_dims, first_a), scatter_axes(pair[1], all_dims, first_b)]

        def more_sums(pair):
            return [
                scatter_axes(pair[0], [d for d in all_dims if d not in first_a], rest_a),
                scatter_axes(pair[1], [d for d in all_dims if d not in first_b], rest_b),
            ]

        def last_sums(pair):
            return [scatter_axes(x, g_axes, g_axes) for x in pair]

        grad_attended = [transposed_product(x, w_sout).astype(bf16) for x in branch_blocks]
        sout_grad = outer_product_sum(attended, joined(branch_blocks)).astype(bf16)
        sout_pieces = from_ranks(sout_grad.reshape(sets, ranks, weight_rows, width), 1)
        memory_kept, memory_came = sum_rows(
            row_blocks(grad_mem_kv), lambda x: transposed_product(x, w_ckv)
        )
        memory_rows = (memory_kept + memory_came.astype(f32)).astype(bf16)

        query_blocks = row_blocks(queries)
        chip_rows = queries.shape[0] // z_size
        grad_queries, sums = [], []
        for b in range(z_size):
            grad_rows, *sums = attention_backward(
                query_blocks[b],
                keys,
                values,
                self_probs,
                b * chip_rows,
                grad_attended[b],
                sums,
                b == z_size - 1,
            )
            grad_queries.append(grad_rows)
        grad_qk = jnp.concatenate([joined(grad_queries), sums[0]], axis=1)
        grad_values = sums[1]
        def by_group(grads):
            return grads.reshape(groups, rank_rows, -1)

        qk_grad = outer_product_sum(all_tokens, grad_qk).astype(bf16)
        grads_a = pack_grads(rank_own, by_group(qk_grad), by_group(mem_kv_grad))
        v_grad = outer_product_sum(all_tokens, grad_values).astype(bf16)
        grads_b = pack_grads(rank_own, by_group(v_grad), sout_pieces, by_group(cross_grad), cout_pieces)
        grads_a, grads_b, ffn_grads = sync(grads_a, grads_b, ffn_grads)
        sums = first_sums([grads_a, grads_b])
        ffn_grads = ffn_grads.reshape(g_size, 2, rank_rows, ff_part)
        ffn_grads = scatter_axes(ffn_grads, g_axes, g_axes)
        up_grad, down_grad = ffn_grads[0], ffn_grads[1]

        row_pairs = zip(row_blocks(tie(grad_qk, grads_a, grads_b)), row_blocks(grad_values))
        kept, came = sum_rows(
            list(row_pairs),
            lambda x: transposed_product(x[0], w_qk) + transposed_product(x[1], w_v),
        )
        tokens_grad = (residual_scale * grad_one + (kept + came.astype(f32))).astype(bf16)
        sums[0], sums[1], tokens_grad, memory_rows = sync(*sums, tokens_grad, memory_rows)
        sums = more_sums(sums)
        tokens_grad = send_back(tokens_grad)
        memory_grad = send_back(memory_rows)
        up_pieces = to_ranks(tie(up_grad, *sums).astype(bf16).reshape(ranks, weight_rows, ff_part))
        vec_sums = tie(vec_sums, *sums)
        for name, size in (("c", CORES), ("z", z_size), ("g", g_size)):
            for flip in flip_bits(size):
                vec_sums = vec_sums + swap(vec_sums, name, size, flip)
        sums = last_sums(sums)

        down_grad = down_grad.reshape(ff_blocks, ff_rows, ff_part).transpose(1, 0, 2)
        down_grad = down_grad.reshape(ff_rows, width)

        def own_rows_of(values):
            return values.reshape(ranks, weight_rows, part).transpose(1, 0, 2).reshape(weight_rows, width)

        (up_grad,) = columns_back(up_pieces, (ff_part,), ff_rows)
        pieces = [sums[0][:, : 2 * part], sums[1][:, :part], sums[0][:, 2 * part :], sums[1][:, 2 * part : 3 * part]]
        pieces = jnp.concatenate([x.astype(bf16) for x in pieces], axis=1)
        pieces = to_ranks(pieces.reshape(ranks, weight_rows, 6 * part))
        query_grad, key_grad, value_grad, mem_key_grad, mem_value_grad, cross_grad = columns_back(
            pieces, (part,) * 6, 0
        )

        first = ((dp_own * g_size + g_own) * ranks + rank_own) * weight_rows
        vec_grads = lax.dynamic_slice_in_dim(vec_sums, first, weight_rows, axis=1)

        return (
            layer_out,
            tokens_grad,
            memory_grad,
            query_grad,
            key_grad,
            value_grad,
            own_rows_of(sums[1][:, part : 2 * part]),
            cross_grad,
            mem_key_grad,
            mem_value_grad,
            own_rows_of(sums[1][:, 3 * part :]),
            up_grad,
            down_grad,
            vec_grads[0],
            vec_grads[1],
            vec_grads[2],
            vec_grads[3],
            vec_grads[4],
            vec_grads[5],
        )

    return body


def solution(mesh):
    dp_size, seq_size = mesh.shape["dp"], mesh.shape["seq"]

    def layer_step(*args):
        g_size = args[0].shape[0] // dp_size
        z_size = seq_size // (g_size * CORES)
        split_mesh = Mesh(
            mesh.devices.reshape(dp_size, g_size, z_size, CORES), ("dp", "g", "z", "c")
        )
        seq = ("g", "z", "c")
        every = ("dp", "g", "z", "c")
        rows = P("dp", seq, None)
        matrix = P(every, None)
        vector = P(every)
        return jax.shard_map(
            make_body(dp_size, g_size, z_size),
            mesh=split_mesh,
            in_specs=(rows,) * 3 + (P("dp", None), P("dp")) + (matrix,) * 10 + (vector,) * 6,
            out_specs=(rows,) * 3 + (matrix,) * 10 + (vector,) * 6,
            check_vma=False,
        )(*args)

    return layer_step
```

```python
import jax
import jax.numpy as jnp
from jax import lax
from jax.experimental import pallas as pl
from jax.experimental.pallas import tpu as pltpu
from jax.sharding import Mesh, PartitionSpec as P

HEAD_DIM = 64
CORES = 2

eps_norm = 1e-05
residual_scale = 18.0**0.25
gelu_coef = 0.7978845608028654
neg_large = -1e30
bf16 = jnp.bfloat16
f32 = jnp.float32


def gelu_tanh(values_in):
    inner = gelu_coef * (values_in + 0.044715 * values_in * values_in * values_in)
    return 0.5 * values_in * (1.0 + jnp.tanh(inner))


def gelu_slope(values_in):
    squared = values_in * values_in
    tanh_val = jnp.tanh(gelu_coef * (values_in + 0.044715 * squared * values_in))
    return 0.5 * (1.0 + tanh_val) + 0.5 * values_in * (1.0 - tanh_val * tanh_val) * gelu_coef * (
        1.0 + 3.0 * 0.044715 * squared
    )


def matmul(first_mat, second_mat):
    return jnp.dot(first_mat, second_mat, preferred_element_type=f32)


def transposed_product(first_mat, second_mat):
    return lax.dot_general(first_mat, second_mat, (((1,), (1,)), ((), ())), preferred_element_type=f32)


def outer_product_sum(first_mat, second_mat):
    return lax.dot_general(first_mat, second_mat, (((0,), (0,)), ((), ())), preferred_element_type=f32)


LIMIT = pltpu.CompilerParams(vmem_limit_bytes=16 * 1024 * 1024)
ALL_OF_IT = pltpu.CompilerParams(vmem_limit_bytes=60 * 1024 * 1024)
SCALAR = pl.BlockSpec(memory_space=pltpu.SMEM)
WHOLE = pl.BlockSpec(memory_space=pltpu.VMEM)


def on_chip(values):
    return pltpu.with_memory_space_constraint(values, pltpu.VMEM)


def chip_call(kernel, outs, name, *args, scalar=None):
    scalars = [] if scalar is None else [scalar.reshape(1)]
    return pl.pallas_call(
        kernel,
        in_specs=[SCALAR] * len(scalars) + [WHOLE] * len(args),
        out_specs=[WHOLE] * len(outs),
        out_shape=[pltpu.VMEM(shape, dtype) for shape, dtype in outs],
        compiler_params=LIMIT,
        name=name,
    )(*scalars, *[on_chip(x) for x in args])


ANY = pl.BlockSpec(memory_space=pl.ANY)
FAR = pl.BlockSpec(memory_space=pltpu.HBM)


def copy_call(copies, out, name, scalar, *args):
    count = []

    def kernel(scalar_ref, *refs):
        sems = refs[-1]
        running = [
            pltpu.make_async_copy(source, target, sems.at[i])
            for i, (source, target) in enumerate(copies(scalar_ref[0], refs[:-2], refs[-2]))
        ]
        for one in running:
            one.start()
        for one in running:
            one.wait()

    class Probe:
        at = property(lambda self: self)

        def __getitem__(self, index):
            return self

    count = len(copies(0, [Probe()] * len(args), Probe()))
    return pl.pallas_call(
        kernel,
        in_specs=[SCALAR] + [ANY] * len(args),
        out_specs=ANY,
        out_shape=jax.ShapeDtypeStruct(*out),
        scratch_shapes=[pltpu.SemaphoreType.DMA((count,))],
        compiler_params=LIMIT,
        name=name,
    )(scalar.reshape(1), *args)


def _mean(values):
    return jnp.mean(values, axis=-1, keepdims=True)


def _normed(residual, kept, came):
    values = residual_scale * residual.astype(f32) + (kept + came.astype(f32))
    centred = values - _mean(values)
    inv_std = lax.rsqrt(_mean(centred * centred) + eps_norm)
    return centred * inv_std, inv_std


def _norm_back(grad_out, normed, inv_std, gain):
    scaled = grad_out * gain
    grad_in = inv_std * (scaled - _mean(scaled) - normed * _mean(scaled * normed))
    sums = [jnp.sum(grad_out * normed, axis=0, keepdims=True), jnp.sum(grad_out, axis=0, keepdims=True)]
    return grad_in, jnp.concatenate(sums, axis=0)


def norm_rows(residual, kept, came, vectors, row):
    def kernel(res, kept, came, vec, hidden, normed, inv):
        n, r = _normed(res[...], kept[...], came[...])
        hidden[...] = (n * vec[row : row + 1, :] + vec[row + 1 : row + 2, :]).astype(bf16)
        normed[...] = n
        inv[...] = jnp.broadcast_to(r, inv.shape)

    shape = residual.shape
    outs = [(shape, bf16), (shape, f32), ((shape[0], 128), f32)]
    return chip_call(kernel, outs, "norm_rows", residual, kept, came, vectors)


def norm_turn(residual, kept, came, vectors, row, cotangent):
    def kernel(res, kept, came, vec, cot, layer, grad, rounded, sums):
        gain = vec[row : row + 1, :]
        n, r = _normed(res[...], kept[...], came[...])
        layer[...] = (n * gain + vec[row + 1 : row + 2, :]).astype(bf16)
        g, s = _norm_back(cot[...].astype(f32), n, r, gain)
        grad[...] = g
        rounded[...] = g.astype(bf16)
        sums[...] = s

    shape = residual.shape
    outs = [(shape, bf16), (shape, f32), (shape, bf16), ((2, shape[1]), f32)]
    return chip_call(kernel, outs, "norm_turn", residual, kept, came, vectors, cotangent)


def norm_back(grad_prev, kept, came, normed, inv_std, vectors, row, limit=LIMIT):
    shape = grad_prev.shape
    args = [grad_prev, kept, came, normed, inv_std]

    def kernel(*refs):
        vec, grad, rounded, sums = refs[5:9]
        prev, kept, came, normed, inv = refs[9:14]
        running = [pltpu.make_async_copy(refs[i], refs[9 + i], refs[14].at[i]) for i in range(5)]
        for one in running:
            one.start()
        for one in running:
            one.wait()
        grad_out = residual_scale * prev[...] + (kept[...] + came[...].astype(f32))
        g, s = _norm_back(grad_out, normed[...], inv[:, :1], vec[row : row + 1, :])
        grad[...] = g
        rounded[...] = g.astype(bf16)
        sums[...] = s

    outs = [(shape, f32), (shape, bf16), ((2, shape[1]), f32)]
    return pl.pallas_call(
        kernel,
        in_specs=[FAR] * 5 + [WHOLE],
        out_specs=[WHOLE] * 3,
        out_shape=[pltpu.VMEM(x, dtype) for x, dtype in outs],
        scratch_shapes=[pltpu.VMEM(x.shape, x.dtype) for x in args] + [pltpu.SemaphoreType.DMA((5,))],
        compiler_params=limit,
        name="norm_back",
    )(*args, on_chip(vectors))


PAIR = 2 * HEAD_DIM


def _head_of_pair(values, head):
    lane = lax.broadcasted_iota(jnp.int32, (1, PAIR), 1)
    return jnp.where((lane // HEAD_DIM) == head, values, jnp.zeros((), values.dtype))


def _times(first, second, dims):
    return lax.dot_general(first, second, ((dims[:1], dims[1:]), ((), ())), preferred_element_type=f32)


def attention_forward(queries, keys, values, bias):
    rows, width = queries.shape
    key_rows = keys.shape[0]
    scale = HEAD_DIM ** (-0.5)

    def kernel(q_ref, k_ref, v_ref, *rest):
        out_ref, probs_ref = rest[-2:]
        for pair in range(width // PAIR):
            cols = slice(pair * PAIR, (pair + 1) * PAIR)
            q, k, v = q_ref[:, cols] * jnp.asarray(scale, bf16), k_ref[:, cols], v_ref[:, cols]
            mixed = None
            for head in range(2):
                scores = _times(k, _head_of_pair(q, head), (1, 1))
                if bias is not None:
                    scores = scores + rest[0][...]
                expo = jnp.exp(scores - jnp.max(scores, axis=0, keepdims=True))
                probs = (expo * (1.0 / jnp.sum(expo, axis=0, keepdims=True))).astype(bf16)
                probs_ref[2 * pair + head] = probs
                part = _times(_head_of_pair(v, head), probs, (0, 0))
                mixed = part if mixed is None else mixed + part
            out_ref[:, cols] = mixed.T.astype(bf16)

    args = [queries, keys, values] + ([] if bias is None else [bias])
    outs = [((rows, width), bf16), ((width // HEAD_DIM, key_rows, rows), bf16)]
    return chip_call(kernel, outs, "attend", *args)


def attention_backward(queries, keys, values, probs, first, grad_mixed, sums, last):
    rows, width = queries.shape
    key_rows = keys.shape[0]
    scale = HEAD_DIM ** (-0.5)

    def kernel(q_ref, k_ref, v_ref, p_ref, g_ref, *rest):
        before, (dq_ref, dk_ref, dv_ref) = rest[: len(sums)], rest[len(sums) :]
        for pair in range(width // PAIR):
            cols = slice(pair * PAIR, (pair + 1) * PAIR)
            q, k, v, g = q_ref[:, cols], k_ref[:, cols], v_ref[:, cols], g_ref[:, cols]
            dq = None
            dk, dv = [x[:, cols] for x in before] if sums else (None, None)
            for head in range(2):
                g_one = _head_of_pair(g, head)
                rounded = p_ref[2 * pair + head, :, first : first + rows]
                wide = rounded.astype(f32)
                weighted = _times(v, g_one, (1, 1)) * wide
                g_scores = (weighted - wide * jnp.sum(weighted, axis=0, keepdims=True)).astype(bf16)
                part_q = _times(_head_of_pair(k, head), g_scores, (0, 0))
                part_k = _times(g_scores, _head_of_pair(q, head), (1, 0))
                part_v = _times(rounded, g_one, (1, 0))
                dq = part_q if dq is None else dq + part_q
                dk = part_k if dk is None else dk + part_k
                dv = part_v if dv is None else dv + part_v
            dq_ref[:, cols] = (dq.T * scale).astype(bf16)
            dk_ref[:, cols] = (dk * scale).astype(bf16) if last else dk
            dv_ref[:, cols] = dv.astype(dv_ref.dtype)

    kind = bf16 if last else f32
    outs = [((rows, width), bf16), ((key_rows, width), kind), ((key_rows, width), kind)]
    return chip_call(kernel, outs, "attend_back", queries, keys, values, probs, grad_mixed, *sums)


def swap(values, name, size, flip):
    return lax.ppermute(values, name, [(i, i ^ flip) for i in range(size)])


def flip_bits(size):
    return [1 << b for b in range(size.bit_length() - 1)]


sync = lambda *values: lax.optimization_barrier(values)


def tie(value, *others):
    return lax.optimization_barrier((value,) + others)[0]


def lay_out(ranks, query, key, value, mem_key, mem_value, cross, up, own_out, mem_out):
    rows, width = query.shape
    part = width // ranks
    ff_part = up.shape[1] // ranks
    groups = ff_part * ranks // up.shape[1] * (width // (ranks * rows))
    unit = ff_part // groups

    def kernel(*refs):
        (self_ref, cross_ref, up_ref, so_ref, co_ref), ins, sems = refs[9:14], refs[14:23], refs[23]
        running = [pltpu.make_async_copy(refs[i], ins[i], sems.at[i]) for i in range(9)]
        for one in running:
            one.start()
        for one in running:
            one.wait()
        for r in range(ranks):
            cols = slice(r * part, (r + 1) * part)
            for i in range(3):
                self_ref[r, :, i * part : (i + 1) * part] = ins[i][:, cols]
                cross_ref[r, :, i * part : (i + 1) * part] = ins[3 + i][:, cols]
            so_ref[r] = ins[7][:, cols]
            co_ref[r] = ins[8][:, cols]
            for g in range(groups):
                first = (g * ranks + r) * unit
                up_ref[r, :, g * unit : (g + 1) * unit] = ins[6][:, first : first + unit]

    shapes = [3 * part, 3 * part, ff_part, part, part]
    return pl.pallas_call(
        kernel,
        in_specs=[FAR] * 9,
        out_specs=[WHOLE] * 5,
        scratch_shapes=[pltpu.VMEM((rows, width), bf16)] * 6
        + [pltpu.VMEM(up.shape, bf16)]
        + [pltpu.VMEM((rows, width), bf16)] * 2
        + [pltpu.SemaphoreType.DMA((9,))],
        out_shape=[pltpu.VMEM((ranks, rows, n), bf16) for n in shapes],
        compiler_params=ALL_OF_IT,
        name="lay_out",
    )(query, key, value, mem_key, mem_value, cross, up, own_out, mem_out)


def columns_back(pieces, ranks, counts, unit_first):
    terms, rows = pieces.shape[0] // ranks, pieces.shape[1]

    def kernel(in_ref, *outs):
        def total(r, cols):
            found = in_ref[r, :, cols].astype(f32)
            for term in range(1, terms):
                found = found + in_ref[term * ranks + r, :, cols].astype(f32)
            return found

        first = 0
        for out, count in zip(outs, counts):
            if out is outs[0] and unit_first:
                units = count // unit_first
                for r in range(ranks):
                    for g in range(units):
                        at = (g * ranks + r) * unit_first
                        cols = slice(first + g * unit_first, first + (g + 1) * unit_first)
                        out[:, at : at + unit_first] = total(r, cols)
            else:
                for r in range(ranks):
                    out[:, r * count : (r + 1) * count] = total(r, slice(first, first + count))
            first += count

    return pl.pallas_call(
        kernel,
        in_specs=[WHOLE],
        out_specs=[WHOLE] * len(counts),
        out_shape=[jax.ShapeDtypeStruct((rows, ranks * n), f32) for n in counts],
        compiler_params=LIMIT,
        name="columns_back",
    )(on_chip(pieces))


def join_rows(pieces, rank):
    ranks = len(pieces)
    sets, blocks, rows, part = pieces[0].shape

    def copies(own, refs, out):
        return [
            (refs[r].at[p, b], out.at[p, own ^ r, :, b * part : (b + 1) * part])
            for r in range(ranks)
            for p in range(sets)
            for b in range(blocks)
        ]

    joined = copy_call(copies, ((sets, ranks, rows, blocks * part), bf16), "join_rows", rank, *pieces)
    return joined.reshape(sets * ranks * rows, blocks * part)


def pack_grads(rank, *parts):
    args = []
    places = []
    first = 0
    for one in parts:
        if isinstance(one, list):
            ranks, (sets, rows, width) = len(one), one[0].shape
            part = width // ranks
            for r in range(ranks):
                for p in range(sets):
                    for b in range(ranks):
                        at = slice(b * rows, (b + 1) * rows), slice(first, first + part)
                        places.append((len(args) + r, (p, slice(None), slice(b * part, (b + 1) * part)), (r, sets, p), at))
            args += one
            first += part
        elif one.ndim == 4:
            ranks, sets, rows, width = one.shape
            part = width // ranks
            for r in range(ranks):
                for p in range(sets):
                    for b in range(ranks):
                        at = slice(b * rows, (b + 1) * rows), slice(first, first + part)
                        source = (r, p, slice(None), slice(b * part, (b + 1) * part))
                        places.append((len(args), source, r * sets + p, at))
            args.append(one)
            first += part
        else:
            groups, n, m = one.shape
            places.append((len(args), (slice(None),) * 3, None, (slice(None), slice(first, first + m))))
            args.append(one)
            first += m

    def copies(own, refs, out):
        found = []
        for i, source, piece, at in places:
            lead = slice(None) if piece is None else piece
            if isinstance(piece, tuple):
                lead = (own ^ piece[0]) * piece[1] + piece[2]
            found.append((refs[i].at[source], out.at[(lead,) + at]))
        return found

    return copy_call(copies, ((groups, n, first), bf16), "pack_grads", rank, *args)


def make_body(dp_size, g_size, z_size):
    ranks = z_size * CORES
    groups = dp_size * g_size
    every = ("dp", "g", "z", "c")

    def body(
        tokens,
        memory,
        cotangent,
        block_ids,
        seq_lengths,
        self_query,
        self_key,
        self_value,
        self_out,
        cross_query,
        cross_key,
        cross_value,
        cross_out,
        ffn_up,
        ffn_down,
        attn_gain,
        attn_bias,
        cross_gain,
        cross_bias,
        feedforward_norm_gain,
        ffn_bias,
    ):
        dp_own = lax.axis_index("dp")
        g_own = lax.axis_index("g")
        rank_own = lax.axis_index("z") * CORES + lax.axis_index("c")
        piece_rows = tokens.shape[1]
        width = tokens.shape[2]
        weight_rows = self_query.shape[0]
        rank_rows = ranks * weight_rows
        part = width // ranks
        sets = groups // ranks
        ff_rows = ffn_down.shape[0]
        ff_part = groups * ff_rows
        ff_blocks = width // ff_part

        def bits_of(name, size, own):
            return [(name, size, f, (own // f) % 2) for f in reversed(flip_bits(size))]

        axes = bits_of("dp", dp_size, dp_own) + bits_of("g", g_size, g_own)
        n_dp = dp_size.bit_length() - 1
        g_axes = list(range(n_dp, len(axes)))
        order_a = list(reversed(range(n_dp)))
        order_b = list(range(n_dp))

        def gather_axes(values, dims, order, after=()):
            for ax in order:
                name, size, flip, bit = axes[ax]
                other = tie(swap(values, name, size, flip), *after)
                pos = len([d for d in dims if d < ax])
                values = jnp.where(
                    bit == 1, jnp.stack([other, values], pos), jnp.stack([values, other], pos)
                )
                dims = sorted(dims + [ax])
            return values

        def scatter_axes(values, dims, order):
            dims = list(dims)
            for i, ax in enumerate(order):
                name, size, flip, bit = axes[ax]
                pos = dims.index(ax)
                other = swap(
                    lax.dynamic_index_in_dim(values, 1 - bit, pos, keepdims=False), name, size, flip
                )
                kept = lax.dynamic_index_in_dim(values, bit, pos, keepdims=False)
                values = kept.astype(f32) + other.astype(f32)
                dims.remove(ax)
                if dims:
                    values = values.astype(bf16)
            return values

        def halves(n):
            return (2,) * n

        def finish(values):
            shape = values.shape[1:]
            return scatter_axes(values.reshape(halves(len(g_axes)) + shape), g_axes, g_axes)

        def rank_swap(values, flip):
            return swap(values, ("z", "c"), ranks, flip)

        def from_ranks(pieces, axis):
            got = []
            for f in range(ranks):
                piece = lax.dynamic_index_in_dim(pieces, rank_own ^ f, axis, keepdims=False)
                got.append(piece if f == 0 else rank_swap(piece, f))
            return got

        def gather_rows(values):
            return with_partner(gather_chips(values))

        def gather_chips(values):
            blocks = [values]
            for flip in flip_bits(z_size):
                blocks = blocks + [swap(b, "z", z_size, flip) for b in blocks]
            return blocks

        def with_partner(blocks):
            return [jnp.concatenate([b, swap(b, "c", CORES, 1)], axis=0) for b in blocks]

        def sum_rows(blocks, product, fill=None):
            own_rows = piece_rows * g_size
            sums = [None] * z_size
            for b in reversed(range(z_size)):
                partial = product(blocks[b])
                came = swap(partial[own_rows:].astype(bf16), "c", CORES, 1)
                sums[b] = partial[:own_rows] + came.astype(f32)
            for flip in reversed(flip_bits(z_size)):
                leaving = [sums[b + flip].astype(bf16) for b in range(flip)]
                came = [swap(x, "z", z_size, flip) for x in leaving]
                if flip > 1:
                    sums = [sums[b] + came[b].astype(f32) for b in range(flip)]
            if fill is None:
                return sums[0], came[0]
            filled = fill(leaving[0])
            kept, last, filled = lax.optimization_barrier((sums[0], came[0], filled))
            return kept, last, filled

        def bring_home(values, *after):
            got = []
            for f in range(g_size):
                piece = lax.dynamic_index_in_dim(values, g_own ^ f, 0, keepdims=False)
                got.append(piece if f == 0 else tie(swap(piece, "g", g_size, f), *after))
            return jnp.concatenate(got, axis=-2)

        def send_back(values):
            blocks = values.reshape(g_size, piece_rows, width)
            got = [blocks[0]] + [swap(blocks[f], "g", g_size, f) for f in range(1, g_size)]
            got = jnp.stack(got)
            return jnp.stack(
                [lax.dynamic_index_in_dim(got, g_own ^ f, 0, keepdims=False) for f in range(g_size)]
            )

        own_tokens = bring_home(tokens)
        self_parts, cross_parts, up_parts, so_parts, co_parts = lay_out(
            ranks,
            self_query,
            self_key,
            self_value,
            cross_key,
            cross_value,
            cross_query,
            ffn_up,
            self_out,
            cross_out,
        )

        def to_ranks(parts_in):
            return lax.all_to_all(parts_in, ("z", "c"), 0, 0, tiled=True)

        self_own, own_tokens = sync(to_ranks(self_parts), own_tokens)
        self_set = jnp.concatenate([self_own, so_parts], axis=2).reshape(rank_rows, 4 * part)
        self_set = gather_axes(self_set, [], g_axes)
        token_blocks = gather_rows(own_tokens)
        other_own = to_ranks(tie(jnp.concatenate([cross_parts, up_parts], axis=2), self_own))
        half_a, half_b, *token_blocks = sync(
            self_set[..., : 2 * part], self_set[..., 2 * part :], *token_blocks
        )
        other_own = tie(other_own, half_a)

        first_a, rest_a = order_a[:1], order_a[1:]
        first_b, rest_b = order_b[:1], order_b[1:]

        def first_stage(pair):
            return [gather_axes(pair[0], g_axes, first_a), gather_axes(pair[1], g_axes, first_b)]

        def last_stage(pair):
            pair = [
                gather_axes(pair[0], sorted(g_axes + first_a), rest_a),
                gather_axes(pair[1], sorted(g_axes + first_b), rest_b),
            ]
            return [x.reshape((groups,) + x.shape[-2:]) for x in pair]

        assert len(g_axes) == 1
        g_axis = axes[g_axes[0]]

        def swap_groups(values):
            return swap(values, *g_axis[:3])

        def both_groups(own, other):
            return jnp.where(g_axis[3] == 1, jnp.stack([other, own]), jnp.stack([own, other]))

        self_pair = first_stage([half_a, half_b])
        cross_set = jnp.concatenate([other_own[..., : 3 * part], co_parts], axis=2)
        cross_set = cross_set.reshape(rank_rows, 4 * part)
        cross_other = swap_groups(cross_set)
        own_memory = bring_home(tie(memory, self_set), *self_pair)
        all_tokens = jnp.concatenate(token_blocks, axis=0)
        vectors = jnp.stack(
            [attn_gain, attn_bias, cross_gain, cross_bias, feedforward_norm_gain, ffn_bias]
        )
        vectors = jnp.broadcast_to(vectors[None], (groups * ranks,) + vectors.shape)
        self_pair[0], self_pair[1], vectors = sync(*self_pair, vectors)
        vectors = lax.all_to_all(vectors, every, 0, 0, tiled=True)
        vectors = vectors.transpose(1, 0, 2).reshape(6, width).astype(f32)
        self_pair = last_stage(self_pair)
        self_pair[0], self_pair[1], vectors = sync(*self_pair, vectors)
        cross_other = tie(cross_other, *self_pair)
        w_qk = self_pair[0].reshape(width, 2 * part)
        w_v = self_pair[1][..., :part].reshape(width, part)
        cross_set = both_groups(cross_set, cross_other)
        cross_pair = first_stage([cross_set[..., : 2 * part], cross_set[..., 2 * part :]])
        memory_chips = gather_chips(own_memory)

        down_rows = ffn_down.reshape(ff_rows, ff_blocks, ff_part).transpose(1, 0, 2)
        up_own, down_own = sync(
            other_own[..., 3 * part :].reshape(rank_rows, ff_part),
            down_rows.reshape(rank_rows, ff_part),
            self_pair[0],
        )[:2]
        up_other = swap_groups(up_own)
        down_other = swap_groups(tie(down_own, up_other))

        def out_rows(rows_in):
            pieces = rows_in.reshape(ranks, sets, ranks, weight_rows, part)
            return join_rows(from_ranks(pieces, 0), rank_own)

        w_sout = out_rows(self_pair[1][..., part:])

        n_pieces = g_size * ranks
        seq_own = g_own * ranks + rank_own
        ids = lax.dynamic_index_in_dim(block_ids, g_own, 0, keepdims=False)
        length = lax.dynamic_index_in_dim(seq_lengths, g_own, 0, keepdims=False)
        live = jnp.arange(ids.shape[0], dtype=jnp.int32) < length
        both = jnp.stack([ids, jnp.where(live, ids, jnp.int32(2**30))]).reshape(2, n_pieces, piece_rows)
        for flip in flip_bits(n_pieces):
            turned = both.reshape(2, n_pieces // (2 * flip), 2, flip, piece_rows)
            turned = jnp.concatenate([turned[:, :, 1:], turned[:, :, :1]], axis=2).reshape(both.shape)
            both = jnp.where((seq_own & flip) != 0, turned, both)
        both = both.reshape(2, g_size, ranks, piece_rows).transpose(0, 2, 1, 3).reshape(2, -1)
        bias = jnp.where(both[1][:, None] <= both[0][None, :], 0.0, neg_large).astype(f32)

        def row_blocks(values):
            return jnp.split(values, z_size, axis=0)

        def joined(blocks):
            return jnp.concatenate(blocks, axis=0)

        qk = matmul(all_tokens, w_qk).astype(bf16)
        queries, keys = qk[:, :part], qk[:, part:]
        values = matmul(all_tokens, w_v).astype(bf16)
        attended, self_probs = attention_forward(queries, keys, values, bias)
        attended, cross_pair[0], cross_pair[1], up_other = sync(attended, *cross_pair, up_other)
        cross_pair = last_stage(cross_pair)
        kept, came, memory_blocks = sum_rows(
            row_blocks(attended),
            lambda x: matmul(x, w_sout),
            lambda term: with_partner([tie(x, term) for x in memory_chips]),
        )
        kept, came, down_other = sync(kept, came, down_other)
        hidden_one, normed_one, inv_one = norm_rows(own_tokens, kept, came, vectors, 0)
        ffn_pair = first_stage([both_groups(up_own, up_other), both_groups(down_own, down_other)])
        own_cotangent = bring_home(tie(cotangent, down_other))

        all_memory = joined(memory_blocks)
        w_ckv = cross_pair[0].reshape(width, 2 * part)
        w_cq = cross_pair[1][..., :part].reshape(width, part)
        w_cout = out_rows(cross_pair[1][..., part:])
        mem_kv = matmul(all_memory, w_ckv).astype(bf16)
        mem_keys, mem_values = mem_kv[:, :part], mem_kv[:, part:]

        one_blocks = gather_rows(hidden_one)
        one_blocks[-1], mem_keys, mem_values, w_cout, ffn_pair[0], ffn_pair[1] = sync(
            one_blocks[-1], mem_keys, mem_values, w_cout, *ffn_pair
        )
        ffn_pair = last_stage(ffn_pair)
        cross_rows = [matmul(x, w_cq).astype(bf16) for x in one_blocks]
        crossed = [attention_forward(x, mem_keys, mem_values, None) for x in cross_rows]
        cross_probs = [x[1] for x in crossed]
        crossed = [x[0] for x in crossed]
        kept, came = sum_rows(crossed, lambda x: matmul(x, w_cout))
        hidden_two, normed_two, inv_two = norm_rows(hidden_one, kept, came, vectors, 2)
        hidden_two, own_cotangent = sync(hidden_two, own_cotangent)
        two_blocks = gather_rows(hidden_two)
        w_up = ffn_pair[0].reshape(width, ff_part)
        w_down = ffn_pair[1].reshape(groups, ff_blocks, ff_rows, ff_part).transpose(0, 2, 1, 3)
        w_down = w_down.reshape(ff_part, width)
        upper_rows = [matmul(x, w_up) for x in two_blocks]
        active_rows = [gelu_tanh(x).astype(bf16) for x in upper_rows]
        kept, came, slopes = sum_rows(
            active_rows,
            lambda x: matmul(x, w_down),
            lambda term: [gelu_slope(tie(x, term)) for x in upper_rows],
        )
        layer_rows, grad_three, branch, sums_three = norm_turn(
            hidden_two, kept, came, vectors, 4, own_cotangent
        )

        all_dims = list(range(len(axes)))

        def first_sums(pair):
            pair = [x.reshape(halves(len(axes)) + x.shape[-2:]) for x in pair]
            return [scatter_axes(pair[0], all_dims, first_a), scatter_axes(pair[1], all_dims, first_b)]

        def more_sums(pair):
            return [
                scatter_axes(pair[0], [d for d in all_dims if d not in first_a], rest_a),
                scatter_axes(pair[1], [d for d in all_dims if d not in first_b], rest_b),
            ]

        def last_sums(pair):
            return [scatter_axes(x, g_axes, g_axes) for x in pair]

        branch_blocks = gather_rows(branch)
        grad_upper = [
            (transposed_product(x, w_down) * y).astype(bf16) for x, y in zip(branch_blocks, slopes)
        ]

        def ffn_gradients(term):
            rows, _ = lax.optimization_barrier((branch_blocks, term))
            down = outer_product_sum(joined(active_rows), joined(rows)).astype(bf16)
            down = down.reshape(groups, ff_rows, ff_blocks, ff_part).transpose(0, 2, 1, 3)
            up = outer_product_sum(joined(two_blocks), joined(grad_upper)).astype(bf16)
            return [up.reshape(groups, rank_rows, ff_part), down.reshape(groups, rank_rows, ff_part)]

        kept, came, ffn_grads = sum_rows(
            grad_upper, lambda x: transposed_product(x, w_up), ffn_gradients
        )
        ffn_grads = first_sums(ffn_grads)
        grad_two, branch, sums_two = norm_back(
            grad_three, kept, came, normed_two, inv_two, vectors, 2, ALL_OF_IT
        )
        layer_out = send_back(tie(layer_rows, branch))

        branch_blocks = gather_rows(branch)
        grad_crossed = [transposed_product(x, w_cout).astype(bf16) for x in branch_blocks]
        grad_cross_rows, sums = [], []
        for b in range(z_size):
            grad_rows, *sums = attention_backward(
                cross_rows[b], mem_keys, mem_values, cross_probs[b], 0, grad_crossed[b], sums, b == z_size - 1
            )
            grad_cross_rows.append(grad_rows)
        grad_mem_kv = jnp.concatenate(sums, axis=1)

        def cout_gradient(term):
            rows, _ = lax.optimization_barrier((branch_blocks, term))
            return outer_product_sum(joined(crossed), joined(rows)).astype(bf16)

        kept, came, cout_grad = sum_rows(
            grad_cross_rows, lambda x: transposed_product(x, w_cq), cout_gradient
        )
        kept, layer_out, *ffn_grads = sync(kept, layer_out, *ffn_grads)
        ffn_grads = more_sums(ffn_grads)
        grad_one, branch, sums_one = norm_back(grad_two, kept, came, normed_one, inv_one, vectors, 0)
        branch_blocks = gather_rows(branch)
        cout_grad = tie(cout_grad, branch).reshape(sets, ranks, weight_rows, width)
        cout_pieces = from_ranks(cout_grad, 1)
        vec_sums = jnp.concatenate([sums_one, sums_two, sums_three], axis=0)
        for flip in flip_bits(dp_size):
            vec_sums = vec_sums + swap(vec_sums, "dp", dp_size, flip)
        branch_blocks[-1], vec_sums = sync(branch_blocks[-1], vec_sums)
        grad_mem_kv = tie(grad_mem_kv, branch)
        mem_kv_grad = outer_product_sum(all_memory, grad_mem_kv).astype(bf16)
        cross_grad = outer_product_sum(joined(one_blocks), joined(grad_cross_rows)).astype(bf16)
        grad_attended = [transposed_product(x, w_sout).astype(bf16) for x in branch_blocks]
        sout_grad = outer_product_sum(attended, joined(branch_blocks)).astype(bf16)
        sout_pieces = from_ranks(sout_grad.reshape(sets, ranks, weight_rows, width), 1)
        memory_kept, memory_came = sum_rows(
            row_blocks(grad_mem_kv), lambda x: transposed_product(x, w_ckv)
        )
        memory_rows = (memory_kept + memory_came.astype(f32)).astype(bf16)

        query_blocks = row_blocks(queries)
        chip_rows = queries.shape[0] // z_size
        grad_queries, sums = [], []
        for b in range(z_size):
            grad_rows, *sums = attention_backward(
                query_blocks[b],
                keys,
                values,
                self_probs,
                b * chip_rows,
                grad_attended[b],
                sums,
                b == z_size - 1,
            )
            grad_queries.append(grad_rows)
        grad_qk = jnp.concatenate([joined(grad_queries), sums[0]], axis=1)
        grad_values = sums[1]
        def by_group(grads):
            return grads.reshape(groups, rank_rows, -1)

        qk_grad = outer_product_sum(all_tokens, grad_qk).astype(bf16)
        grads_a = jnp.concatenate([by_group(qk_grad), by_group(mem_kv_grad)], axis=2)
        v_grad = outer_product_sum(all_tokens, grad_values).astype(bf16)
        grads_b = pack_grads(rank_own, by_group(v_grad), sout_pieces, by_group(cross_grad), cout_pieces)
        grads_a, grads_b, *ffn_grads = sync(grads_a, grads_b, *ffn_grads)
        sums = first_sums([grads_a, grads_b])
        down_grad = scatter_axes(ffn_grads[1], g_axes, g_axes)
        up_pieces = ffn_grads[0].reshape(g_size * ranks, weight_rows, ff_part)
        up_pieces = lax.all_to_all(up_pieces, ("g", "z", "c"), 0, 0, tiled=True)

        row_pairs = zip(row_blocks(tie(grad_qk, grads_a, grads_b)), row_blocks(grad_values))
        kept, came = sum_rows(
            list(row_pairs),
            lambda x: transposed_product(x[0], w_qk) + transposed_product(x[1], w_v),
        )
        tokens_grad = (residual_scale * grad_one + (kept + came.astype(f32))).astype(bf16)
        sums[0], sums[1], tokens_grad, memory_rows = sync(*sums, tokens_grad, memory_rows)
        sums = more_sums(sums)
        tokens_grad = send_back(tokens_grad)
        memory_grad = send_back(memory_rows)
        vec_sums = tie(vec_sums, *sums)
        for name, size in (("c", CORES), ("z", z_size), ("g", g_size)):
            for flip in flip_bits(size):
                vec_sums = vec_sums + swap(vec_sums, name, size, flip)
        by_ranks = (g_size * ranks, weight_rows)

        def to_own(parts_in):
            return lax.all_to_all(parts_in, ("g", "z", "c"), 0, 0, tiled=True)

        pieces = jnp.concatenate([sums[0], sums[1][..., :part], sums[1][..., 2 * part : 3 * part]], axis=2)
        pieces = to_own(pieces.reshape(by_ranks + (6 * part,)))
        out_grads = jnp.concatenate([sums[1][..., part : 2 * part], sums[1][..., 3 * part :]], axis=2)
        out_grads = scatter_axes(out_grads, g_axes, g_axes)

        down_grad = down_grad.reshape(ff_blocks, ff_rows, ff_part).transpose(1, 0, 2)
        down_grad = down_grad.reshape(ff_rows, width)

        def own_rows_of(values):
            return values.reshape(ranks, weight_rows, part).transpose(1, 0, 2).reshape(weight_rows, width)

        (up_grad,) = columns_back(up_pieces, ranks, (ff_part,), ff_rows)
        query_grad, key_grad, mem_key_grad, mem_value_grad, value_grad, cross_grad = columns_back(
            pieces, ranks, (part,) * 6, 0
        )

        first = ((dp_own * g_size + g_own) * ranks + rank_own) * weight_rows
        vec_grads = lax.dynamic_slice_in_dim(vec_sums, first, weight_rows, axis=1)

        return (
            layer_out,
            tokens_grad,
            memory_grad,
            query_grad,
            key_grad,
            value_grad,
            own_rows_of(out_grads[:, :part]),
            cross_grad,
            mem_key_grad,
            mem_value_grad,
            own_rows_of(out_grads[:, part:]),
            up_grad,
            down_grad,
            vec_grads[0],
            vec_grads[1],
            vec_grads[2],
            vec_grads[3],
            vec_grads[4],
            vec_grads[5],
        )

    return body


def solution(mesh):
    dp_size, seq_size = mesh.shape["dp"], mesh.shape["seq"]

    def layer_step(*args):
        g_size = args[0].shape[0] // dp_size
        z_size = seq_size // (g_size * CORES)
        split_mesh = Mesh(
            mesh.devices.reshape(dp_size, g_size, z_size, CORES), ("dp", "g", "z", "c")
        )
        seq = ("g", "z", "c")
        every = ("dp", "g", "z", "c")
        rows = P("dp", seq, None)
        matrix = P(every, None)
        vector = P(every)
        return jax.shard_map(
            make_body(dp_size, g_size, z_size),
            mesh=split_mesh,
            in_specs=(rows,) * 3 + (P("dp", None), P("dp")) + (matrix,) * 10 + (vector,) * 6,
            out_specs=(rows,) * 3 + (matrix,) * 10 + (vector,) * 6,
            check_vma=False,
        )(*args)

    return layer_step
```

```python
import jax
import jax.numpy as jnp
from jax import lax
from jax.experimental import pallas as pl
from jax.experimental.pallas import tpu as pltpu
from jax.sharding import Mesh, PartitionSpec as P

HEAD_DIM = 64
CORES = 2

eps_norm = 1e-05
residual_scale = 18.0**0.25
gelu_coef = 0.7978845608028654
neg_large = -1e30
bf16 = jnp.bfloat16
f32 = jnp.float32


def gelu_tanh(values_in):
    inner = gelu_coef * (values_in + 0.044715 * values_in * values_in * values_in)
    return 0.5 * values_in * (1.0 + jnp.tanh(inner))


def gelu_slope(values_in):
    squared = values_in * values_in
    tanh_val = jnp.tanh(gelu_coef * (values_in + 0.044715 * squared * values_in))
    return 0.5 * (1.0 + tanh_val) + 0.5 * values_in * (1.0 - tanh_val * tanh_val) * gelu_coef * (
        1.0 + 3.0 * 0.044715 * squared
    )


def matmul(first_mat, second_mat):
    return jnp.dot(first_mat, second_mat, preferred_element_type=f32)


def transposed_product(first_mat, second_mat):
    return lax.dot_general(first_mat, second_mat, (((1,), (1,)), ((), ())), preferred_element_type=f32)


def outer_product_sum(first_mat, second_mat):
    return lax.dot_general(first_mat, second_mat, (((0,), (0,)), ((), ())), preferred_element_type=f32)


LIMIT = pltpu.CompilerParams(vmem_limit_bytes=16 * 1024 * 1024)
ALL_OF_IT = pltpu.CompilerParams(vmem_limit_bytes=60 * 1024 * 1024)
SCALAR = pl.BlockSpec(memory_space=pltpu.SMEM)
WHOLE = pl.BlockSpec(memory_space=pltpu.VMEM)


def on_chip(values):
    return pltpu.with_memory_space_constraint(values, pltpu.VMEM)


def chip_call(kernel, outs, name, *args, scalar=None):
    scalars = [] if scalar is None else [scalar.reshape(1)]
    return pl.pallas_call(
        kernel,
        in_specs=[SCALAR] * len(scalars) + [WHOLE] * len(args),
        out_specs=[WHOLE] * len(outs),
        out_shape=[pltpu.VMEM(shape, dtype) for shape, dtype in outs],
        compiler_params=LIMIT,
        name=name,
    )(*scalars, *[on_chip(x) for x in args])


ANY = pl.BlockSpec(memory_space=pl.ANY)
FAR = pl.BlockSpec(memory_space=pltpu.HBM)


def copy_call(copies, out, name, scalar, *args):
    count = []

    def kernel(scalar_ref, *refs):
        sems = refs[-1]
        running = [
            pltpu.make_async_copy(source, target, sems.at[i])
            for i, (source, target) in enumerate(copies(scalar_ref[0], refs[:-2], refs[-2]))
        ]
        for one in running:
            one.start()
        for one in running:
            one.wait()

    class Probe:
        at = property(lambda self: self)

        def __getitem__(self, index):
            return self

    count = len(copies(0, [Probe()] * len(args), Probe()))
    return pl.pallas_call(
        kernel,
        in_specs=[SCALAR] + [ANY] * len(args),
        out_specs=ANY,
        out_shape=jax.ShapeDtypeStruct(*out),
        scratch_shapes=[pltpu.SemaphoreType.DMA((count,))],
        compiler_params=LIMIT,
        name=name,
    )(scalar.reshape(1), *args)


def _mean(values):
    return jnp.mean(values, axis=-1, keepdims=True)


def _normed(residual, kept, came):
    values = residual_scale * residual.astype(f32) + (kept + came.astype(f32))
    centred = values - _mean(values)
    inv_std = lax.rsqrt(_mean(centred * centred) + eps_norm)
    return centred * inv_std, inv_std


def _norm_back(grad_out, normed, inv_std, gain):
    scaled = grad_out * gain
    grad_in = inv_std * (scaled - _mean(scaled) - normed * _mean(scaled * normed))
    sums = [jnp.sum(grad_out * normed, axis=0, keepdims=True), jnp.sum(grad_out, axis=0, keepdims=True)]
    return grad_in, jnp.concatenate(sums, axis=0)


def norm_rows(residual, kept, came, vectors, row):
    def kernel(res, kept, came, vec, hidden, normed, inv):
        n, r = _normed(res[...], kept[...], came[...])
        hidden[...] = (n * vec[row : row + 1, :] + vec[row + 1 : row + 2, :]).astype(bf16)
        normed[...] = n
        inv[...] = jnp.broadcast_to(r, inv.shape)

    shape = residual.shape
    outs = [(shape, bf16), (shape, f32), ((shape[0], 128), f32)]
    return chip_call(kernel, outs, "norm_rows", residual, kept, came, vectors)


def norm_turn(residual, kept, came, vectors, row, cotangent):
    def kernel(res, kept, came, vec, cot, layer, grad, rounded, sums):
        gain = vec[row : row + 1, :]
        n, r = _normed(res[...], kept[...], came[...])
        layer[...] = (n * gain + vec[row + 1 : row + 2, :]).astype(bf16)
        g, s = _norm_back(cot[...].astype(f32), n, r, gain)
        grad[...] = g
        rounded[...] = g.astype(bf16)
        sums[...] = s

    shape = residual.shape
    outs = [(shape, bf16), (shape, f32), (shape, bf16), ((2, shape[1]), f32)]
    return chip_call(kernel, outs, "norm_turn", residual, kept, came, vectors, cotangent)


def norm_back(grad_prev, kept, came, normed, inv_std, vectors, row, limit=LIMIT):
    shape = grad_prev.shape
    args = [grad_prev, kept, came, normed, inv_std]

    def kernel(*refs):
        vec, grad, rounded, sums = refs[5:9]
        prev, kept, came, normed, inv = refs[9:14]
        running = [pltpu.make_async_copy(refs[i], refs[9 + i], refs[14].at[i]) for i in range(5)]
        for one in running:
            one.start()
        for one in running:
            one.wait()
        grad_out = residual_scale * prev[...] + (kept[...] + came[...].astype(f32))
        g, s = _norm_back(grad_out, normed[...], inv[:, :1], vec[row : row + 1, :])
        grad[...] = g
        rounded[...] = g.astype(bf16)
        sums[...] = s

    outs = [(shape, f32), (shape, bf16), ((2, shape[1]), f32)]
    return pl.pallas_call(
        kernel,
        in_specs=[FAR] * 5 + [WHOLE],
        out_specs=[WHOLE] * 3,
        out_shape=[pltpu.VMEM(x, dtype) for x, dtype in outs],
        scratch_shapes=[pltpu.VMEM(x.shape, x.dtype) for x in args] + [pltpu.SemaphoreType.DMA((5,))],
        compiler_params=limit,
        name="norm_back",
    )(*args, on_chip(vectors))


PAIR = 2 * HEAD_DIM


def _head_of_pair(values, head):
    lane = lax.broadcasted_iota(jnp.int32, (1, PAIR), 1)
    return jnp.where((lane // HEAD_DIM) == head, values, jnp.zeros((), values.dtype))


def _times(first, second, dims):
    return lax.dot_general(first, second, ((dims[:1], dims[1:]), ((), ())), preferred_element_type=f32)


def attention_forward(queries, keys, values, bias):
    rows, width = queries.shape
    key_rows = keys.shape[0]
    scale = HEAD_DIM ** (-0.5)

    def kernel(q_ref, k_ref, v_ref, *rest):
        out_ref, probs_ref = rest[-2:]
        for pair in range(width // PAIR):
            cols = slice(pair * PAIR, (pair + 1) * PAIR)
            q, k, v = q_ref[:, cols] * jnp.asarray(scale, bf16), k_ref[:, cols], v_ref[:, cols]
            mixed = None
            for head in range(2):
                scores = _times(k, _head_of_pair(q, head), (1, 1))
                if bias is not None:
                    scores = scores + rest[0][...]
                expo = jnp.exp(scores - jnp.max(scores, axis=0, keepdims=True))
                probs = (expo * (1.0 / jnp.sum(expo, axis=0, keepdims=True))).astype(bf16)
                probs_ref[2 * pair + head] = probs
                part = _times(_head_of_pair(v, head), probs, (0, 0))
                mixed = part if mixed is None else mixed + part
            out_ref[:, cols] = mixed.T.astype(bf16)

    args = [queries, keys, values] + ([] if bias is None else [bias])
    outs = [((rows, width), bf16), ((width // HEAD_DIM, key_rows, rows), bf16)]
    return chip_call(kernel, outs, "attend", *args)


def attention_backward(queries, keys, values, probs, first, grad_mixed, sums, last):
    rows, width = queries.shape
    key_rows = keys.shape[0]
    scale = HEAD_DIM ** (-0.5)

    def kernel(q_ref, k_ref, v_ref, p_ref, g_ref, *rest):
        before, (dq_ref, dk_ref, dv_ref) = rest[: len(sums)], rest[len(sums) :]
        for pair in range(width // PAIR):
            cols = slice(pair * PAIR, (pair + 1) * PAIR)
            q, k, v, g = q_ref[:, cols], k_ref[:, cols], v_ref[:, cols], g_ref[:, cols]
            dq = None
            dk, dv = [x[:, cols] for x in before] if sums else (None, None)
            for head in range(2):
                g_one = _head_of_pair(g, head)
                rounded = p_ref[2 * pair + head, :, first : first + rows]
                wide = rounded.astype(f32)
                weighted = _times(v, g_one, (1, 1)) * wide
                g_scores = (weighted - wide * jnp.sum(weighted, axis=0, keepdims=True)).astype(bf16)
                part_q = _times(_head_of_pair(k, head), g_scores, (0, 0))
                part_k = _times(g_scores, _head_of_pair(q, head), (1, 0))
                part_v = _times(rounded, g_one, (1, 0))
                dq = part_q if dq is None else dq + part_q
                dk = part_k if dk is None else dk + part_k
                dv = part_v if dv is None else dv + part_v
            dq_ref[:, cols] = (dq.T * scale).astype(bf16)
            dk_ref[:, cols] = (dk * scale).astype(bf16) if last else dk
            dv_ref[:, cols] = dv.astype(dv_ref.dtype)

    kind = bf16 if last else f32
    outs = [((rows, width), bf16), ((key_rows, width), kind), ((key_rows, width), kind)]
    return chip_call(kernel, outs, "attend_back", queries, keys, values, probs, grad_mixed, *sums)


def swap(values, name, size, flip):
    return lax.ppermute(values, name, [(i, i ^ flip) for i in range(size)])


def flip_bits(size):
    return [1 << b for b in range(size.bit_length() - 1)]


sync = lambda *values: lax.optimization_barrier(values)


def tie(value, *others):
    return lax.optimization_barrier((value,) + others)[0]


def lay_out(ranks, query, key, value, mem_key, mem_value, cross, up, own_out, mem_out):
    rows, width = query.shape
    part = width // ranks
    ff_part = up.shape[1] // ranks
    groups = ff_part * ranks // up.shape[1] * (width // (ranks * rows))
    unit = ff_part // groups

    def kernel(*refs):
        (self_ref, cross_ref, up_ref, so_ref, co_ref), ins, sems = refs[9:14], refs[14:23], refs[23]
        running = [pltpu.make_async_copy(refs[i], ins[i], sems.at[i]) for i in range(9)]
        for one in running:
            one.start()
        for one in running:
            one.wait()
        for r in range(ranks):
            cols = slice(r * part, (r + 1) * part)
            for i in range(3):
                self_ref[r, :, i * part : (i + 1) * part] = ins[i][:, cols]
                cross_ref[r, :, i * part : (i + 1) * part] = ins[3 + i][:, cols]
            so_ref[r] = ins[7][:, cols]
            co_ref[r] = ins[8][:, cols]
            for g in range(groups):
                first = (g * ranks + r) * unit
                up_ref[r, :, g * unit : (g + 1) * unit] = ins[6][:, first : first + unit]

    shapes = [3 * part, 3 * part, ff_part, part, part]
    return pl.pallas_call(
        kernel,
        in_specs=[FAR] * 9,
        out_specs=[WHOLE] * 5,
        scratch_shapes=[pltpu.VMEM((rows, width), bf16)] * 6
        + [pltpu.VMEM(up.shape, bf16)]
        + [pltpu.VMEM((rows, width), bf16)] * 2
        + [pltpu.SemaphoreType.DMA((9,))],
        out_shape=[pltpu.VMEM((ranks, rows, n), bf16) for n in shapes],
        compiler_params=ALL_OF_IT,
        name="lay_out",
    )(query, key, value, mem_key, mem_value, cross, up, own_out, mem_out)


def columns_back(pieces, ranks, counts, unit_first):
    terms, rows = pieces.shape[0] // ranks, pieces.shape[1]

    def kernel(in_ref, *outs):
        def total(r, cols):
            found = in_ref[r, :, cols].astype(f32)
            for term in range(1, terms):
                found = found + in_ref[term * ranks + r, :, cols].astype(f32)
            return found

        first = 0
        for out, count in zip(outs, counts):
            if out is outs[0] and unit_first:
                units = count // unit_first
                for r in range(ranks):
                    for g in range(units):
                        at = (g * ranks + r) * unit_first
                        cols = slice(first + g * unit_first, first + (g + 1) * unit_first)
                        out[:, at : at + unit_first] = total(r, cols)
            else:
                for r in range(ranks):
                    out[:, r * count : (r + 1) * count] = total(r, slice(first, first + count))
            first += count

    return pl.pallas_call(
        kernel,
        in_specs=[WHOLE],
        out_specs=[WHOLE] * len(counts),
        out_shape=[jax.ShapeDtypeStruct((rows, ranks * n), f32) for n in counts],
        compiler_params=LIMIT,
        name="columns_back",
    )(on_chip(pieces))


def join_rows(pieces, rank):
    ranks = len(pieces)
    sets, blocks, rows, part = pieces[0].shape

    def copies(own, refs, out):
        return [
            (refs[r].at[p, b], out.at[p, own ^ r, :, b * part : (b + 1) * part])
            for r in range(ranks)
            for p in range(sets)
            for b in range(blocks)
        ]

    joined = copy_call(copies, ((sets, ranks, rows, blocks * part), bf16), "join_rows", rank, *pieces)
    return joined.reshape(sets * ranks * rows, blocks * part)


def pack_grads(rank, *parts):
    args = []
    places = []
    first = 0
    for one in parts:
        if isinstance(one, list):
            ranks, (sets, rows, width) = len(one), one[0].shape
            part = width // ranks
            for r in range(ranks):
                for p in range(sets):
                    for b in range(ranks):
                        at = slice(b * rows, (b + 1) * rows), slice(first, first + part)
                        places.append((len(args) + r, (p, slice(None), slice(b * part, (b + 1) * part)), (r, sets, p), at))
            args += one
            first += part
        elif one.ndim == 4:
            ranks, sets, rows, width = one.shape
            part = width // ranks
            for r in range(ranks):
                for p in range(sets):
                    for b in range(ranks):
                        at = slice(b * rows, (b + 1) * rows), slice(first, first + part)
                        source = (r, p, slice(None), slice(b * part, (b + 1) * part))
                        places.append((len(args), source, r * sets + p, at))
            args.append(one)
            first += part
        else:
            groups, n, m = one.shape
            places.append((len(args), (slice(None),) * 3, None, (slice(None), slice(first, first + m))))
            args.append(one)
            first += m

    def copies(own, refs, out):
        found = []
        for i, source, piece, at in places:
            lead = slice(None) if piece is None else piece
            if isinstance(piece, tuple):
                lead = (own ^ piece[0]) * piece[1] + piece[2]
            found.append((refs[i].at[source], out.at[(lead,) + at]))
        return found

    return copy_call(copies, ((groups, n, first), bf16), "pack_grads", rank, *args)


def make_body(dp_size, g_size, z_size):
    ranks = z_size * CORES
    groups = dp_size * g_size
    every = ("dp", "g", "z", "c")

    def body(
        tokens,
        memory,
        cotangent,
        block_ids,
        seq_lengths,
        self_query,
        self_key,
        self_value,
        self_out,
        cross_query,
        cross_key,
        cross_value,
        cross_out,
        ffn_up,
        ffn_down,
        attn_gain,
        attn_bias,
        cross_gain,
        cross_bias,
        feedforward_norm_gain,
        ffn_bias,
    ):
        dp_own = lax.axis_index("dp")
        g_own = lax.axis_index("g")
        rank_own = lax.axis_index("z") * CORES + lax.axis_index("c")
        piece_rows = tokens.shape[1]
        width = tokens.shape[2]
        weight_rows = self_query.shape[0]
        rank_rows = ranks * weight_rows
        part = width // ranks
        sets = groups // ranks
        ff_rows = ffn_down.shape[0]
        ff_part = groups * ff_rows
        ff_blocks = width // ff_part

        def bits_of(name, size, own):
            return [(name, size, f, (own // f) % 2) for f in reversed(flip_bits(size))]

        axes = bits_of("dp", dp_size, dp_own) + bits_of("g", g_size, g_own)
        n_dp = dp_size.bit_length() - 1
        g_axes = list(range(n_dp, len(axes)))
        order_a = list(reversed(range(n_dp)))
        order_b = list(range(n_dp))

        def gather_axes(values, dims, order, after=()):
            for ax in order:
                name, size, flip, bit = axes[ax]
                other = tie(swap(values, name, size, flip), *after)
                pos = len([d for d in dims if d < ax])
                values = jnp.where(
                    bit == 1, jnp.stack([other, values], pos), jnp.stack([values, other], pos)
                )
                dims = sorted(dims + [ax])
            return values

        def scatter_axes(values, dims, order):
            dims = list(dims)
            for i, ax in enumerate(order):
                name, size, flip, bit = axes[ax]
                pos = dims.index(ax)
                other = swap(
                    lax.dynamic_index_in_dim(values, 1 - bit, pos, keepdims=False), name, size, flip
                )
                kept = lax.dynamic_index_in_dim(values, bit, pos, keepdims=False)
                values = kept.astype(f32) + other.astype(f32)
                dims.remove(ax)
                if dims:
                    values = values.astype(bf16)
            return values

        def halves(n):
            return (2,) * n

        def finish(values):
            shape = values.shape[1:]
            return scatter_axes(values.reshape(halves(len(g_axes)) + shape), g_axes, g_axes)

        def rank_swap(values, flip):
            return swap(values, ("z", "c"), ranks, flip)

        def from_ranks(pieces, axis):
            got = []
            for f in range(ranks):
                piece = lax.dynamic_index_in_dim(pieces, rank_own ^ f, axis, keepdims=False)
                got.append(piece if f == 0 else rank_swap(piece, f))
            return got

        def gather_rows(values):
            return with_partner(gather_chips(values))

        def gather_chips(values):
            blocks = [values]
            for flip in flip_bits(z_size):
                blocks = blocks + [swap(b, "z", z_size, flip) for b in blocks]
            return blocks

        def with_partner(blocks):
            return [jnp.concatenate([b, swap(b, "c", CORES, 1)], axis=0) for b in blocks]

        def sum_rows(blocks, product, fill=None):
            own_rows = piece_rows * g_size
            sums = [None] * z_size
            for b in reversed(range(z_size)):
                partial = product(blocks[b])
                came = swap(partial[own_rows:].astype(bf16), "c", CORES, 1)
                sums[b] = partial[:own_rows] + came.astype(f32)
            for flip in reversed(flip_bits(z_size)):
                leaving = [sums[b + flip].astype(bf16) for b in range(flip)]
                came = [swap(x, "z", z_size, flip) for x in leaving]
                if flip > 1:
                    sums = [sums[b] + came[b].astype(f32) for b in range(flip)]
            if fill is None:
                return sums[0], came[0]
            filled = fill(leaving[0])
            kept, last, filled = lax.optimization_barrier((sums[0], came[0], filled))
            return kept, last, filled

        def bring_home(values, *after):
            got = []
            for f in range(g_size):
                piece = lax.dynamic_index_in_dim(values, g_own ^ f, 0, keepdims=False)
                got.append(piece if f == 0 else tie(swap(piece, "g", g_size, f), *after))
            return jnp.concatenate(got, axis=-2)

        def send_back(values):
            blocks = values.reshape(g_size, piece_rows, width)
            got = [blocks[0]] + [swap(blocks[f], "g", g_size, f) for f in range(1, g_size)]
            got = jnp.stack(got)
            return jnp.stack(
                [lax.dynamic_index_in_dim(got, g_own ^ f, 0, keepdims=False) for f in range(g_size)]
            )

        own_tokens = bring_home(tokens)
        self_parts, cross_parts, up_parts, so_parts, co_parts = lay_out(
            ranks,
            self_query,
            self_key,
            self_value,
            cross_key,
            cross_value,
            cross_query,
            ffn_up,
            self_out,
            cross_out,
        )

        def to_ranks(parts_in):
            return lax.all_to_all(parts_in, ("z", "c"), 0, 0, tiled=True)

        self_own, own_tokens = sync(to_ranks(self_parts), own_tokens)
        self_set = jnp.concatenate([self_own, so_parts], axis=2).reshape(rank_rows, 4 * part)
        self_set = gather_axes(self_set, [], g_axes)
        token_blocks = gather_rows(own_tokens)
        other_own = to_ranks(tie(jnp.concatenate([cross_parts, up_parts], axis=2), self_own))
        half_a, half_b, *token_blocks = sync(
            self_set[..., : 2 * part], self_set[..., 2 * part :], *token_blocks
        )
        other_own = tie(other_own, half_a)

        first_a, rest_a = order_a[:1], order_a[1:]
        first_b, rest_b = order_b[:1], order_b[1:]

        def first_stage(pair):
            return [gather_axes(pair[0], g_axes, first_a), gather_axes(pair[1], g_axes, first_b)]

        def last_stage(pair):
            pair = [
                gather_axes(pair[0], sorted(g_axes + first_a), rest_a),
                gather_axes(pair[1], sorted(g_axes + first_b), rest_b),
            ]
            return [x.reshape((groups,) + x.shape[-2:]) for x in pair]

        assert len(g_axes) == 1
        g_axis = axes[g_axes[0]]

        def swap_groups(values):
            return swap(values, *g_axis[:3])

        def both_groups(own, other):
            return jnp.where(g_axis[3] == 1, jnp.stack([other, own]), jnp.stack([own, other]))

        self_pair = first_stage([half_a, half_b])
        cross_set = jnp.concatenate([other_own[..., : 3 * part], co_parts], axis=2)
        cross_set = cross_set.reshape(rank_rows, 4 * part)
        cross_other = swap_groups(cross_set)
        own_memory = bring_home(tie(memory, self_set), *self_pair)
        all_tokens = jnp.concatenate(token_blocks, axis=0)
        vectors = jnp.stack(
            [attn_gain, attn_bias, cross_gain, cross_bias, feedforward_norm_gain, ffn_bias]
        )
        vectors = jnp.broadcast_to(vectors[None], (groups * ranks,) + vectors.shape)
        self_pair[0], self_pair[1], vectors = sync(*self_pair, vectors)
        vectors = lax.all_to_all(vectors, every, 0, 0, tiled=True)
        vectors = vectors.transpose(1, 0, 2).reshape(6, width).astype(f32)
        self_pair = last_stage(self_pair)
        self_pair[0], self_pair[1], vectors = sync(*self_pair, vectors)
        cross_other = tie(cross_other, *self_pair)
        w_qk = self_pair[0].reshape(width, 2 * part)
        w_v = self_pair[1][..., :part].reshape(width, part)
        cross_set = both_groups(cross_set, cross_other)
        cross_pair = first_stage([cross_set[..., : 2 * part], cross_set[..., 2 * part :]])
        memory_chips = gather_chips(own_memory)

        down_rows = ffn_down.reshape(ff_rows, ff_blocks, ff_part).transpose(1, 0, 2)
        up_own, down_own = sync(
            other_own[..., 3 * part :].reshape(rank_rows, ff_part),
            down_rows.reshape(rank_rows, ff_part),
            self_pair[0],
        )[:2]
        up_other = swap_groups(up_own)
        down_other = swap_groups(tie(down_own, up_other))

        def out_rows(rows_in):
            pieces = rows_in.reshape(ranks, sets, ranks, weight_rows, part)
            return join_rows(from_ranks(pieces, 0), rank_own)

        w_sout = out_rows(self_pair[1][..., part:])

        n_pieces = g_size * ranks
        seq_own = g_own * ranks + rank_own
        ids = lax.dynamic_index_in_dim(block_ids, g_own, 0, keepdims=False)
        length = lax.dynamic_index_in_dim(seq_lengths, g_own, 0, keepdims=False)
        live = jnp.arange(ids.shape[0], dtype=jnp.int32) < length
        both = jnp.stack([ids, jnp.where(live, ids, jnp.int32(2**30))]).reshape(2, n_pieces, piece_rows)
        for flip in flip_bits(n_pieces):
            turned = both.reshape(2, n_pieces // (2 * flip), 2, flip, piece_rows)
            turned = jnp.concatenate([turned[:, :, 1:], turned[:, :, :1]], axis=2).reshape(both.shape)
            both = jnp.where((seq_own & flip) != 0, turned, both)
        both = both.reshape(2, g_size, ranks, piece_rows).transpose(0, 2, 1, 3).reshape(2, -1)
        bias = jnp.where(both[1][:, None] <= both[0][None, :], 0.0, neg_large).astype(f32)

        def row_blocks(values):
            return jnp.split(values, z_size, axis=0)

        def joined(blocks):
            return jnp.concatenate(blocks, axis=0)

        qk = matmul(all_tokens, w_qk).astype(bf16)
        queries, keys = qk[:, :part], qk[:, part:]
        values = matmul(all_tokens, w_v).astype(bf16)
        attended, self_probs = attention_forward(queries, keys, values, bias)
        attended, cross_pair[0], cross_pair[1], up_other = sync(attended, *cross_pair, up_other)
        cross_pair = last_stage(cross_pair)
        kept, came, memory_blocks = sum_rows(
            row_blocks(attended),
            lambda x: matmul(x, w_sout),
            lambda term: with_partner([tie(x, term) for x in memory_chips]),
        )
        kept, came, down_other = sync(kept, came, down_other)
        hidden_one, normed_one, inv_one = norm_rows(own_tokens, kept, came, vectors, 0)
        ffn_pair = first_stage([both_groups(up_own, up_other), both_groups(down_own, down_other)])
        own_cotangent = bring_home(tie(cotangent, down_other))

        all_memory = joined(memory_blocks)
        w_ckv = cross_pair[0].reshape(width, 2 * part)
        w_cq = cross_pair[1][..., :part].reshape(width, part)
        w_cout = out_rows(cross_pair[1][..., part:])
        mem_kv = matmul(all_memory, w_ckv).astype(bf16)
        mem_keys, mem_values = mem_kv[:, :part], mem_kv[:, part:]

        one_blocks = gather_rows(hidden_one)
        one_blocks[-1], mem_keys, mem_values, w_cout, ffn_pair[0], ffn_pair[1] = sync(
            one_blocks[-1], mem_keys, mem_values, w_cout, *ffn_pair
        )
        ffn_pair = last_stage(ffn_pair)
        cross_rows = [matmul(x, w_cq).astype(bf16) for x in one_blocks]
        crossed = [attention_forward(x, mem_keys, mem_values, None) for x in cross_rows]
        cross_probs = [x[1] for x in crossed]
        crossed = [x[0] for x in crossed]
        kept, came = sum_rows(crossed, lambda x: matmul(x, w_cout))
        hidden_two, normed_two, inv_two = norm_rows(hidden_one, kept, came, vectors, 2)
        hidden_two, own_cotangent = sync(hidden_two, own_cotangent)
        two_blocks = gather_rows(hidden_two)
        w_up = ffn_pair[0].reshape(width, ff_part)
        w_down = ffn_pair[1].reshape(groups, ff_blocks, ff_rows, ff_part).transpose(0, 2, 1, 3)
        w_down = w_down.reshape(ff_part, width)
        upper_rows = [matmul(x, w_up) for x in two_blocks]
        active_rows = [gelu_tanh(x).astype(bf16) for x in upper_rows]
        kept, came, slopes = sum_rows(
            active_rows,
            lambda x: matmul(x, w_down),
            lambda term: [gelu_slope(tie(x, term)) for x in upper_rows],
        )
        layer_rows, grad_three, branch, sums_three = norm_turn(
            hidden_two, kept, came, vectors, 4, own_cotangent
        )

        branch_blocks = gather_rows(branch)
        grad_upper = [
            (transposed_product(x, w_down) * y).astype(bf16) for x, y in zip(branch_blocks, slopes)
        ]

        def ffn_gradients(term):
            rows, _ = lax.optimization_barrier((branch_blocks, term))
            down = outer_product_sum(joined(active_rows), joined(rows)).astype(bf16)
            down = down.reshape(groups, ff_rows, ff_blocks, ff_part).transpose(0, 2, 1, 3)
            up = outer_product_sum(joined(two_blocks), joined(grad_upper)).astype(bf16)
            return jnp.concatenate(
                [up.reshape(groups, rank_rows, ff_part), down.reshape(groups, rank_rows, ff_part)],
                axis=1,
            )

        kept, came, ffn_grads = sum_rows(
            grad_upper, lambda x: transposed_product(x, w_up), ffn_gradients
        )
        ffn_grads = lax.psum_scatter(
            ffn_grads.reshape(groups * 2 * rank_rows, ff_part), "dp", scatter_dimension=0, tiled=True
        )
        grad_two, branch, sums_two = norm_back(
            grad_three, kept, came, normed_two, inv_two, vectors, 2, ALL_OF_IT
        )
        layer_out = send_back(tie(layer_rows, branch))

        branch_blocks = gather_rows(branch)
        grad_crossed = [transposed_product(x, w_cout).astype(bf16) for x in branch_blocks]
        grad_cross_rows, sums = [], []
        for b in range(z_size):
            grad_rows, *sums = attention_backward(
                cross_rows[b], mem_keys, mem_values, cross_probs[b], 0, grad_crossed[b], sums, b == z_size - 1
            )
            grad_cross_rows.append(grad_rows)
        grad_mem_kv = jnp.concatenate(sums, axis=1)

        def cout_gradient(term):
            rows, _ = lax.optimization_barrier((branch_blocks, term))
            return outer_product_sum(joined(crossed), joined(rows)).astype(bf16)

        kept, came, cout_grad = sum_rows(
            grad_cross_rows, lambda x: transposed_product(x, w_cq), cout_gradient
        )
        kept, layer_out = sync(kept, layer_out)
        grad_one, branch, sums_one = norm_back(grad_two, kept, came, normed_one, inv_one, vectors, 0)
        branch_blocks = gather_rows(branch)
        cout_grad = tie(cout_grad, branch).reshape(sets, ranks, weight_rows, width)
        cout_pieces = from_ranks(cout_grad, 1)
        vec_sums = jnp.concatenate([sums_one, sums_two, sums_three], axis=0)
        for flip in flip_bits(dp_size):
            vec_sums = vec_sums + swap(vec_sums, "dp", dp_size, flip)
        branch_blocks[-1], vec_sums = sync(branch_blocks[-1], vec_sums)
        grad_mem_kv = tie(grad_mem_kv, branch)
        mem_kv_grad = outer_product_sum(all_memory, grad_mem_kv).astype(bf16)
        cross_grad = outer_product_sum(joined(one_blocks), joined(grad_cross_rows)).astype(bf16)
        all_dims = list(range(len(axes)))

        def first_sums(pair):
            pair = [x.reshape(halves(len(axes)) + x.shape[-2:]) for x in pair]
            return [scatter_axes(pair[0], all_dims, first_a), scatter_axes(pair[1], all_dims, first_b)]

        def more_sums(pair):
            return [
                scatter_axes(pair[0], [d for d in all_dims if d not in first_a], rest_a),
                scatter_axes(pair[1], [d for d in all_dims if d not in first_b], rest_b),
            ]

        def last_sums(pair):
            return [scatter_axes(x, g_axes, g_axes) for x in pair]

        grad_attended = [transposed_product(x, w_sout).astype(bf16) for x in branch_blocks]
        sout_grad = outer_product_sum(attended, joined(branch_blocks)).astype(bf16)
        sout_pieces = from_ranks(sout_grad.reshape(sets, ranks, weight_rows, width), 1)
        memory_kept, memory_came = sum_rows(
            row_blocks(grad_mem_kv), lambda x: transposed_product(x, w_ckv)
        )
        memory_rows = (memory_kept + memory_came.astype(f32)).astype(bf16)

        query_blocks = row_blocks(queries)
        chip_rows = queries.shape[0] // z_size
        grad_queries, sums = [], []
        for b in range(z_size):
            grad_rows, *sums = attention_backward(
                query_blocks[b],
                keys,
                values,
                self_probs,
                b * chip_rows,
                grad_attended[b],
                sums,
                b == z_size - 1,
            )
            grad_queries.append(grad_rows)
        grad_qk = jnp.concatenate([joined(grad_queries), sums[0]], axis=1)
        grad_values = sums[1]
        def by_group(grads):
            return grads.reshape(groups, rank_rows, -1)

        qk_grad = outer_product_sum(all_tokens, grad_qk).astype(bf16)
        grads_a = jnp.concatenate([by_group(qk_grad), by_group(mem_kv_grad)], axis=2)
        v_grad = outer_product_sum(all_tokens, grad_values).astype(bf16)
        grads_b = pack_grads(rank_own, by_group(v_grad), sout_pieces, by_group(cross_grad), cout_pieces)
        grads_a, grads_b, ffn_grads = sync(grads_a, grads_b, ffn_grads)
        sums = first_sums([grads_a, grads_b])
        ffn_grads = ffn_grads.reshape(g_size, 2, rank_rows, ff_part)
        down_grad = scatter_axes(ffn_grads[:, 1], g_axes, g_axes)
        up_pieces = ffn_grads[:, 0].reshape(g_size * ranks, weight_rows, ff_part)
        up_pieces = lax.all_to_all(up_pieces, ("g", "z", "c"), 0, 0, tiled=True)

        row_pairs = zip(row_blocks(tie(grad_qk, grads_a, grads_b)), row_blocks(grad_values))
        kept, came = sum_rows(
            list(row_pairs),
            lambda x: transposed_product(x[0], w_qk) + transposed_product(x[1], w_v),
        )
        tokens_grad = (residual_scale * grad_one + (kept + came.astype(f32))).astype(bf16)
        sums[0], sums[1], tokens_grad, memory_rows = sync(*sums, tokens_grad, memory_rows)
        sums = more_sums(sums)
        tokens_grad = send_back(tokens_grad)
        memory_grad = send_back(memory_rows)
        vec_sums = tie(vec_sums, *sums)
        for name, size in (("c", CORES), ("z", z_size), ("g", g_size)):
            for flip in flip_bits(size):
                vec_sums = vec_sums + swap(vec_sums, name, size, flip)
        by_ranks = (g_size * ranks, weight_rows)

        def to_own(parts_in):
            return lax.all_to_all(parts_in, ("g", "z", "c"), 0, 0, tiled=True)

        pieces = jnp.concatenate([sums[0], sums[1][..., :part], sums[1][..., 2 * part : 3 * part]], axis=2)
        pieces = to_own(pieces.reshape(by_ranks + (6 * part,)))
        out_grads = jnp.concatenate([sums[1][..., part : 2 * part], sums[1][..., 3 * part :]], axis=2)
        out_grads = scatter_axes(out_grads, g_axes, g_axes)

        down_grad = down_grad.reshape(ff_blocks, ff_rows, ff_part).transpose(1, 0, 2)
        down_grad = down_grad.reshape(ff_rows, width)

        def own_rows_of(values):
            return values.reshape(ranks, weight_rows, part).transpose(1, 0, 2).reshape(weight_rows, width)

        (up_grad,) = columns_back(up_pieces, ranks, (ff_part,), ff_rows)
        query_grad, key_grad, mem_key_grad, mem_value_grad, value_grad, cross_grad = columns_back(
            pieces, ranks, (part,) * 6, 0
        )

        first = ((dp_own * g_size + g_own) * ranks + rank_own) * weight_rows
        vec_grads = lax.dynamic_slice_in_dim(vec_sums, first, weight_rows, axis=1)

        return (
            layer_out,
            tokens_grad,
            memory_grad,
            query_grad,
            key_grad,
            value_grad,
            own_rows_of(out_grads[:, :part]),
            cross_grad,
            mem_key_grad,
            mem_value_grad,
            own_rows_of(out_grads[:, part:]),
            up_grad,
            down_grad,
            vec_grads[0],
            vec_grads[1],
            vec_grads[2],
            vec_grads[3],
            vec_grads[4],
            vec_grads[5],
        )

    return body


def solution(mesh):
    dp_size, seq_size = mesh.shape["dp"], mesh.shape["seq"]

    def layer_step(*args):
        g_size = args[0].shape[0] // dp_size
        z_size = seq_size // (g_size * CORES)
        split_mesh = Mesh(
            mesh.devices.reshape(dp_size, g_size, z_size, CORES), ("dp", "g", "z", "c")
        )
        seq = ("g", "z", "c")
        every = ("dp", "g", "z", "c")
        rows = P("dp", seq, None)
        matrix = P(every, None)
        vector = P(every)
        return jax.shard_map(
            make_body(dp_size, g_size, z_size),
            mesh=split_mesh,
            in_specs=(rows,) * 3 + (P("dp", None), P("dp")) + (matrix,) * 10 + (vector,) * 6,
            out_specs=(rows,) * 3 + (matrix,) * 10 + (vector,) * 6,
            check_vma=False,
        )(*args)

    return layer_step
```

```python
import jax
import jax.numpy as jnp
from jax import lax
from jax.experimental import pallas as pl
from jax.experimental.pallas import tpu as pltpu
from jax.sharding import Mesh, PartitionSpec as P

HEAD_DIM = 64
CORES = 2

eps_norm = 1e-05
residual_scale = 18.0**0.25
gelu_coef = 0.7978845608028654
neg_large = -1e30
bf16 = jnp.bfloat16
f32 = jnp.float32


def gelu_tanh(values_in):
    inner = gelu_coef * (values_in + 0.044715 * values_in * values_in * values_in)
    return 0.5 * values_in * (1.0 + jnp.tanh(inner))


def gelu_slope(values_in):
    squared = values_in * values_in
    tanh_val = jnp.tanh(gelu_coef * (values_in + 0.044715 * squared * values_in))
    return 0.5 * (1.0 + tanh_val) + 0.5 * values_in * (1.0 - tanh_val * tanh_val) * gelu_coef * (
        1.0 + 3.0 * 0.044715 * squared
    )


def matmul(first_mat, second_mat):
    return jnp.dot(first_mat, second_mat, preferred_element_type=f32)


def transposed_product(first_mat, second_mat):
    return lax.dot_general(first_mat, second_mat, (((1,), (1,)), ((), ())), preferred_element_type=f32)


def outer_product_sum(first_mat, second_mat):
    return lax.dot_general(first_mat, second_mat, (((0,), (0,)), ((), ())), preferred_element_type=f32)


LIMIT = pltpu.CompilerParams(vmem_limit_bytes=16 * 1024 * 1024)
ALL_OF_IT = pltpu.CompilerParams(vmem_limit_bytes=60 * 1024 * 1024)
SCALAR = pl.BlockSpec(memory_space=pltpu.SMEM)
WHOLE = pl.BlockSpec(memory_space=pltpu.VMEM)


def on_chip(values):
    return pltpu.with_memory_space_constraint(values, pltpu.VMEM)


def chip_call(kernel, outs, name, *args, scalar=None):
    scalars = [] if scalar is None else [scalar.reshape(1)]
    return pl.pallas_call(
        kernel,
        in_specs=[SCALAR] * len(scalars) + [WHOLE] * len(args),
        out_specs=[WHOLE] * len(outs),
        out_shape=[pltpu.VMEM(shape, dtype) for shape, dtype in outs],
        compiler_params=LIMIT,
        name=name,
    )(*scalars, *[on_chip(x) for x in args])


ANY = pl.BlockSpec(memory_space=pl.ANY)
FAR = pl.BlockSpec(memory_space=pltpu.HBM)


def copy_call(copies, out, name, scalar, *args):
    count = []

    def kernel(scalar_ref, *refs):
        sems = refs[-1]
        running = [
            pltpu.make_async_copy(source, target, sems.at[i])
            for i, (source, target) in enumerate(copies(scalar_ref[0], refs[:-2], refs[-2]))
        ]
        for one in running:
            one.start()
        for one in running:
            one.wait()

    class Probe:
        at = property(lambda self: self)

        def __getitem__(self, index):
            return self

    count = len(copies(0, [Probe()] * len(args), Probe()))
    return pl.pallas_call(
        kernel,
        in_specs=[SCALAR] + [ANY] * len(args),
        out_specs=ANY,
        out_shape=jax.ShapeDtypeStruct(*out),
        scratch_shapes=[pltpu.SemaphoreType.DMA((count,))],
        compiler_params=LIMIT,
        name=name,
    )(scalar.reshape(1), *args)


def _mean(values):
    return jnp.mean(values, axis=-1, keepdims=True)


def _normed(residual, kept, came):
    values = residual_scale * residual.astype(f32) + (kept + came.astype(f32))
    centred = values - _mean(values)
    inv_std = lax.rsqrt(_mean(centred * centred) + eps_norm)
    return centred * inv_std, inv_std


def _norm_back(grad_out, normed, inv_std, gain):
    scaled = grad_out * gain
    grad_in = inv_std * (scaled - _mean(scaled) - normed * _mean(scaled * normed))
    sums = [jnp.sum(grad_out * normed, axis=0, keepdims=True), jnp.sum(grad_out, axis=0, keepdims=True)]
    return grad_in, jnp.concatenate(sums, axis=0)


def norm_rows(residual, kept, came, vectors, row):
    def kernel(res, kept, came, vec, hidden, normed, inv):
        n, r = _normed(res[...], kept[...], came[...])
        hidden[...] = (n * vec[row : row + 1, :] + vec[row + 1 : row + 2, :]).astype(bf16)
        normed[...] = n
        inv[...] = jnp.broadcast_to(r, inv.shape)

    shape = residual.shape
    outs = [(shape, bf16), (shape, f32), ((shape[0], 128), f32)]
    return chip_call(kernel, outs, "norm_rows", residual, kept, came, vectors)


def norm_turn(residual, kept, came, vectors, row, cotangent):
    def kernel(res, kept, came, vec, cot, layer, grad, rounded, sums):
        gain = vec[row : row + 1, :]
        n, r = _normed(res[...], kept[...], came[...])
        layer[...] = (n * gain + vec[row + 1 : row + 2, :]).astype(bf16)
        g, s = _norm_back(cot[...].astype(f32), n, r, gain)
        grad[...] = g
        rounded[...] = g.astype(bf16)
        sums[...] = s

    shape = residual.shape
    outs = [(shape, bf16), (shape, f32), (shape, bf16), ((2, shape[1]), f32)]
    return chip_call(kernel, outs, "norm_turn", residual, kept, came, vectors, cotangent)


def norm_back(grad_prev, kept, came, normed, inv_std, vectors, row, limit=LIMIT):
    shape = grad_prev.shape
    args = [grad_prev, kept, came, normed, inv_std]

    def kernel(*refs):
        vec, grad, rounded, sums = refs[5:9]
        prev, kept, came, normed, inv = refs[9:14]
        running = [pltpu.make_async_copy(refs[i], refs[9 + i], refs[14].at[i]) for i in range(5)]
        for one in running:
            one.start()
        for one in running:
            one.wait()
        grad_out = residual_scale * prev[...] + (kept[...] + came[...].astype(f32))
        g, s = _norm_back(grad_out, normed[...], inv[:, :1], vec[row : row + 1, :])
        grad[...] = g
        rounded[...] = g.astype(bf16)
        sums[...] = s

    outs = [(shape, f32), (shape, bf16), ((2, shape[1]), f32)]
    return pl.pallas_call(
        kernel,
        in_specs=[FAR] * 5 + [WHOLE],
        out_specs=[WHOLE] * 3,
        out_shape=[pltpu.VMEM(x, dtype) for x, dtype in outs],
        scratch_shapes=[pltpu.VMEM(x.shape, x.dtype) for x in args] + [pltpu.SemaphoreType.DMA((5,))],
        compiler_params=limit,
        name="norm_back",
    )(*args, on_chip(vectors))


PAIR = 2 * HEAD_DIM


def _head_of_pair(values, head):
    lane = lax.broadcasted_iota(jnp.int32, (1, PAIR), 1)
    return jnp.where((lane // HEAD_DIM) == head, values, jnp.zeros((), values.dtype))


def _times(first, second, dims):
    return lax.dot_general(first, second, ((dims[:1], dims[1:]), ((), ())), preferred_element_type=f32)


def attention_forward(queries, keys, values, bias):
    rows, width = queries.shape
    key_rows = keys.shape[0]
    scale = HEAD_DIM ** (-0.5)

    def kernel(q_ref, k_ref, v_ref, *rest):
        out_ref, probs_ref = rest[-2:]
        for pair in range(width // PAIR):
            cols = slice(pair * PAIR, (pair + 1) * PAIR)
            q, k, v = q_ref[:, cols] * jnp.asarray(scale, bf16), k_ref[:, cols], v_ref[:, cols]
            mixed = None
            for head in range(2):
                scores = _times(k, _head_of_pair(q, head), (1, 1))
                if bias is not None:
                    scores = scores + rest[0][...]
                expo = jnp.exp(scores - jnp.max(scores, axis=0, keepdims=True))
                probs = (expo * (1.0 / jnp.sum(expo, axis=0, keepdims=True))).astype(bf16)
                probs_ref[2 * pair + head] = probs
                part = _times(_head_of_pair(v, head), probs, (0, 0))
                mixed = part if mixed is None else mixed + part
            out_ref[:, cols] = mixed.T.astype(bf16)

    args = [queries, keys, values] + ([] if bias is None else [bias])
    outs = [((rows, width), bf16), ((width // HEAD_DIM, key_rows, rows), bf16)]
    return chip_call(kernel, outs, "attend", *args)


def attention_backward(queries, keys, values, probs, first, grad_mixed, sums, last):
    rows, width = queries.shape
    key_rows = keys.shape[0]
    scale = HEAD_DIM ** (-0.5)

    def kernel(q_ref, k_ref, v_ref, p_ref, g_ref, *rest):
        before, (dq_ref, dk_ref, dv_ref) = rest[: len(sums)], rest[len(sums) :]
        for pair in range(width // PAIR):
            cols = slice(pair * PAIR, (pair + 1) * PAIR)
            q, k, v, g = q_ref[:, cols], k_ref[:, cols], v_ref[:, cols], g_ref[:, cols]
            dq = None
            dk, dv = [x[:, cols] for x in before] if sums else (None, None)
            for head in range(2):
                g_one = _head_of_pair(g, head)
                rounded = p_ref[2 * pair + head, :, first : first + rows]
                wide = rounded.astype(f32)
                weighted = _times(v, g_one, (1, 1)) * wide
                g_scores = (weighted - wide * jnp.sum(weighted, axis=0, keepdims=True)).astype(bf16)
                part_q = _times(_head_of_pair(k, head), g_scores, (0, 0))
                part_k = _times(g_scores, _head_of_pair(q, head), (1, 0))
                part_v = _times(rounded, g_one, (1, 0))
                dq = part_q if dq is None else dq + part_q
                dk = part_k if dk is None else dk + part_k
                dv = part_v if dv is None else dv + part_v
            dq_ref[:, cols] = (dq.T * scale).astype(bf16)
            dk_ref[:, cols] = (dk * scale).astype(bf16) if last else dk
            dv_ref[:, cols] = dv.astype(dv_ref.dtype)

    kind = bf16 if last else f32
    outs = [((rows, width), bf16), ((key_rows, width), kind), ((key_rows, width), kind)]
    return chip_call(kernel, outs, "attend_back", queries, keys, values, probs, grad_mixed, *sums)


def swap(values, name, size, flip):
    return lax.ppermute(values, name, [(i, i ^ flip) for i in range(size)])


def flip_bits(size):
    return [1 << b for b in range(size.bit_length() - 1)]


sync = lambda *values: lax.optimization_barrier(values)


def tie(value, *others):
    return lax.optimization_barrier((value,) + others)[0]


def lay_out(ranks, query, key, value, mem_key, mem_value, cross, up, own_out, mem_out):
    rows, width = query.shape
    part = width // ranks
    ff_part = up.shape[1] // ranks
    groups = ff_part * ranks // up.shape[1] * (width // (ranks * rows))
    unit = ff_part // groups

    def kernel(*refs):
        (self_ref, cross_ref, up_ref, so_ref, co_ref), ins, sems = refs[9:14], refs[14:23], refs[23]
        running = [pltpu.make_async_copy(refs[i], ins[i], sems.at[i]) for i in range(9)]
        for one in running:
            one.start()
        for one in running:
            one.wait()
        for r in range(ranks):
            cols = slice(r * part, (r + 1) * part)
            for i in range(3):
                self_ref[r, :, i * part : (i + 1) * part] = ins[i][:, cols]
                cross_ref[r, :, i * part : (i + 1) * part] = ins[3 + i][:, cols]
            so_ref[r] = ins[7][:, cols]
            co_ref[r] = ins[8][:, cols]
            for g in range(groups):
                first = (g * ranks + r) * unit
                up_ref[r, :, g * unit : (g + 1) * unit] = ins[6][:, first : first + unit]

    shapes = [3 * part, 3 * part, ff_part, part, part]
    return pl.pallas_call(
        kernel,
        in_specs=[FAR] * 9,
        out_specs=[WHOLE] * 5,
        scratch_shapes=[pltpu.VMEM((rows, width), bf16)] * 6
        + [pltpu.VMEM(up.shape, bf16)]
        + [pltpu.VMEM((rows, width), bf16)] * 2
        + [pltpu.SemaphoreType.DMA((9,))],
        out_shape=[pltpu.VMEM((ranks, rows, n), bf16) for n in shapes],
        compiler_params=ALL_OF_IT,
        name="lay_out",
    )(query, key, value, mem_key, mem_value, cross, up, own_out, mem_out)


def columns_back(pieces, ranks, counts, unit_first):
    terms, rows = pieces.shape[0] // ranks, pieces.shape[1]

    def kernel(in_ref, *outs):
        def total(r, cols):
            found = in_ref[r, :, cols].astype(f32)
            for term in range(1, terms):
                found = found + in_ref[term * ranks + r, :, cols].astype(f32)
            return found

        first = 0
        for out, count in zip(outs, counts):
            if out is outs[0] and unit_first:
                units = count // unit_first
                for r in range(ranks):
                    for g in range(units):
                        at = (g * ranks + r) * unit_first
                        cols = slice(first + g * unit_first, first + (g + 1) * unit_first)
                        out[:, at : at + unit_first] = total(r, cols)
            else:
                for r in range(ranks):
                    out[:, r * count : (r + 1) * count] = total(r, slice(first, first + count))
            first += count

    return pl.pallas_call(
        kernel,
        in_specs=[WHOLE],
        out_specs=[WHOLE] * len(counts),
        out_shape=[jax.ShapeDtypeStruct((rows, ranks * n), f32) for n in counts],
        compiler_params=LIMIT,
        name="columns_back",
    )(on_chip(pieces))


def join_rows(pieces, rank):
    ranks = len(pieces)
    sets, blocks, rows, part = pieces[0].shape

    def copies(own, refs, out):
        return [
            (refs[r].at[p, b], out.at[p, own ^ r, :, b * part : (b + 1) * part])
            for r in range(ranks)
            for p in range(sets)
            for b in range(blocks)
        ]

    joined = copy_call(copies, ((sets, ranks, rows, blocks * part), bf16), "join_rows", rank, *pieces)
    return joined.reshape(sets * ranks * rows, blocks * part)


def pack_grads(rank, *parts):
    args = []
    places = []
    first = 0
    for one in parts:
        if isinstance(one, list):
            ranks, (sets, rows, width) = len(one), one[0].shape
            part = width // ranks
            for r in range(ranks):
                for p in range(sets):
                    for b in range(ranks):
                        at = slice(b * rows, (b + 1) * rows), slice(first, first + part)
                        places.append((len(args) + r, (p, slice(None), slice(b * part, (b + 1) * part)), (r, sets, p), at))
            args += one
            first += part
        elif one.ndim == 4:
            ranks, sets, rows, width = one.shape
            part = width // ranks
            for r in range(ranks):
                for p in range(sets):
                    for b in range(ranks):
                        at = slice(b * rows, (b + 1) * rows), slice(first, first + part)
                        source = (r, p, slice(None), slice(b * part, (b + 1) * part))
                        places.append((len(args), source, r * sets + p, at))
            args.append(one)
            first += part
        else:
            groups, n, m = one.shape
            places.append((len(args), (slice(None),) * 3, None, (slice(None), slice(first, first + m))))
            args.append(one)
            first += m

    def copies(own, refs, out):
        found = []
        for i, source, piece, at in places:
            lead = slice(None) if piece is None else piece
            if isinstance(piece, tuple):
                lead = (own ^ piece[0]) * piece[1] + piece[2]
            found.append((refs[i].at[source], out.at[(lead,) + at]))
        return found

    return copy_call(copies, ((groups, n, first), bf16), "pack_grads", rank, *args)


def make_body(dp_size, g_size, z_size):
    ranks = z_size * CORES
    groups = dp_size * g_size
    every = ("dp", "g", "z", "c")

    def body(
        tokens,
        memory,
        cotangent,
        block_ids,
        seq_lengths,
        self_query,
        self_key,
        self_value,
        self_out,
        cross_query,
        cross_key,
        cross_value,
        cross_out,
        ffn_up,
        ffn_down,
        attn_gain,
        attn_bias,
        cross_gain,
        cross_bias,
        feedforward_norm_gain,
        ffn_bias,
    ):
        dp_own = lax.axis_index("dp")
        g_own = lax.axis_index("g")
        rank_own = lax.axis_index("z") * CORES + lax.axis_index("c")
        piece_rows = tokens.shape[1]
        width = tokens.shape[2]
        weight_rows = self_query.shape[0]
        rank_rows = ranks * weight_rows
        part = width // ranks
        sets = groups // ranks
        ff_rows = ffn_down.shape[0]
        ff_part = groups * ff_rows
        ff_blocks = width // ff_part

        def bits_of(name, size, own):
            return [(name, size, f, (own // f) % 2) for f in reversed(flip_bits(size))]

        axes = bits_of("dp", dp_size, dp_own) + bits_of("g", g_size, g_own)
        n_dp = dp_size.bit_length() - 1
        g_axes = list(range(n_dp, len(axes)))
        order_a = list(reversed(range(n_dp)))
        order_b = list(range(n_dp))

        def gather_axes(values, dims, order, after=()):
            for ax in order:
                name, size, flip, bit = axes[ax]
                other = tie(swap(values, name, size, flip), *after)
                pos = len([d for d in dims if d < ax])
                values = jnp.where(
                    bit == 1, jnp.stack([other, values], pos), jnp.stack([values, other], pos)
                )
                dims = sorted(dims + [ax])
            return values

        def scatter_axes(values, dims, order):
            dims = list(dims)
            for i, ax in enumerate(order):
                name, size, flip, bit = axes[ax]
                pos = dims.index(ax)
                other = swap(
                    lax.dynamic_index_in_dim(values, 1 - bit, pos, keepdims=False), name, size, flip
                )
                kept = lax.dynamic_index_in_dim(values, bit, pos, keepdims=False)
                values = kept.astype(f32) + other.astype(f32)
                dims.remove(ax)
                if dims:
                    values = values.astype(bf16)
            return values

        def halves(n):
            return (2,) * n

        def finish(values):
            shape = values.shape[1:]
            return scatter_axes(values.reshape(halves(len(g_axes)) + shape), g_axes, g_axes)

        def rank_swap(values, flip):
            return swap(values, ("z", "c"), ranks, flip)

        def from_ranks(pieces, axis):
            got = []
            for f in range(ranks):
                piece = lax.dynamic_index_in_dim(pieces, rank_own ^ f, axis, keepdims=False)
                got.append(piece if f == 0 else rank_swap(piece, f))
            return got

        def gather_rows(values):
            return with_partner(gather_chips(values))

        def gather_chips(values):
            blocks = [values]
            for flip in flip_bits(z_size):
                blocks = blocks + [swap(b, "z", z_size, flip) for b in blocks]
            return blocks

        def with_partner(blocks):
            return [jnp.concatenate([b, swap(b, "c", CORES, 1)], axis=0) for b in blocks]

        def sum_rows(blocks, product, fill=None):
            own_rows = piece_rows * g_size
            sums = [None] * z_size
            for b in reversed(range(z_size)):
                partial = product(blocks[b])
                came = swap(partial[own_rows:].astype(bf16), "c", CORES, 1)
                sums[b] = partial[:own_rows] + came.astype(f32)
            for flip in reversed(flip_bits(z_size)):
                leaving = [sums[b + flip].astype(bf16) for b in range(flip)]
                came = [swap(x, "z", z_size, flip) for x in leaving]
                if flip > 1:
                    sums = [sums[b] + came[b].astype(f32) for b in range(flip)]
            if fill is None:
                return sums[0], came[0]
            filled = fill(leaving[0])
            kept, last, filled = lax.optimization_barrier((sums[0], came[0], filled))
            return kept, last, filled

        def bring_home(values, *after):
            got = []
            for f in range(g_size):
                piece = lax.dynamic_index_in_dim(values, g_own ^ f, 0, keepdims=False)
                got.append(piece if f == 0 else tie(swap(piece, "g", g_size, f), *after))
            return jnp.concatenate(got, axis=-2)

        def send_back(values):
            blocks = values.reshape(g_size, piece_rows, width)
            got = [blocks[0]] + [swap(blocks[f], "g", g_size, f) for f in range(1, g_size)]
            got = jnp.stack(got)
            return jnp.stack(
                [lax.dynamic_index_in_dim(got, g_own ^ f, 0, keepdims=False) for f in range(g_size)]
            )

        own_tokens = bring_home(tokens)
        self_parts, cross_parts, up_parts, so_parts, co_parts = lay_out(
            ranks,
            self_query,
            self_key,
            self_value,
            cross_key,
            cross_value,
            cross_query,
            ffn_up,
            self_out,
            cross_out,
        )

        def to_ranks(parts_in):
            return lax.all_to_all(parts_in, ("z", "c"), 0, 0, tiled=True)

        self_own, own_tokens = sync(to_ranks(self_parts), own_tokens)
        self_set = jnp.concatenate([self_own, so_parts], axis=2).reshape(rank_rows, 4 * part)
        self_set = gather_axes(self_set, [], g_axes)
        token_blocks = gather_rows(own_tokens)
        other_own = to_ranks(tie(jnp.concatenate([cross_parts, up_parts], axis=2), self_own))
        half_a, half_b, *token_blocks = sync(
            self_set[..., : 2 * part], self_set[..., 2 * part :], *token_blocks
        )
        other_own = tie(other_own, half_a)

        first_a, rest_a = order_a[:1], order_a[1:]
        first_b, rest_b = order_b[:1], order_b[1:]

        def first_stage(pair):
            return [gather_axes(pair[0], g_axes, first_a), gather_axes(pair[1], g_axes, first_b)]

        def last_stage(pair):
            pair = [
                gather_axes(pair[0], sorted(g_axes + first_a), rest_a),
                gather_axes(pair[1], sorted(g_axes + first_b), rest_b),
            ]
            return [x.reshape((groups,) + x.shape[-2:]) for x in pair]

        assert len(g_axes) == 1
        g_axis = axes[g_axes[0]]

        def swap_groups(values):
            return swap(values, *g_axis[:3])

        def both_groups(own, other):
            return jnp.where(g_axis[3] == 1, jnp.stack([other, own]), jnp.stack([own, other]))

        self_pair = first_stage([half_a, half_b])
        cross_set = jnp.concatenate([other_own[..., : 3 * part], co_parts], axis=2)
        cross_set = cross_set.reshape(rank_rows, 4 * part)
        cross_other = swap_groups(cross_set)
        own_memory = bring_home(tie(memory, self_set), *self_pair)
        all_tokens = jnp.concatenate(token_blocks, axis=0)
        vectors = jnp.stack(
            [attn_gain, attn_bias, cross_gain, cross_bias, feedforward_norm_gain, ffn_bias]
        )
        vectors = jnp.broadcast_to(vectors[None], (groups * ranks,) + vectors.shape)
        self_pair[0], self_pair[1], vectors = sync(*self_pair, vectors)
        vectors = lax.all_to_all(vectors, every, 0, 0, tiled=True)
        vectors = vectors.transpose(1, 0, 2).reshape(6, width).astype(f32)
        self_pair = last_stage(self_pair)
        self_pair[0], self_pair[1], vectors = sync(*self_pair, vectors)
        cross_other = tie(cross_other, *self_pair)
        w_qk = self_pair[0].reshape(width, 2 * part)
        w_v = self_pair[1][..., :part].reshape(width, part)
        cross_set = both_groups(cross_set, cross_other)
        cross_pair = first_stage([cross_set[..., : 2 * part], cross_set[..., 2 * part :]])
        memory_chips = gather_chips(own_memory)

        down_rows = ffn_down.reshape(ff_rows, ff_blocks, ff_part).transpose(1, 0, 2)
        up_own, down_own = sync(
            other_own[..., 3 * part :].reshape(rank_rows, ff_part),
            down_rows.reshape(rank_rows, ff_part),
            self_pair[0],
        )[:2]
        up_other = swap_groups(up_own)
        down_other = swap_groups(tie(down_own, up_other))

        def out_rows(rows_in):
            pieces = rows_in.reshape(ranks, sets, ranks, weight_rows, part)
            return join_rows(from_ranks(pieces, 0), rank_own)

        w_sout = out_rows(self_pair[1][..., part:])

        n_pieces = g_size * ranks
        seq_own = g_own * ranks + rank_own
        ids = lax.dynamic_index_in_dim(block_ids, g_own, 0, keepdims=False)
        length = lax.dynamic_index_in_dim(seq_lengths, g_own, 0, keepdims=False)
        live = jnp.arange(ids.shape[0], dtype=jnp.int32) < length
        both = jnp.stack([ids, jnp.where(live, ids, jnp.int32(2**30))]).reshape(2, n_pieces, piece_rows)
        for flip in flip_bits(n_pieces):
            turned = both.reshape(2, n_pieces // (2 * flip), 2, flip, piece_rows)
            turned = jnp.concatenate([turned[:, :, 1:], turned[:, :, :1]], axis=2).reshape(both.shape)
            both = jnp.where((seq_own & flip) != 0, turned, both)
        both = both.reshape(2, g_size, ranks, piece_rows).transpose(0, 2, 1, 3).reshape(2, -1)
        bias = jnp.where(both[1][:, None] <= both[0][None, :], 0.0, neg_large).astype(f32)

        def row_blocks(values):
            return jnp.split(values, z_size, axis=0)

        def joined(blocks):
            return jnp.concatenate(blocks, axis=0)

        qk = matmul(all_tokens, w_qk).astype(bf16)
        queries, keys = qk[:, :part], qk[:, part:]
        values = matmul(all_tokens, w_v).astype(bf16)
        attended, self_probs = attention_forward(queries, keys, values, bias)
        attended, cross_pair[0], cross_pair[1], up_other = sync(attended, *cross_pair, up_other)
        cross_pair = last_stage(cross_pair)
        kept, came, memory_blocks = sum_rows(
            row_blocks(attended),
            lambda x: matmul(x, w_sout),
            lambda term: with_partner([tie(x, term) for x in memory_chips]),
        )
        kept, came, down_other = sync(kept, came, down_other)
        hidden_one, normed_one, inv_one = norm_rows(own_tokens, kept, came, vectors, 0)
        ffn_pair = first_stage([both_groups(up_own, up_other), both_groups(down_own, down_other)])
        own_cotangent = bring_home(tie(cotangent, down_other))

        all_memory = joined(memory_blocks)
        w_ckv = cross_pair[0].reshape(width, 2 * part)
        w_cq = cross_pair[1][..., :part].reshape(width, part)
        cout_rows = from_ranks(cross_pair[1][..., part:].reshape(ranks, sets, ranks, weight_rows, part), 0)
        mem_kv = matmul(all_memory, w_ckv).astype(bf16)
        mem_keys, mem_values = mem_kv[:, :part], mem_kv[:, part:]

        one_blocks = gather_rows(hidden_one)
        one_blocks[-1], mem_keys, mem_values, ffn_pair[0], ffn_pair[1] = sync(
            one_blocks[-1], mem_keys, mem_values, *ffn_pair
        )
        ffn_pair = last_stage(ffn_pair)
        cross_rows = [matmul(x, w_cq).astype(bf16) for x in one_blocks]
        crossed = [attention_forward(x, mem_keys, mem_values, None) for x in cross_rows]
        cross_probs = [x[1] for x in crossed]
        crossed = [x[0] for x in crossed]
        w_cout = join_rows([tie(x, *crossed) for x in cout_rows], rank_own)
        kept, came = sum_rows(crossed, lambda x: matmul(x, w_cout))
        hidden_two, normed_two, inv_two = norm_rows(hidden_one, kept, came, vectors, 2)
        hidden_two, own_cotangent = sync(hidden_two, own_cotangent)
        two_blocks = gather_rows(hidden_two)
        w_up = ffn_pair[0].reshape(width, ff_part)
        w_down = ffn_pair[1].reshape(groups, ff_blocks, ff_rows, ff_part).transpose(0, 2, 1, 3)
        w_down = w_down.reshape(ff_part, width)
        upper_rows = [matmul(x, w_up) for x in two_blocks]
        active_rows = [gelu_tanh(x).astype(bf16) for x in upper_rows]
        kept, came, slopes = sum_rows(
            active_rows,
            lambda x: matmul(x, w_down),
            lambda term: [gelu_slope(tie(x, term)) for x in upper_rows],
        )
        layer_rows, grad_three, branch, sums_three = norm_turn(
            hidden_two, kept, came, vectors, 4, own_cotangent
        )

        branch_blocks = gather_rows(branch)
        grad_upper = [
            (transposed_product(x, w_down) * y).astype(bf16) for x, y in zip(branch_blocks, slopes)
        ]

        def ffn_gradients(term):
            rows, _ = lax.optimization_barrier((branch_blocks, term))
            down = outer_product_sum(joined(active_rows), joined(rows)).astype(bf16)
            down = down.reshape(groups, ff_rows, ff_blocks, ff_part).transpose(0, 2, 1, 3)
            up = outer_product_sum(joined(two_blocks), joined(grad_upper)).astype(bf16)
            return jnp.concatenate(
                [up.reshape(groups, rank_rows, ff_part), down.reshape(groups, rank_rows, ff_part)],
                axis=1,
            )

        kept, came, ffn_grads = sum_rows(
            grad_upper, lambda x: transposed_product(x, w_up), ffn_gradients
        )
        ffn_grads = lax.psum_scatter(
            ffn_grads.reshape(groups * 2 * rank_rows, ff_part), "dp", scatter_dimension=0, tiled=True
        )
        grad_two, branch, sums_two = norm_back(
            grad_three, kept, came, normed_two, inv_two, vectors, 2, ALL_OF_IT
        )
        layer_out = send_back(tie(layer_rows, branch))

        branch_blocks = gather_rows(branch)
        grad_crossed = [transposed_product(x, w_cout).astype(bf16) for x in branch_blocks]
        grad_cross_rows, sums = [], []
        for b in range(z_size):
            grad_rows, *sums = attention_backward(
                cross_rows[b], mem_keys, mem_values, cross_probs[b], 0, grad_crossed[b], sums, b == z_size - 1
            )
            grad_cross_rows.append(grad_rows)
        grad_mem_kv = jnp.concatenate(sums, axis=1)

        def cout_gradient(term):
            rows, _ = lax.optimization_barrier((branch_blocks, term))
            return outer_product_sum(joined(crossed), joined(rows)).astype(bf16)

        kept, came, cout_grad = sum_rows(
            grad_cross_rows, lambda x: transposed_product(x, w_cq), cout_gradient
        )
        kept, layer_out = sync(kept, layer_out)
        grad_one, branch, sums_one = norm_back(grad_two, kept, came, normed_one, inv_one, vectors, 0)
        branch_blocks = gather_rows(branch)
        cout_grad = tie(cout_grad, branch).reshape(sets, ranks, weight_rows, width)
        cout_pieces = from_ranks(cout_grad, 1)
        vec_sums = jnp.concatenate([sums_one, sums_two, sums_three], axis=0)
        for flip in flip_bits(dp_size):
            vec_sums = vec_sums + swap(vec_sums, "dp", dp_size, flip)
        branch_blocks[-1], vec_sums = sync(branch_blocks[-1], vec_sums)
        grad_mem_kv = tie(grad_mem_kv, branch)
        mem_kv_grad = outer_product_sum(all_memory, grad_mem_kv).astype(bf16)
        cross_grad = outer_product_sum(joined(one_blocks), joined(grad_cross_rows)).astype(bf16)
        all_dims = list(range(len(axes)))

        def first_sums(pair):
            pair = [x.reshape(halves(len(axes)) + x.shape[-2:]) for x in pair]
            return [scatter_axes(pair[0], all_dims, first_a), scatter_axes(pair[1], all_dims, first_b)]

        def more_sums(pair):
            return [
                scatter_axes(pair[0], [d for d in all_dims if d not in first_a], rest_a),
                scatter_axes(pair[1], [d for d in all_dims if d not in first_b], rest_b),
            ]

        def last_sums(pair):
            return [scatter_axes(x, g_axes, g_axes) for x in pair]

        grad_attended = [transposed_product(x, w_sout).astype(bf16) for x in branch_blocks]
        sout_grad = outer_product_sum(attended, joined(branch_blocks)).astype(bf16)
        sout_pieces = from_ranks(sout_grad.reshape(sets, ranks, weight_rows, width), 1)
        memory_kept, memory_came = sum_rows(
            row_blocks(grad_mem_kv), lambda x: transposed_product(x, w_ckv)
        )
        memory_rows = (memory_kept + memory_came.astype(f32)).astype(bf16)

        query_blocks = row_blocks(queries)
        chip_rows = queries.shape[0] // z_size
        grad_queries, sums = [], []
        for b in range(z_size):
            grad_rows, *sums = attention_backward(
                query_blocks[b],
                keys,
                values,
                self_probs,
                b * chip_rows,
                grad_attended[b],
                sums,
                b == z_size - 1,
            )
            grad_queries.append(grad_rows)
        grad_qk = jnp.concatenate([joined(grad_queries), sums[0]], axis=1)
        grad_values = sums[1]
        def by_group(grads):
            return grads.reshape(groups, rank_rows, -1)

        qk_grad = outer_product_sum(all_tokens, grad_qk).astype(bf16)
        grads_a = jnp.concatenate([by_group(qk_grad), by_group(mem_kv_grad)], axis=2)
        v_grad = outer_product_sum(all_tokens, grad_values).astype(bf16)
        grads_b = pack_grads(rank_own, by_group(v_grad), sout_pieces, by_group(cross_grad), cout_pieces)
        grads_a, grads_b, ffn_grads = sync(grads_a, grads_b, ffn_grads)
        sums = first_sums([grads_a, grads_b])
        ffn_grads = ffn_grads.reshape(g_size, 2, rank_rows, ff_part)
        down_grad = scatter_axes(ffn_grads[:, 1], g_axes, g_axes)
        up_pieces = ffn_grads[:, 0].reshape(g_size * ranks, weight_rows, ff_part)
        up_pieces = lax.all_to_all(up_pieces, ("g", "z", "c"), 0, 0, tiled=True)

        row_pairs = zip(row_blocks(tie(grad_qk, grads_a, grads_b)), row_blocks(grad_values))
        kept, came = sum_rows(
            list(row_pairs),
            lambda x: transposed_product(x[0], w_qk) + transposed_product(x[1], w_v),
        )
        tokens_grad = (residual_scale * grad_one + (kept + came.astype(f32))).astype(bf16)
        sums[0], sums[1], tokens_grad, memory_rows = sync(*sums, tokens_grad, memory_rows)
        sums = more_sums(sums)
        tokens_grad = send_back(tokens_grad)
        memory_grad = send_back(memory_rows)
        vec_sums = tie(vec_sums, *sums)
        for name, size in (("c", CORES), ("z", z_size), ("g", g_size)):
            for flip in flip_bits(size):
                vec_sums = vec_sums + swap(vec_sums, name, size, flip)
        by_ranks = (g_size * ranks, weight_rows)

        def to_own(parts_in):
            return lax.all_to_all(parts_in, ("g", "z", "c"), 0, 0, tiled=True)

        pieces = jnp.concatenate([sums[0], sums[1][..., :part], sums[1][..., 2 * part : 3 * part]], axis=2)
        pieces = to_own(pieces.reshape(by_ranks + (6 * part,)))
        out_grads = jnp.concatenate([sums[1][..., part : 2 * part], sums[1][..., 3 * part :]], axis=2)
        out_grads = scatter_axes(out_grads, g_axes, g_axes)

        down_grad = down_grad.reshape(ff_blocks, ff_rows, ff_part).transpose(1, 0, 2)
        down_grad = down_grad.reshape(ff_rows, width)

        def own_rows_of(values):
            return values.reshape(ranks, weight_rows, part).transpose(1, 0, 2).reshape(weight_rows, width)

        (up_grad,) = columns_back(up_pieces, ranks, (ff_part,), ff_rows)
        query_grad, key_grad, mem_key_grad, mem_value_grad, value_grad, cross_grad = columns_back(
            pieces, ranks, (part,) * 6, 0
        )

        first = ((dp_own * g_size + g_own) * ranks + rank_own) * weight_rows
        vec_grads = lax.dynamic_slice_in_dim(vec_sums, first, weight_rows, axis=1)

        return (
            layer_out,
            tokens_grad,
            memory_grad,
            query_grad,
            key_grad,
            value_grad,
            own_rows_of(out_grads[:, :part]),
            cross_grad,
            mem_key_grad,
            mem_value_grad,
            own_rows_of(out_grads[:, part:]),
            up_grad,
            down_grad,
            vec_grads[0],
            vec_grads[1],
            vec_grads[2],
            vec_grads[3],
            vec_grads[4],
            vec_grads[5],
        )

    return body


def solution(mesh):
    dp_size, seq_size = mesh.shape["dp"], mesh.shape["seq"]

    def layer_step(*args):
        g_size = args[0].shape[0] // dp_size
        z_size = seq_size // (g_size * CORES)
        split_mesh = Mesh(
            mesh.devices.reshape(dp_size, g_size, z_size, CORES), ("dp", "g", "z", "c")
        )
        seq = ("g", "z", "c")
        every = ("dp", "g", "z", "c")
        rows = P("dp", seq, None)
        matrix = P(every, None)
        vector = P(every)
        return jax.shard_map(
            make_body(dp_size, g_size, z_size),
            mesh=split_mesh,
            in_specs=(rows,) * 3 + (P("dp", None), P("dp")) + (matrix,) * 10 + (vector,) * 6,
            out_specs=(rows,) * 3 + (matrix,) * 10 + (vector,) * 6,
            check_vma=False,
        )(*args)

    return layer_step
```
